256 devices in a mesh: sector: 32 (over y_lo, z, core), span: 8 (over y_hi, x).
Axes of the slice: x: 4, y: 4 (y_hi: 2, y_lo: 2; y = y_hi * 2 + y_lo), z: 8, core: 2. Of those that a mesh axis runs over, the one named last changes fastest.
Arguments:
- rhs: float32 [11, 7, 64, 64, 128], P(None, None, 'sector', 'span'), may hold values from -6 to 6
- diag_coef: float32 [64, 64, 128], P('sector', 'span'), may hold values from 2 to 4
- face_coef: float32 [3, 64, 64, 128], P(None, 'sector', 'span'), may hold values from 0.2 to 0.6
- time_coef: float32 [64, 64, 128], P('sector', 'span'), may hold values from 0.05 to 0.4
- jac_up: float32 [3, 7, 7], replicated, may hold values from -1.5 to 1.5
- jac_down: float32 [3, 7, 7], replicated, may hold values from -1.5 to 1.5
- wall_mask: int32 [64, 64, 128], P('sector', 'span'), may hold values 0 or 1
- stator_adj: float32 [11, 7, 128, 64], P(None, None, 'sector', 'span'), may hold values from -6 to 6
- owner: int32 [11, 64, 64], P(None, 'sector', 'span'), may hold values from 0 to 126, as said below
- first_panel_share: float32 [11, 64, 64], P(None, 'sector', 'span'), may hold values from 0 to 1
Outputs:
- adjoint_out: float32 [11, 7, 64, 64, 128], P(None, None, 'sector', 'span')
- stator_sens: float32 [11, 7, 128, 64], P(None, None, 'sector', 'span')
The draws below stay inside these ranges and needn't reach their ends.
Inputs may be any that keep to these rules, and one draw needn't show every extreme that they name: For instance t and an inlet cell in azimuthal block b (cells b * 2 to (b + 1) * 2 - 1), owner and owner + 1 both lie in panel block q = (b + (t * 32) // 10 - t // 10) mod 32, that is between q * 4 and (q + 1) * 4 - 1.
All inputs are finite; a program needn't handle non-finite values. No bound on the sum of `wall_mask` on one device may be relied on, other than what follows from the above.
Results may differ from the reference program's by a relative error of at most 0.0001.
Values sent between devices are 32-bit elements; how exact they have to be, the bound alone decides.
A program may use at most 64 MiB of HBM per device.

```python
import math
import jax
import jax.numpy as jnp
from jax import lax

HB_SNAPSHOTS = 11
FLD = 7
CT = 2
NAX = 128
SWEEPS = 4
PT = 4
NTH = 64
NR = 64
NPT = 128


def draw_owner(key, part):
    period_samples = jnp.arange(HB_SNAPSHOTS)[:, None, None]
    azimuth = jnp.arange(NTH)[None, :, None]
    wheel_passage_count = NTH // CT
    cell_groups = azimuth // CT
    turned = period_samples * wheel_passage_count // (HB_SNAPSHOTS - 1) - period_samples // (HB_SNAPSHOTS - 1)
    destination_solution = jnp.mod(cell_groups + turned, wheel_passage_count)
    nearby_leading = jax.random.randint(key, (HB_SNAPSHOTS, NTH, NR), 0, PT - 1)
    nearby_leading = nearby_leading.at[0, 0, 0].set(0)
    nearby_leading = nearby_leading.at[0, NTH - 1, 0].set(PT - 2)
    return (destination_solution * PT + nearby_leading).astype(jnp.int32)


def with_ends(array, key, low, largest):
    longest = array.shape.index(max(array.shape))
    spots = []
    for shift in (0, 1):
        where = [jax.random.randint(jax.random.fold_in(key, axis), (), 0, length) for axis, length in enumerate(array.shape)]
        where[longest] = (where[longest] + shift) % array.shape[longest]
        spots.append(tuple(where))
    return array.at[spots[0]].set(low).at[spots[1]].set(largest)


def steps_of(own_key, extent, split, smallest, largest):
    def one(axis_at, shards_of):
        steps = jax.random.uniform(jax.random.fold_in(jax.random.fold_in(own_key, 6), axis_at), (shards_of,), jnp.float32, smallest / len(split), largest / len(split))
        return jnp.repeat(jnp.exp(steps), extent[axis_at] // shards_of).reshape((-1,) + (1,) * (len(extent) - axis_at - 1))

    factor_of = one(*split[0])
    for cut in split[1:]:
        factor_of = factor_of * one(*cut)
    return factor_of


def centred(key, shape, scale, bound, cuts=(), held_as=jnp.bfloat16):
    drawn = scale * jax.random.normal(key, shape, jnp.float32)
    if cuts:
        drawn = drawn * steps_of(key, shape, cuts, -0.22, 0.18)
    return jnp.clip(drawn, -bound, bound).astype(held_as)


def setup_inputs(seed: int = 0) -> dict:
    keys = jax.random.split(jax.random.key(seed), 11)
    rhs = centred(keys[0], (HB_SNAPSHOTS, FLD, NTH, NR, NAX), 1.0, 6.0, ((2, 32), (3, 8)), jnp.float32)
    diag_coef = jnp.clip(jnp.exp(math.log(4.0) - 0.6931472 * jax.random.uniform(keys[1], (NTH, NR, NAX), jnp.float32) ** steps_of(keys[1], (NTH, NR, NAX), ((0, 32), (1, 8)), -0.2, 0.2)), 2.0, 4.0)
    face_coef = jnp.clip(jnp.exp(math.log(0.6) - 1.0986123 * jax.random.uniform(keys[2], (3, NTH, NR, NAX), jnp.float32) ** steps_of(keys[2], (3, NTH, NR, NAX), ((1, 32), (2, 8)), -0.2, 0.2)), 0.2, 0.6)
    time_coef = jnp.clip(jnp.exp(math.log(0.4) - 2.0794415 * jax.random.uniform(keys[3], (NTH, NR, NAX), jnp.float32) ** steps_of(keys[3], (NTH, NR, NAX), ((0, 32), (1, 8)), -0.2, 0.2)), 0.05, 0.4)
    jac_up = centred(keys[4], (3, FLD, FLD), (2 * FLD) ** -0.5, 1.5, (), jnp.float32)
    jac_down = centred(keys[5], (3, FLD, FLD), (2 * FLD) ** -0.5, 1.5, (), jnp.float32)
    wall_mask = with_ends((jax.random.randint(keys[6], (NTH, NR, NAX), 0, 8) < 7).astype(jnp.int32), jax.random.fold_in(keys[6], 1), 0, 1)
    stator_adj = centred(keys[7], (HB_SNAPSHOTS, FLD, NPT, NR), 1.0, 6.0, ((2, 32), (3, 8)), jnp.float32)
    owner = draw_owner(jax.random.fold_in(keys[10], 71), 0)
    first_panel_share = jnp.clip(1.0 * jax.random.uniform(keys[9], (HB_SNAPSHOTS, NTH, NR), jnp.float32) ** steps_of(keys[9], (HB_SNAPSHOTS, NTH, NR), ((1, 32), (2, 8)), -0.2, 0.2), 0.0, 1.0)
    return {"rhs": rhs, "diag_coef": diag_coef, "face_coef": face_coef, "time_coef": time_coef, "jac_up": jac_up, "jac_down": jac_down, "wall_mask": wall_mask, "stator_adj": stator_adj, "owner": owner, "first_panel_share": first_panel_share}


def spectral_table(count):
    positions = jnp.arange(count)
    offsets = positions[:, None] - positions[None, :]
    sweep_parity = 1.0 - 2.0 * jnp.mod(offsets, 2).astype(jnp.float32)
    angles = math.pi * offsets.astype(jnp.float32) / count
    sines = jnp.where(offsets == 0, 1.0, jnp.sin(angles))
    return jnp.where(offsets == 0, 0.0, 0.5 * sweep_parity / sines).astype(jnp.float32)


def apply_block(matrix, field):
    return jnp.einsum('ef,tfabc->teabc', matrix, field, precision=lax.Precision.HIGHEST)


def couple(field, face_coef, time_coef, jac_up, jac_down, spectral_matrix):
    coupled = time_coef * jnp.einsum('st,sfabc->tfabc', spectral_matrix, field, precision=lax.Precision.HIGHEST)
    theta = (jnp.roll(field, -1, axis=2), jnp.roll(field, 1, axis=2))
    radial_padding = jnp.pad(field, ((0, 0), (0, 0), (0, 0), (1, 1), (0, 0)))
    radial = (radial_padding[:, :, :, 2:, :], radial_padding[:, :, :, :-2, :])
    axial_pad = jnp.pad(field, ((0, 0), (0, 0), (0, 0), (0, 0), (1, 1)))
    axial = (axial_pad[..., 2:], axial_pad[..., :-2])
    sides = (theta, radial, axial)
    for direction in range(3):
        forward_side, backward_side = sides[direction]
        coupled = coupled + face_coef[direction] * (apply_block(jac_up[direction], forward_side) + apply_block(jac_down[direction], backward_side))
    return coupled


def reference(rhs, diag_coef, face_coef, time_coef, jac_up, jac_down, wall_mask, stator_adj, owner, first_panel_share):
    spectral_matrix = spectral_table(HB_SNAPSHOTS)
    radial_index = jnp.arange(NR)[None, :]
    pieces = []
    for inst in range(HB_SNAPSHOTS):
        panels = stator_adj[inst]
        first = owner[inst]
        weight = first_panel_share[inst]
        pieces.append(weight * panels[:, first, radial_index] + (1.0 - weight) * panels[:, first + 1, radial_index])
    rotor_stator_seam = jnp.stack(pieces)
    forcing = rhs.at[..., 0].add(rotor_stator_seam)
    mask_float = wall_mask.astype(jnp.float32)
    adjoint_field = mask_float * forcing / diag_coef
    for sweep in range(SWEEPS):
        coupled = couple(adjoint_field, face_coef, time_coef, jac_up, jac_down, spectral_matrix)
        adjoint_field = mask_float * (forcing - coupled) / diag_coef
    inlet_plane = adjoint_field[..., 0]
    results = []
    for inst in range(HB_SNAPSHOTS):
        first = owner[inst]
        weight = first_panel_share[inst]
        accum = jnp.zeros((FLD, NPT, NR), jnp.float32)
        accum = accum.at[:, first, radial_index].add(weight * inlet_plane[inst])
        accum = accum.at[:, first + 1, radial_index].add((1.0 - weight) * inlet_plane[inst])
        results.append(accum)
    return adjoint_field, jnp.stack(results)
```

```python
import functools

import jax
import jax.numpy as jnp
import ml_dtypes
import numpy as np
from jax import lax
from jax.experimental import pallas as pl
from jax.experimental.pallas import tpu as pltpu
from jax.sharding import PartitionSpec as P

SWEEPS = 4
NT = 11
NF = 7
ROWS = NT * NF
PAD = 80
NMAT = 7
SPANS = 8
PT = 4
LANES = 128
F32 = jnp.float32
BF16 = jnp.bfloat16
HIGHEST = lax.Precision.HIGHEST
MESH = pl.DeviceIdType.MESH


def constant_tables():
    row = np.arange(PAD)
    col = np.arange(3 * PAD)
    piece, within = col // PAD, col % PAD
    valid_row, valid_col = row < ROWS, within < ROWS
    expand_rows = ((row[:, None] % NF == np.arange(NF)) & valid_row[:, None]).astype(np.float32)
    expand_cols = ((within[None, :] % NF == np.arange(NF)[:, None]) & valid_col).astype(np.float32)
    same_instance = (row[:, None] // NF == within[None, :] // NF) & valid_row[:, None] & valid_col
    instance_rows = ((row[:, None] // NF == np.arange(NT)) & valid_row[:, None]).astype(np.float32)
    step = np.arange(NT)[:, None] - np.arange(NT)[None, :]
    sines = np.where(step == 0, 1.0, np.sin(np.pi * step / NT))
    spectral = np.where(step == 0, 0.0, 0.5 * (1.0 - 2.0 * (step % 2)) / sines)
    time_op = np.zeros((PAD, PAD), np.float32)
    time_op[:ROWS, :ROWS] = np.kron(spectral.T, np.eye(NF))
    high = time_op.astype(ml_dtypes.bfloat16)
    low = (time_op - high.astype(np.float32)).astype(ml_dtypes.bfloat16)
    time_op = np.concatenate([high, high, low], axis=1)
    return expand_rows, expand_cols, same_instance.astype(np.float32), instance_rows, time_op


def shift_of(instance, count):
    return ((instance * count) // (NT - 1) - instance // (NT - 1)) % count


def split(value):
    high = value.astype(BF16)
    low = (value - high.astype(F32)).astype(BF16)
    return high, low


def kernel(
    ns,
    nr,
    rhs,
    diag,
    face,
    time,
    jac_up,
    jac_down,
    wall,
    stator,
    owner,
    share,
    expand_rows,
    expand_cols,
    same_instance,
    instance_rows,
    time_op,
    out,
    sens,
    weights,
    coef,
    base,
    t_buf,
    tu_buf,
    td_buf,
    ru_buf,
    rd_buf,
    xu_buf,
    xd_buf,
    su_buf,
    sd_buf,
    panel_send,
    panel_recv,
    panel_rows,
    panel_weight,
    inlet,
    back_send,
    back_recv,
    theta_send,
    theta_recv,
    span_send,
    span_recv,
    panel_sems,
    back_sems,
):
    sector = lax.axis_index("sector")
    span = lax.axis_index("span")
    shifts = [shift_of(t, ns) for t in range(NT)]
    partners = sorted({d % ns for s in shifts for d in (s, -s)} | {1 % ns, (ns - 1) % ns})
    partners = [d for d in partners if d != 0]

    def at_sector(step):
        return {"sector": lax.rem(sector + step, ns)}

    ru_buf[:, SPANS] = jnp.zeros((SWEEPS,) + ru_buf.shape[2:], F32)
    rd_buf[:, 0] = jnp.zeros((SWEEPS,) + rd_buf.shape[2:], F32)

    barrier = pltpu.get_barrier_semaphore()
    for step in partners:
        pl.semaphore_signal(barrier, inc=1, device_id=at_sector(step), device_id_type=MESH)

    @pl.when(span > 0)
    def _():
        pl.semaphore_signal(barrier, inc=1, device_id={"span": span - 1}, device_id_type=MESH)

    @pl.when(span < nr - 1)
    def _():
        pl.semaphore_signal(barrier, inc=1, device_id={"span": span + 1}, device_id_type=MESH)

    lane = lax.broadcasted_iota(jnp.int32, (PAD, LANES), 1)
    panel_send[...] = jnp.zeros_like(panel_send)
    back_send[...] = jnp.zeros_like(back_send)
    for t in range(NT):
        for p in range(PT):
            panel_send[t, 0:NF, p * SPANS : (p + 1) * SPANS] = stator[t, :, p, :]

    beside = (span > 0).astype(jnp.int32) + (span < nr - 1).astype(jnp.int32)
    pl.semaphore_wait(barrier, len(partners) + beside)

    def panel_copy(t):
        return pltpu.make_async_remote_copy(
            src_ref=panel_send.at[t],
            dst_ref=panel_recv.at[t],
            send_sem=panel_sems.at[0, t],
            recv_sem=panel_sems.at[1, t],
            device_id=at_sector(ns - shifts[t]),
            device_id_type=MESH,
        )

    def back_copy(t):
        return pltpu.make_async_remote_copy(
            src_ref=back_send.at[t],
            dst_ref=back_recv.at[t],
            send_sem=back_sems.at[0, t],
            recv_sem=back_sems.at[1, t],
            device_id=at_sector(shifts[t]),
            device_id_type=MESH,
        )

    for t in range(NT):
        if shifts[t]:
            panel_copy(t).start()

    weights[0:PAD, :] = time_op[...]
    for direction in range(3):
        for side, table in enumerate((jac_up, jac_down)):
            block = jnp.dot(expand_rows[...], table[direction], precision=HIGHEST, preferred_element_type=F32)
            block = jnp.dot(block, expand_cols[...], precision=HIGHEST, preferred_element_type=F32)
            block = block * same_instance[...]
            high, low = split(block)
            piece = lax.broadcasted_iota(jnp.int32, block.shape, 1)
            start = (1 + 2 * direction + side) * PAD
            weights[start : start + PAD, :] = jnp.where(
                piece < 2 * PAD, high.astype(F32), low.astype(F32)
            ).astype(BF16)

    inverse = wall[...].astype(F32) / diag[...]
    axial_lane = lax.broadcasted_iota(jnp.int32, inverse.shape, 1)
    axial = inverse * face[2]
    coef[0] = inverse
    coef[1] = inverse * time[...]
    coef[2] = inverse * face[0]
    coef[3] = inverse * face[1]
    coef[4] = jnp.where(axial_lane == LANES - 1, 0.0, axial)
    coef[5] = jnp.where(axial_lane == 0, 0.0, axial)

    for a in range(2):
        spread = jnp.dot(instance_rows[...], share[:, a, :], precision=HIGHEST, preferred_element_type=F32)
        first = jnp.bitwise_and(owner[:, a, :], PT - 1).astype(F32)
        first = jnp.dot(instance_rows[...], first, preferred_element_type=F32)
        for p in range(PT):
            lower = jnp.where(first == p, spread, 0.0)
            upper = jnp.where(first == p - 1, 1.0 - spread, 0.0)
            panel_weight[a, p, :, 0:SPANS] = lower + upper

    panel_rows[...] = jnp.zeros_like(panel_rows)
    for t in range(NT):
        if shifts[t]:
            panel_copy(t).wait_recv()
            panel_rows[t * NF : (t + 1) * NF, :] = panel_recv[t, 0:NF, :]
        else:
            panel_rows[t * NF : (t + 1) * NF, :] = panel_send[t, 0:NF, :]
    seam = []
    for a in range(2):
        total = jnp.zeros((PAD, LANES), F32)
        for p in range(PT):
            moved = panel_rows[...]
            if p:
                moved = pltpu.roll(moved, LANES - p * SPANS, 1)
            total = total + jnp.where(lane < SPANS, panel_weight[a, p] * moved, 0.0)
        seam.append(total)

    base[...] = jnp.zeros_like(base)
    for r in range(SPANS):
        for a in range(2):
            moved = seam[a] if r == 0 else pltpu.roll(seam[a], LANES - r, 1)
            moved = jnp.where(lane == 0, moved, 0.0)
            plane = rhs[pl.ds(a * SPANS + r, ROWS, stride=2 * SPANS), :] + moved[0:ROWS]
            base[r, a, 0:ROWS, :] = plane * coef[0, a * SPANS + r : a * SPANS + r + 1, :]

    def theta_copies(k, r):
        up = pltpu.make_async_remote_copy(
            src_ref=su_buf.at[k, r],
            dst_ref=tu_buf.at[k, r, 1],
            send_sem=theta_send.at[k, r, 0],
            recv_sem=theta_recv.at[k, r, 0],
            device_id=at_sector(ns - 1),
            device_id_type=MESH,
        )
        down = pltpu.make_async_remote_copy(
            src_ref=sd_buf.at[k, r],
            dst_ref=td_buf.at[k, r, 0],
            send_sem=theta_send.at[k, r, 1],
            recv_sem=theta_recv.at[k, r, 1],
            device_id=at_sector(1),
            device_id_type=MESH,
        )
        return up, down

    def to_lower_span(k):
        return pltpu.make_async_remote_copy(
            src_ref=ru_buf.at[k, 0],
            dst_ref=ru_buf.at[k, SPANS],
            send_sem=span_send.at[k, 0],
            recv_sem=span_recv.at[k, 0],
            device_id={"span": span - 1},
            device_id_type=MESH,
        )

    def to_upper_span(k):
        return pltpu.make_async_remote_copy(
            src_ref=rd_buf.at[k, SPANS],
            dst_ref=rd_buf.at[k, 0],
            send_sem=span_send.at[k, 1],
            recv_sem=span_recv.at[k, 1],
            device_id={"span": span + 1},
            device_id_type=MESH,
        )

    def row_at(i):
        return lax.rem(i, 2) * (SPANS - 1 - 2 * (i // 2)) + i // 2

    def emit(k, r, planes):
        columns = []
        for plane in planes:
            high, low = split(plane)
            columns.append(jnp.concatenate([high, low, high], axis=0))
        data = jnp.concatenate(columns, axis=1)
        product = jnp.dot(weights[...], data, preferred_element_type=F32)

        def part(m, a):
            return product[m * PAD : (m + 1) * PAD, a * LANES : (a + 1) * LANES]

        su_buf[k, r] = part(1, 0)
        sd_buf[k, r] = part(2, 1)
        for copy in theta_copies(k, r):
            copy.start()
        for a in range(2):
            ru_buf[k, r, a] = part(3, a)
            rd_buf[k, r + 1, a] = part(4, a)

        @pl.when((r == 0) & (span > 0))
        def _():
            to_lower_span(k).start()

        @pl.when((r == SPANS - 1) & (span < nr - 1))
        def _():
            to_upper_span(k).start()

        tu_buf[k, r, 0] = part(1, 1)
        td_buf[k, r, 1] = part(2, 0)
        for a in range(2):
            t_buf[k, r, a] = part(0, a)
            xu_buf[k, r, a] = part(5, a)
            xd_buf[k, r, a] = part(6, a)

    def update(k, r):
        for copy in theta_copies(k, r):
            copy.wait_recv()

        @pl.when((r == SPANS - 1) & (span < nr - 1))
        def _():
            to_lower_span(k).wait_recv()

        @pl.when((r == 0) & (span > 0))
        def _():
            to_upper_span(k).wait_recv()

        planes = []
        for a in range(2):

            def coefficient(n):
                return coef[n, pl.ds(a * SPANS + r, 1), :]

            total = base[r, a] - coefficient(1) * t_buf[k, r, a]
            total = total - coefficient(2) * (tu_buf[k, r, a] + td_buf[k, r, a])
            total = total - coefficient(3) * (ru_buf[k, r + 1, a] + rd_buf[k, r, a])
            total = total - coefficient(4) * pltpu.roll(xu_buf[k, r, a], LANES - 1, 1)
            total = total - coefficient(5) * pltpu.roll(xd_buf[k, r, a], 1, 1)
            planes.append(total)
        return planes

    def first(i, carry):
        r = row_at(i)
        emit(0, r, [base[r, a] for a in range(2)])
        return carry

    lax.fori_loop(0, SPANS, first, 0)

    def middle(i, carry):
        k, r = i // SPANS, row_at(lax.rem(i, SPANS))
        emit(k + 1, r, update(k, r))
        return carry

    lax.fori_loop(0, (SWEEPS - 1) * SPANS, middle, 0)

    inlet[...] = jnp.zeros_like(inlet)

    def last(i, carry):
        r = row_at(i)
        planes = update(SWEEPS - 1, r)
        for a in range(2):
            out[pl.ds(a * SPANS + r, ROWS, stride=2 * SPANS), :] = planes[a][0:ROWS]
            inlet[a] = jnp.where(lane == r, pltpu.roll(planes[a], r, 1), inlet[a])
        return carry

    lax.fori_loop(0, SPANS, last, 0)

    back = jnp.zeros((PAD, LANES), F32)
    for p in range(PT):
        total = jnp.zeros((PAD, LANES), F32)
        for a in range(2):
            total = total + panel_weight[a, p] * inlet[a]
        total = jnp.where(lane < SPANS, total, 0.0)
        back = back + (pltpu.roll(total, p * SPANS, 1) if p else total)
    panel_rows[...] = back
    for t in range(NT):
        back_send[t, 0:NF, :] = panel_rows[t * NF : (t + 1) * NF, :]
        if shifts[t]:
            back_copy(t).start()
    for t in range(NT):
        if shifts[t]:
            back_copy(t).wait_recv()
            tile = back_recv[t, 0:NF, :]
        else:
            tile = back_send[t, 0:NF, :]
        for p in range(PT):
            sens[t, :, p, :] = tile[:, p * SPANS : (p + 1) * SPANS]

    for t in range(NT):
        if shifts[t]:
            panel_copy(t).wait_send()
            back_copy(t).wait_send()

    def drain(i, carry):
        k, r = i // SPANS, lax.rem(i, SPANS)
        for copy in theta_copies(k, r):
            copy.wait_send()
        return carry

    lax.fori_loop(0, SWEEPS * SPANS, drain, 0)
    for k in range(SWEEPS):

        @pl.when(span > 0)
        def _():
            to_lower_span(k).wait_send()

        @pl.when(span < nr - 1)
        def _():
            to_upper_span(k).wait_send()


def on_device(ns, nr, rhs, diag_coef, face_coef, time_coef, jac_up, jac_down, wall_mask, stator_adj, owner, share):
    nt, nf, ct, spans, nax = rhs.shape
    tables = constant_tables()
    plane = (SWEEPS, SPANS, 2, PAD, LANES)
    ring = (SWEEPS, SPANS + 1, 2, PAD, LANES)
    edge = (SWEEPS, SPANS, PAD, LANES)
    out, sens = pl.pallas_call(
        functools.partial(kernel, ns, nr),
        out_shape=(
            jax.ShapeDtypeStruct((nt * nf * ct * spans, nax), F32),
            jax.ShapeDtypeStruct(stator_adj.shape, F32),
        ),
        in_specs=[pl.BlockSpec(memory_space=pltpu.VMEM)] * (10 + len(tables)),
        out_specs=(pl.BlockSpec(memory_space=pltpu.VMEM),) * 2,
        scratch_shapes=[
            pltpu.VMEM((NMAT * PAD, 3 * PAD), BF16),
            pltpu.VMEM((6, 2 * SPANS, LANES), F32),
            pltpu.VMEM(plane[1:], F32),
            pltpu.VMEM(plane, F32),
            pltpu.VMEM(plane, F32),
            pltpu.VMEM(plane, F32),
            pltpu.VMEM(ring, F32),
            pltpu.VMEM(ring, F32),
            pltpu.VMEM(plane, F32),
            pltpu.VMEM(plane, F32),
            pltpu.VMEM(edge, F32),
            pltpu.VMEM(edge, F32),
            pltpu.VMEM((NT, 8, LANES), F32),
            pltpu.VMEM((NT, 8, LANES), F32),
            pltpu.VMEM((PAD, LANES), F32),
            pltpu.VMEM((2, PT, PAD, LANES), F32),
            pltpu.VMEM((2, PAD, LANES), F32),
            pltpu.VMEM((NT, 8, LANES), F32),
            pltpu.VMEM((NT, 8, LANES), F32),
            pltpu.SemaphoreType.DMA((SWEEPS, SPANS, 2)),
            pltpu.SemaphoreType.DMA((SWEEPS, SPANS, 2)),
            pltpu.SemaphoreType.DMA((SWEEPS, 2)),
            pltpu.SemaphoreType.DMA((SWEEPS, 2)),
            pltpu.SemaphoreType.DMA((2, NT)),
            pltpu.SemaphoreType.DMA((2, NT)),
        ],
        compiler_params=pltpu.CompilerParams(
            collective_id=0, has_side_effects=True, vmem_limit_bytes=56 * 2**20
        ),
    )(
        rhs.reshape(nt * nf * ct * spans, nax),
        diag_coef.reshape(ct * spans, nax),
        face_coef.reshape(3, ct * spans, nax),
        time_coef.reshape(ct * spans, nax),
        jac_up,
        jac_down,
        wall_mask.reshape(ct * spans, nax),
        stator_adj,
        owner,
        share,
        *tables,
    )
    return out.reshape(rhs.shape), sens


def solution(mesh):
    in_specs = (
        P(None, None, "sector", "span", None),
        P("sector", "span", None),
        P(None, "sector", "span", None),
        P("sector", "span", None),
        P(),
        P(),
        P("sector", "span", None),
        P(None, None, "sector", "span"),
        P(None, "sector", "span"),
        P(None, "sector", "span"),
    )
    out_specs = (P(None, None, "sector", "span", None), P(None, None, "sector", "span"))
    return jax.shard_map(
        functools.partial(on_device, mesh.shape["sector"], mesh.shape["span"]),
        mesh=mesh,
        in_specs=in_specs,
        out_specs=out_specs,
        check_vma=False,
    )
```

```python
import functools

import jax
import jax.numpy as jnp
import ml_dtypes
import numpy as np
from jax import lax
from jax.experimental import pallas as pl
from jax.experimental.pallas import tpu as pltpu
from jax.sharding import PartitionSpec as P

SWEEPS = 4
NT = 11
NF = 7
ROWS = NT * NF
PAD = 80
NMAT = 7
SPANS = 8
PT = 4
LANES = 128
WIDE = 256
F32 = jnp.float32
BF16 = jnp.bfloat16
HIGHEST = lax.Precision.HIGHEST
MESH = pl.DeviceIdType.MESH


def time_operator():
    step = np.arange(NT)[:, None] - np.arange(NT)[None, :]
    sines = np.where(step == 0, 1.0, np.sin(np.pi * step / NT))
    spectral = np.where(step == 0, 0.0, 0.5 * (1.0 - 2.0 * (step % 2)) / sines)
    table = np.zeros((PAD, PAD), np.float32)
    table[:ROWS, :ROWS] = np.kron(spectral.T, np.eye(NF))
    high = table.astype(ml_dtypes.bfloat16)
    low = (table - high.astype(np.float32)).astype(ml_dtypes.bfloat16)
    return np.concatenate([high, high, low], axis=1)


def shift_of(instance, count):
    return ((instance * count) // (NT - 1) - instance // (NT - 1)) % count


def split(value):
    high = value.astype(BF16)
    low = (value - high.astype(F32)).astype(BF16)
    return high, low


def index_of(shape, dim):
    return lax.broadcasted_iota(jnp.int32, shape, dim).astype(F32)


def over_fields(rows):
    instance = jnp.floor((rows + 0.5) * (1.0 / NF))
    return instance, rows - NF * instance


def exact_dot(left, right):
    return jnp.dot(left, right, precision=HIGHEST, preferred_element_type=F32)


def kernel(ns, nr, *refs):
    hbm, refs = refs[:11], refs[11:]
    (out, sens), refs = refs[:2], refs[2:]
    vmem, refs = refs[:11], refs[11:]
    rhs, diag, face, time, jac_up, jac_down, wall, stator, owner, share, time_op = vmem
    (
        weights,
        coef,
        base,
        t_buf,
        tu_buf,
        td_buf,
        ru_buf,
        rd_buf,
        xu_buf,
        xd_buf,
        su_buf,
        sd_buf,
        panel_send,
        panel_recv,
        panel_rows,
        panel_weight,
        inlet,
        back_send,
        back_recv,
        input_sems,
        theta_send,
        theta_recv,
        span_send,
        span_recv,
        panel_sems,
        back_sems,
    ) = refs
    sector = lax.axis_index("sector")
    span = lax.axis_index("span")
    shifts = [shift_of(t, ns) for t in range(NT)]
    partners = sorted({d % ns for s in shifts for d in (s, -s)} | {1 % ns, (ns - 1) % ns})
    partners = [d for d in partners if d != 0]

    def at_sector(step):
        return {"sector": lax.rem(sector + step, ns)}

    def load(n):
        return pltpu.make_async_copy(hbm[n], vmem[n], input_sems.at[n])

    for n in (7, 0, 1, 6, 8, 9, 4, 5, 10, 2, 3):
        load(n).start()

    ru_buf[:, SPANS] = jnp.zeros((SWEEPS,) + ru_buf.shape[2:], F32)
    rd_buf[:, 0] = jnp.zeros((SWEEPS,) + rd_buf.shape[2:], F32)

    barrier = pltpu.get_barrier_semaphore()
    for step in partners:
        pl.semaphore_signal(barrier, inc=1, device_id=at_sector(step), device_id_type=MESH)

    @pl.when(span > 0)
    def _():
        pl.semaphore_signal(barrier, inc=1, device_id={"span": span - 1}, device_id_type=MESH)

    @pl.when(span < nr - 1)
    def _():
        pl.semaphore_signal(barrier, inc=1, device_id={"span": span + 1}, device_id_type=MESH)

    wide = (NT, WIDE)
    load(7).wait()
    panel_rows[...] = jnp.zeros_like(panel_rows)
    panel_rows[0:NT, 0 : NF * PT * SPANS] = jnp.transpose(stator[...])
    for t in range(NT):
        panel_send[t, 0:1, :] = panel_rows[t : t + 1, :]

    beside = (span > 0).astype(jnp.int32) + (span < nr - 1).astype(jnp.int32)
    pl.semaphore_wait(barrier, len(partners) + beside)

    def panel_copy(t):
        return pltpu.make_async_remote_copy(
            src_ref=panel_send.at[t],
            dst_ref=panel_recv.at[t],
            send_sem=panel_sems.at[0, t],
            recv_sem=panel_sems.at[1, t],
            device_id=at_sector(ns - shifts[t]),
            device_id_type=MESH,
        )

    def back_copy(t):
        return pltpu.make_async_remote_copy(
            src_ref=back_send.at[t],
            dst_ref=back_recv.at[t],
            send_sem=back_sems.at[0, t],
            recv_sem=back_sems.at[1, t],
            device_id=at_sector(shifts[t]),
            device_id_type=MESH,
        )

    for t in range(NT):
        if shifts[t]:
            panel_copy(t).start()

    lane = lax.broadcasted_iota(jnp.int32, (PAD, LANES), 1)
    row = index_of((PAD, 3 * PAD), 0)
    column = index_of((PAD, 3 * PAD), 1)
    column = column - PAD * jnp.floor((column + 0.5) * (1.0 / PAD))
    row_instance, _ = over_fields(row)
    column_instance, _ = over_fields(column)
    same_instance = (row_instance == column_instance) & (row < ROWS) & (column < ROWS)
    _, row_field = over_fields(index_of((PAD, NF), 0))
    expand_rows = jnp.where(row_field == index_of((PAD, NF), 1), 1.0, 0.0)
    column = index_of((NF, 3 * PAD), 1)
    column = column - PAD * jnp.floor((column + 0.5) * (1.0 / PAD))
    expand_columns = jnp.where(over_fields(column)[1] == index_of((NF, 3 * PAD), 0), 1.0, 0.0)
    instance_rows = jnp.where(
        (over_fields(index_of((PAD, NT), 0))[0] == index_of((PAD, NT), 1)) & (index_of((PAD, NT), 0) < ROWS), 1.0, 0.0
    )
    instance_columns = jnp.where(
        (over_fields(index_of((NT, PAD), 1))[0] == index_of((NT, PAD), 0)) & (index_of((NT, PAD), 1) < ROWS), 1.0, 0.0
    )
    wide_lane = lax.broadcasted_iota(jnp.int32, (PAD, WIDE), 1)
    wide_field = lax.shift_right_logical(wide_lane, 5).astype(F32)
    same_field = over_fields(index_of((PAD, WIDE), 0))[1] == wide_field
    lane_panel = jnp.bitwise_and(lax.shift_right_logical(lax.broadcasted_iota(jnp.int32, wide, 1), 3), PT - 1)

    load(4).wait()
    load(5).wait()
    load(10).wait()
    weights[0:PAD, :] = time_op[...]
    for direction in range(3):
        for side, table in enumerate((jac_up, jac_down)):
            block = exact_dot(exact_dot(expand_rows, table[direction]), expand_columns)
            block = jnp.where(same_instance, block, 0.0)
            high, low = split(block)
            piece = lax.broadcasted_iota(jnp.int32, block.shape, 1)
            start = (1 + 2 * direction + side) * PAD
            weights[start : start + PAD, :] = jnp.where(
                piece < 2 * PAD, high.astype(F32), low.astype(F32)
            ).astype(BF16)

    for n in (0, 1, 2, 3, 6, 8, 9):
        load(n).wait()
    inverse = wall[...].astype(F32) / diag[...]
    axial_lane = lax.broadcasted_iota(jnp.int32, inverse.shape, 1)
    axial = inverse * face[2]
    coef[0] = inverse
    coef[1] = inverse * time[...]
    coef[2] = inverse * face[0]
    coef[3] = inverse * face[1]
    coef[4] = jnp.where(axial_lane == LANES - 1, 0.0, axial)
    coef[5] = jnp.where(axial_lane == 0, 0.0, axial)

    spread_lanes = lax.broadcasted_iota(jnp.int32, (SPANS, WIDE), 1)
    spread_span = jnp.where(
        jnp.bitwise_and(spread_lanes, SPANS - 1) == lax.broadcasted_iota(jnp.int32, (SPANS, WIDE), 0), 1.0, 0.0
    )
    for a in range(2):
        cells = pl.ds(a * SPANS, SPANS)
        share_wide = exact_dot(jnp.transpose(share[cells, :]), spread_span)
        first = jnp.bitwise_and(owner[cells, :], PT - 1).astype(F32)
        first_wide = exact_dot(jnp.transpose(first), spread_span)
        own_panel = lane_panel.astype(F32)
        lower = jnp.where(first_wide == own_panel, share_wide, 0.0)
        upper = jnp.where(first_wide == own_panel - 1.0, 1.0 - share_wide, 0.0)
        panel_weight[a] = lower + upper

    for t in range(NT):
        if shifts[t]:
            panel_copy(t).wait_recv()
            panel_rows[t : t + 1, :] = panel_recv[t, 0:1, :]
    cells_wide = jnp.zeros(wide, F32)
    for a in range(2):
        shares = panel_weight[a] * panel_rows[0:NT, :]
        shares = shares + pltpu.roll(shares, WIDE - SPANS, 1)
        shares = shares + pltpu.roll(shares, WIDE - 2 * SPANS, 1)
        if a:
            shares = pltpu.roll(shares, a * SPANS, 1)
        cells_wide = jnp.where(lane_panel == a, shares, cells_wide)
    spread = jnp.where(same_field, exact_dot(instance_rows, cells_wide), 0.0)
    gather_cells = jnp.where(
        jnp.bitwise_and(lax.broadcasted_iota(jnp.int32, (WIDE, LANES), 0), 4 * SPANS - 1)
        == lax.broadcasted_iota(jnp.int32, (WIDE, LANES), 1),
        1.0,
        0.0,
    )
    seam = exact_dot(spread, gather_cells)

    base[...] = jnp.zeros_like(base)
    for r in range(SPANS):
        for a in range(2):
            cell = a * SPANS + r
            moved = pltpu.roll(seam, LANES - cell, 1) if cell else seam
            moved = jnp.where(lane == 0, moved, 0.0)
            plane = rhs[pl.ds(cell, ROWS, stride=2 * SPANS), :] + moved[0:ROWS]
            base[r, a, 0:ROWS, :] = plane * coef[0, cell : cell + 1, :]

    def theta_copies(k, r):
        up = pltpu.make_async_remote_copy(
            src_ref=su_buf.at[k, r],
            dst_ref=tu_buf.at[k, r, 1],
            send_sem=theta_send.at[k, r, 0],
            recv_sem=theta_recv.at[k, r, 0],
            device_id=at_sector(ns - 1),
            device_id_type=MESH,
        )
        down = pltpu.make_async_remote_copy(
            src_ref=sd_buf.at[k, r],
            dst_ref=td_buf.at[k, r, 0],
            send_sem=theta_send.at[k, r, 1],
            recv_sem=theta_recv.at[k, r, 1],
            device_id=at_sector(1),
            device_id_type=MESH,
        )
        return up, down

    def to_lower_span(k):
        return pltpu.make_async_remote_copy(
            src_ref=ru_buf.at[k, 0],
            dst_ref=ru_buf.at[k, SPANS],
            send_sem=span_send.at[k, 0],
            recv_sem=span_recv.at[k, 0],
            device_id={"span": span - 1},
            device_id_type=MESH,
        )

    def to_upper_span(k):
        return pltpu.make_async_remote_copy(
            src_ref=rd_buf.at[k, SPANS],
            dst_ref=rd_buf.at[k, 0],
            send_sem=span_send.at[k, 1],
            recv_sem=span_recv.at[k, 1],
            device_id={"span": span + 1},
            device_id_type=MESH,
        )

    def row_at(i):
        return lax.rem(i, 2) * (SPANS - 1 - 2 * (i // 2)) + i // 2

    def emit(k, r, planes):
        columns = []
        for plane in planes:
            high, low = split(plane)
            columns.append(jnp.concatenate([high, low, high], axis=0))
        data = jnp.concatenate(columns, axis=1)
        product = jnp.dot(weights[...], data, preferred_element_type=F32)

        def part(m, a):
            return product[m * PAD : (m + 1) * PAD, a * LANES : (a + 1) * LANES]

        su_buf[k, r] = part(1, 0)
        sd_buf[k, r] = part(2, 1)
        for copy in theta_copies(k, r):
            copy.start()
        for a in range(2):
            ru_buf[k, r, a] = part(3, a)
            rd_buf[k, r + 1, a] = part(4, a)

        @pl.when((r == 0) & (span > 0))
        def _():
            to_lower_span(k).start()

        @pl.when((r == SPANS - 1) & (span < nr - 1))
        def _():
            to_upper_span(k).start()

        tu_buf[k, r, 0] = part(1, 1)
        td_buf[k, r, 1] = part(2, 0)
        for a in range(2):
            t_buf[k, r, a] = part(0, a)
            xu_buf[k, r, a] = part(5, a)
            xd_buf[k, r, a] = part(6, a)

    def update(k, r):
        for copy in theta_copies(k, r):
            copy.wait_recv()

        @pl.when((r == SPANS - 1) & (span < nr - 1))
        def _():
            to_lower_span(k).wait_recv()

        @pl.when((r == 0) & (span > 0))
        def _():
            to_upper_span(k).wait_recv()

        planes = []
        for a in range(2):

            def coefficient(n):
                return coef[n, pl.ds(a * SPANS + r, 1), :]

            total = base[r, a] - coefficient(1) * t_buf[k, r, a]
            total = total - coefficient(2) * (tu_buf[k, r, a] + td_buf[k, r, a])
            total = total - coefficient(3) * (ru_buf[k, r + 1, a] + rd_buf[k, r, a])
            total = total - coefficient(4) * pltpu.roll(xu_buf[k, r, a], LANES - 1, 1)
            total = total - coefficient(5) * pltpu.roll(xd_buf[k, r, a], 1, 1)
            planes.append(total)
        return planes

    def first(i, carry):
        r = row_at(i)
        emit(0, r, [base[r, a] for a in range(2)])
        return carry

    lax.fori_loop(0, SPANS, first, 0)

    def middle(i, carry):
        k, r = i // SPANS, row_at(lax.rem(i, SPANS))
        emit(k + 1, r, update(k, r))
        return carry

    lax.fori_loop(0, (SWEEPS - 1) * SPANS, middle, 0)

    inlet[...] = jnp.zeros_like(inlet)

    def last(i, carry):
        r = row_at(i)
        planes = update(SWEEPS - 1, r)
        for a in range(2):
            out[a * SPANS + r] = planes[a]
            inlet[...] = jnp.where(lane == a * SPANS + r, pltpu.roll(planes[a], a * SPANS + r, 1), inlet[...])
        return carry

    lax.fori_loop(0, SPANS, last, 0)

    back = jnp.zeros(wide, F32)
    for a in range(2):
        spread = exact_dot(inlet[:, a * SPANS : (a + 1) * SPANS], spread_span)
        spread = jnp.where(same_field, spread, 0.0)
        back = back + panel_weight[a] * exact_dot(instance_columns, spread)
    panel_rows[0:NT, :] = back
    for t in range(NT):
        if shifts[t]:
            back_send[t, 0:1, :] = panel_rows[t : t + 1, :]
            back_copy(t).start()
    for t in range(NT):
        if shifts[t]:
            back_copy(t).wait_recv()
            panel_rows[t : t + 1, :] = back_recv[t, 0:1, :]
    sens[...] = jnp.transpose(panel_rows[0:NT, 0 : NF * PT * SPANS])

    for t in range(NT):
        if shifts[t]:
            panel_copy(t).wait_send()
            back_copy(t).wait_send()

    def drain(i, carry):
        k, r = i // SPANS, lax.rem(i, SPANS)
        for copy in theta_copies(k, r):
            copy.wait_send()
        return carry

    lax.fori_loop(0, SWEEPS * SPANS, drain, 0)
    for k in range(SWEEPS):

        @pl.when(span > 0)
        def _():
            to_lower_span(k).wait_send()

        @pl.when(span < nr - 1)
        def _():
            to_upper_span(k).wait_send()


def store(planes, table, out, sens, sems):
    copies = [pltpu.make_async_copy(table, sens, sems.at[2 * SPANS])]
    for cell in range(2 * SPANS):
        copies.append(pltpu.make_async_copy(planes.at[cell, 0:ROWS], out.at[:, cell], sems.at[cell]))
    for copy in copies:
        copy.start()
    for copy in copies:
        copy.wait()


def on_device(ns, nr, rhs, diag_coef, face_coef, time_coef, jac_up, jac_down, wall_mask, stator_adj, owner, share):
    nt, nf, ct, spans, nax = rhs.shape
    plane = (SWEEPS, SPANS, 2, PAD, LANES)
    ring = (SWEEPS, SPANS + 1, 2, PAD, LANES)
    edge = (SWEEPS, SPANS, PAD, LANES)
    inputs = (
        rhs.reshape(nt * nf * ct * spans, nax),
        diag_coef.reshape(ct * spans, nax),
        face_coef.reshape(3, ct * spans, nax),
        time_coef.reshape(ct * spans, nax),
        jac_up,
        jac_down,
        wall_mask.reshape(ct * spans, nax),
        stator_adj.transpose(1, 2, 3, 0).reshape(nf * PT * spans, nt),
        owner.transpose(1, 2, 0).reshape(ct * spans, nt),
        share.transpose(1, 2, 0).reshape(ct * spans, nt),
        jnp.asarray(time_operator()),
    )
    planes, table = pl.pallas_call(
        functools.partial(kernel, ns, nr),
        out_shape=(
            pltpu.VMEM((ct * spans, PAD, nax), F32),
            pltpu.VMEM((nf * PT * spans, nt), F32),
        ),
        in_specs=[pl.BlockSpec(memory_space=pltpu.HBM)] * len(inputs),
        out_specs=(pl.BlockSpec(memory_space=pltpu.VMEM),) * 2,
        scratch_shapes=[pltpu.VMEM(x.shape, x.dtype) for x in inputs]
        + [
            pltpu.VMEM((NMAT * PAD, 3 * PAD), BF16),
            pltpu.VMEM((6, 2 * SPANS, LANES), F32),
            pltpu.VMEM(plane[1:], F32),
            pltpu.VMEM(plane, F32),
            pltpu.VMEM(plane, F32),
            pltpu.VMEM(plane, F32),
            pltpu.VMEM(ring, F32),
            pltpu.VMEM(ring, F32),
            pltpu.VMEM(plane, F32),
            pltpu.VMEM(plane, F32),
            pltpu.VMEM(edge, F32),
            pltpu.VMEM(edge, F32),
            pltpu.VMEM((NT, 1, WIDE), F32),
            pltpu.VMEM((NT, 1, WIDE), F32),
            pltpu.VMEM((16, WIDE), F32),
            pltpu.VMEM((2, NT, WIDE), F32),
            pltpu.VMEM((PAD, LANES), F32),
            pltpu.VMEM((NT, 1, WIDE), F32),
            pltpu.VMEM((NT, 1, WIDE), F32),
            pltpu.SemaphoreType.DMA((len(inputs),)),
            pltpu.SemaphoreType.DMA((SWEEPS, SPANS, 2)),
            pltpu.SemaphoreType.DMA((SWEEPS, SPANS, 2)),
            pltpu.SemaphoreType.DMA((SWEEPS, 2)),
            pltpu.SemaphoreType.DMA((SWEEPS, 2)),
            pltpu.SemaphoreType.DMA((2, NT)),
            pltpu.SemaphoreType.DMA((2, NT)),
        ],
        compiler_params=pltpu.CompilerParams(
            collective_id=0, has_side_effects=True, vmem_limit_bytes=60 * 2**20
        ),
    )(*inputs)
    out, sens = pl.pallas_call(
        store,
        out_shape=(
            jax.ShapeDtypeStruct((nt * nf, ct * spans, nax), F32),
            jax.ShapeDtypeStruct((nf * PT * spans, nt), F32),
        ),
        in_specs=[pl.BlockSpec(memory_space=pltpu.VMEM)] * 2,
        out_specs=(pl.BlockSpec(memory_space=pltpu.HBM),) * 2,
        scratch_shapes=[pltpu.SemaphoreType.DMA((2 * SPANS + 1,))],
    )(pltpu.with_memory_space_constraint(planes, pltpu.VMEM), pltpu.with_memory_space_constraint(table, pltpu.VMEM))
    sens = sens.reshape(nf, PT, spans, nt).transpose(3, 0, 1, 2)
    return out.reshape(rhs.shape), sens


def solution(mesh):
    in_specs = (
        P(None, None, "sector", "span", None),
        P("sector", "span", None),
        P(None, "sector", "span", None),
        P("sector", "span", None),
        P(),
        P(),
        P("sector", "span", None),
        P(None, None, "sector", "span"),
        P(None, "sector", "span"),
        P(None, "sector", "span"),
    )
    out_specs = (P(None, None, "sector", "span", None), P(None, None, "sector", "span"))
    return jax.shard_map(
        functools.partial(on_device, mesh.shape["sector"], mesh.shape["span"]),
        mesh=mesh,
        in_specs=in_specs,
        out_specs=out_specs,
        check_vma=False,
    )
```

```python
import functools

import jax
import jax.numpy as jnp
import ml_dtypes
import numpy as np
from jax import lax
from jax.experimental import pallas as pl
from jax.experimental.pallas import tpu as pltpu
from jax.sharding import PartitionSpec as P

SWEEPS = 4
NT = 11
NF = 7
ROWS = NT * NF
PAD = 80
NMAT = 7
SPANS = 8
PT = 4
LANES = 128
WIDE = 256
F32 = jnp.float32
BF16 = jnp.bfloat16
HIGHEST = lax.Precision.HIGHEST
MESH = pl.DeviceIdType.MESH


def time_operator():
    step = np.arange(NT)[:, None] - np.arange(NT)[None, :]
    sines = np.where(step == 0, 1.0, np.sin(np.pi * step / NT))
    spectral = np.where(step == 0, 0.0, 0.5 * (1.0 - 2.0 * (step % 2)) / sines)
    table = np.zeros((PAD, PAD), np.float32)
    table[:ROWS, :ROWS] = np.kron(spectral.T, np.eye(NF))
    high = table.astype(ml_dtypes.bfloat16)
    low = (table - high.astype(np.float32)).astype(ml_dtypes.bfloat16)
    return np.concatenate([high, high, low], axis=1)


def shift_of(instance, count):
    return ((instance * count) // (NT - 1) - instance // (NT - 1)) % count


def split(value):
    high = value.astype(BF16)
    low = (value - high.astype(F32)).astype(BF16)
    return high, low


def index_of(shape, dim):
    return lax.broadcasted_iota(jnp.int32, shape, dim).astype(F32)


def over_fields(rows):
    instance = jnp.floor((rows + 0.5) * (1.0 / NF))
    return instance, rows - NF * instance


def exact_dot(left, right):
    return jnp.dot(left, right, precision=HIGHEST, preferred_element_type=F32)


def kernel(ns, nr, *refs):
    hbm, refs = refs[:11], refs[11:]
    (out, sens), refs = refs[:2], refs[2:]
    vmem, refs = refs[:11], refs[11:]
    rhs, diag, face, time, jac_up, jac_down, wall, stator, owner, share, time_op = vmem
    (
        weights,
        coef,
        base,
        t_buf,
        tu_buf,
        td_buf,
        ru_buf,
        rd_buf,
        xu_buf,
        xd_buf,
        su_buf,
        sd_buf,
        panel_send,
        panel_recv,
        panel_rows,
        panel_weight,
        inlet,
        back_send,
        back_recv,
        jac_rows,
        delta_send,
        delta_recv,
        delta_columns,
        delta_shift,
        input_sems,
        theta_send,
        theta_recv,
        span_send,
        span_recv,
        panel_sems,
        back_sems,
        delta_sems,
    ) = refs
    sector = lax.axis_index("sector")
    span = lax.axis_index("span")
    shifts = [shift_of(t, ns) for t in range(NT)]
    partners = sorted({d % ns for s in shifts for d in (s, -s)} | {1 % ns, (ns - 1) % ns})
    partners = [d for d in partners if d != 0]

    def at_sector(step):
        return {"sector": lax.rem(sector + step, ns)}

    def load(n):
        return pltpu.make_async_copy(hbm[n], vmem[n], input_sems.at[n])

    for n in (7, 0, 1, 6, 8, 9, 4, 5, 10, 2, 3):
        load(n).start()

    ru_buf[:, SPANS] = jnp.zeros((SWEEPS,) + ru_buf.shape[2:], F32)
    rd_buf[:, 0] = jnp.zeros((SWEEPS,) + rd_buf.shape[2:], F32)

    delta_recv[...] = jnp.zeros_like(delta_recv)

    barrier = pltpu.get_barrier_semaphore()
    for step in partners:
        pl.semaphore_signal(barrier, inc=1, device_id=at_sector(step), device_id_type=MESH)

    @pl.when(span > 0)
    def _():
        pl.semaphore_signal(barrier, inc=1, device_id={"span": span - 1}, device_id_type=MESH)

    @pl.when(span < nr - 1)
    def _():
        pl.semaphore_signal(barrier, inc=1, device_id={"span": span + 1}, device_id_type=MESH)

    wide = (NT, WIDE)
    load(7).wait()
    panel_rows[...] = jnp.zeros_like(panel_rows)
    panel_rows[0:NT, 0 : NF * PT * SPANS] = jnp.transpose(stator[...])
    for t in range(NT):
        panel_send[t, 0:1, :] = panel_rows[t : t + 1, :]

    def panel_copy(t):
        return pltpu.make_async_remote_copy(
            src_ref=panel_send.at[t],
            dst_ref=panel_recv.at[t],
            send_sem=panel_sems.at[0, t],
            recv_sem=panel_sems.at[1, t],
            device_id=at_sector(ns - shifts[t]),
            device_id_type=MESH,
        )

    def back_copy(t):
        return pltpu.make_async_remote_copy(
            src_ref=back_send.at[t],
            dst_ref=back_recv.at[t],
            send_sem=back_sems.at[0, t],
            recv_sem=back_sems.at[1, t],
            device_id=at_sector(shifts[t]),
            device_id_type=MESH,
        )

    lane = lax.broadcasted_iota(jnp.int32, (PAD, LANES), 1)
    row = index_of((PAD, 3 * PAD), 0)
    column = index_of((PAD, 3 * PAD), 1)
    column = column - PAD * jnp.floor((column + 0.5) * (1.0 / PAD))
    row_instance, _ = over_fields(row)
    column_instance, _ = over_fields(column)
    same_instance = (row_instance == column_instance) & (row < ROWS) & (column < ROWS)
    instance_rows = jnp.where(
        (over_fields(index_of((PAD, NT), 0))[0] == index_of((PAD, NT), 1)) & (index_of((PAD, NT), 0) < ROWS), 1.0, 0.0
    )
    instance_columns = jnp.where(
        (over_fields(index_of((NT, PAD), 1))[0] == index_of((NT, PAD), 0)) & (index_of((NT, PAD), 1) < ROWS), 1.0, 0.0
    )
    wide_lane = lax.broadcasted_iota(jnp.int32, (PAD, WIDE), 1)
    wide_field = lax.shift_right_logical(wide_lane, 5).astype(F32)
    same_field = over_fields(index_of((PAD, WIDE), 0))[1] == wide_field
    lane_panel = jnp.bitwise_and(lax.shift_right_logical(lax.broadcasted_iota(jnp.int32, wide, 1), 3), PT - 1)

    load(4).wait()
    load(5).wait()
    load(10).wait()
    jac_rows[...] = jnp.zeros_like(jac_rows)
    for direction in range(3):
        for side, table in enumerate((jac_up, jac_down)):
            start = (2 * direction + side) * 8
            jac_rows[start : start + NF, 0:NF] = table[direction]
    high, low = split(jac_rows[...])
    wide_columns = index_of((8, 3 * PAD), 1)
    piece = jnp.floor((wide_columns + 0.5) * (1.0 / PAD))
    chosen = over_fields(wide_columns - PAD * piece)[1] == index_of((8, 3 * PAD), 0)
    pick_high = jnp.where(chosen & (piece < 2.0), 1.0, 0.0).astype(BF16)
    pick_low = jnp.where(chosen & (piece > 1.0), 1.0, 0.0).astype(BF16)
    columns = jnp.dot(high, pick_high, preferred_element_type=F32)
    columns = (columns + jnp.dot(low, pick_low, preferred_element_type=F32)).astype(BF16)
    _, field_of_row = over_fields(index_of((PAD, 8), 0))
    pick_row = jnp.where(field_of_row == index_of((PAD, 8), 1), 1.0, 0.0).astype(BF16)
    weights[0:PAD, :] = time_op[...]
    for m in range(1, NMAT):
        block = jnp.dot(pick_row, columns[8 * (m - 1) : 8 * m, :], preferred_element_type=F32)
        weights[m * PAD : (m + 1) * PAD, :] = jnp.where(same_instance, block, 0.0).astype(BF16)

    for n in (0, 1, 2, 3, 6, 8, 9):
        load(n).wait()
    inverse = wall[...].astype(F32) / diag[...]
    axial_lane = lax.broadcasted_iota(jnp.int32, inverse.shape, 1)
    axial = inverse * face[2]
    coef[0] = inverse
    coef[1] = inverse * time[...]
    coef[2] = inverse * face[0]
    coef[3] = inverse * face[1]
    coef[4] = jnp.where(axial_lane == LANES - 1, 0.0, axial)
    coef[5] = jnp.where(axial_lane == 0, 0.0, axial)
    coef[6] = jnp.zeros_like(inverse)
    coef[7] = jnp.zeros_like(inverse)
    coef_columns = jnp.transpose(coef[...].reshape(8 * 2 * SPANS, LANES))
    cell_lanes = jnp.bitwise_and(lax.broadcasted_iota(jnp.int32, (LANES, WIDE), 1), 4 * SPANS - 1)
    to_cells = jnp.where(
        (cell_lanes == lax.broadcasted_iota(jnp.int32, (LANES, WIDE), 0)) & (cell_lanes < 2 * SPANS), 1.0, 0.0
    )
    inlet_inverse = exact_dot(coef_columns[0:8, :], to_cells)[0:1, :]

    spread_lanes = lax.broadcasted_iota(jnp.int32, (SPANS, WIDE), 1)
    spread_span = jnp.where(
        jnp.bitwise_and(spread_lanes, SPANS - 1) == lax.broadcasted_iota(jnp.int32, (SPANS, WIDE), 0), 1.0, 0.0
    )
    for a in range(2):
        cells = pl.ds(a * SPANS, SPANS)
        share_wide = exact_dot(jnp.transpose(share[cells, :]), spread_span)
        first = jnp.bitwise_and(owner[cells, :], PT - 1).astype(F32)
        first_wide = exact_dot(jnp.transpose(first), spread_span)
        own_panel = lane_panel.astype(F32)
        lower = jnp.where(first_wide == own_panel, share_wide, 0.0)
        upper = jnp.where(first_wide == own_panel - 1.0, 1.0 - share_wide, 0.0)
        panel_weight[a] = lower + upper

    base[...] = jnp.zeros_like(base)
    for r in range(SPANS):
        for a in range(2):
            cell = a * SPANS + r
            plane = rhs[pl.ds(cell, ROWS, stride=2 * SPANS), :]
            base[r, a, 0:ROWS, :] = plane * coef[0, cell : cell + 1, :]

    beside = (span > 0).astype(jnp.int32) + (span < nr - 1).astype(jnp.int32)
    pl.semaphore_wait(barrier, len(partners) + beside)

    for t in range(NT):
        if shifts[t]:
            panel_copy(t).start()

    def theta_copies(k, r):
        up = pltpu.make_async_remote_copy(
            src_ref=su_buf.at[k, r],
            dst_ref=tu_buf.at[k, r, 1],
            send_sem=theta_send.at[k, r, 0],
            recv_sem=theta_recv.at[k, r, 0],
            device_id=at_sector(ns - 1),
            device_id_type=MESH,
        )
        down = pltpu.make_async_remote_copy(
            src_ref=sd_buf.at[k, r],
            dst_ref=td_buf.at[k, r, 0],
            send_sem=theta_send.at[k, r, 1],
            recv_sem=theta_recv.at[k, r, 1],
            device_id=at_sector(1),
            device_id_type=MESH,
        )
        return up, down

    def to_lower_span(k):
        return pltpu.make_async_remote_copy(
            src_ref=ru_buf.at[k, 0],
            dst_ref=ru_buf.at[k, SPANS],
            send_sem=span_send.at[k, 0],
            recv_sem=span_recv.at[k, 0],
            device_id={"span": span - 1},
            device_id_type=MESH,
        )

    def to_upper_span(k):
        return pltpu.make_async_remote_copy(
            src_ref=rd_buf.at[k, SPANS],
            dst_ref=rd_buf.at[k, 0],
            send_sem=span_send.at[k, 1],
            recv_sem=span_recv.at[k, 1],
            device_id={"span": span + 1},
            device_id_type=MESH,
        )

    def row_at(i):
        return lax.rem(i, 2) * (SPANS - 1 - 2 * (i // 2)) + i // 2

    def emit(k, r, planes):
        columns = []
        for plane in planes:
            high, low = split(plane)
            columns.append(jnp.concatenate([high, low, high], axis=0))
        data = jnp.concatenate(columns, axis=1)
        product = jnp.dot(weights[...], data, preferred_element_type=F32)

        def part(m, a):
            return product[m * PAD : (m + 1) * PAD, a * LANES : (a + 1) * LANES]

        su_buf[k, r] = part(1, 0)
        sd_buf[k, r] = part(2, 1)
        for copy in theta_copies(k, r):
            copy.start()
        for a in range(2):
            ru_buf[k, r, a] = part(3, a)
            rd_buf[k, r + 1, a] = part(4, a)

        @pl.when((r == 0) & (span > 0))
        def _():
            to_lower_span(k).start()

        @pl.when((r == SPANS - 1) & (span < nr - 1))
        def _():
            to_upper_span(k).start()

        tu_buf[k, r, 0] = part(1, 1)
        td_buf[k, r, 1] = part(2, 0)
        for a in range(2):
            t_buf[k, r, a] = part(0, a)
            xu_buf[k, r, a] = part(5, a)
            xd_buf[k, r, a] = part(6, a)

    def update(k, r):
        for copy in theta_copies(k, r):
            copy.wait_recv()

        @pl.when((r == SPANS - 1) & (span < nr - 1))
        def _():
            to_lower_span(k).wait_recv()

        @pl.when((r == 0) & (span > 0))
        def _():
            to_upper_span(k).wait_recv()

        planes = []
        for a in range(2):

            def coefficient(n):
                return coef[n, pl.ds(a * SPANS + r, 1), :]

            total = base[r, a] - coefficient(1) * t_buf[k, r, a]
            total = total - coefficient(2) * (tu_buf[k, r, a] + td_buf[k, r, a])
            total = total - coefficient(3) * (ru_buf[k, r + 1, a] + rd_buf[k, r, a])
            total = total - coefficient(4) * pltpu.roll(xu_buf[k, r, a], LANES - 1, 1)
            total = total - coefficient(5) * pltpu.roll(xd_buf[k, r, a], 1, 1)
            planes.append(total)
        return planes

    def first(i, carry):
        r = row_at(i)
        emit(0, r, [base[r, a] for a in range(2)])
        return carry

    lax.fori_loop(0, SPANS, first, 0)

    for t in range(NT):
        if shifts[t]:
            panel_copy(t).wait_recv()
            panel_rows[t : t + 1, :] = panel_recv[t, 0:1, :]
    cells_wide = jnp.zeros(wide, F32)
    for a in range(2):
        shares = panel_weight[a] * panel_rows[0:NT, :]
        shares = shares + pltpu.roll(shares, WIDE - SPANS, 1)
        shares = shares + pltpu.roll(shares, WIDE - 2 * SPANS, 1)
        if a:
            shares = pltpu.roll(shares, a * SPANS, 1)
        cells_wide = jnp.where(lane_panel == a, shares, cells_wide)
    cells_wide = cells_wide * inlet_inverse
    delta_send[0:NT, :] = cells_wide

    def delta_copy(n, device):
        return pltpu.make_async_remote_copy(
            src_ref=delta_send,
            dst_ref=delta_recv.at[n],
            send_sem=delta_sems.at[0, n],
            recv_sem=delta_sems.at[1, n],
            device_id=device,
            device_id_type=MESH,
        )

    from_left = delta_copy(0, at_sector(1))
    from_right = delta_copy(1, at_sector(ns - 1))
    from_lower = delta_copy(2, {"span": span + 1})
    from_upper = delta_copy(3, {"span": span - 1})

    @pl.when(span < nr - 1)
    def _():
        from_lower.start()

    @pl.when(span > 0)
    def _():
        from_upper.start()

    from_left.start()
    from_right.start()
    from_left.wait_recv()
    from_right.wait_recv()

    @pl.when(span > 0)
    def _():
        from_lower.wait_recv()

    @pl.when(span < nr - 1)
    def _():
        from_upper.wait_recv()

    slot = jnp.bitwise_and(lax.broadcasted_iota(jnp.int32, wide, 1), 4 * SPANS - 1)

    def place(values, n, shift, low, high):
        moved = pltpu.roll(delta_recv[n, 0:NT, :], shift % WIDE, 1)
        return jnp.where((slot >= low) & (slot < high), moved, values)

    around = place(cells_wide, 0, SPANS, 2 * SPANS, 3 * SPANS)
    around = place(around, 1, 3 * SPANS, 3 * SPANS, 4 * SPANS)
    beyond = jnp.zeros(wide, F32)
    beyond = place(beyond, 2, 1 - SPANS, 0, 1)
    beyond = place(beyond, 2, 2 - 2 * SPANS, 1, 2)
    beyond = place(beyond, 3, 2, 2, 3)
    beyond = place(beyond, 3, 3 - SPANS, 3, 4)
    gather_slot = jnp.bitwise_and(lax.broadcasted_iota(jnp.int32, (WIDE, LANES), 0), 4 * SPANS - 1)
    gather_lane = lax.broadcasted_iota(jnp.int32, (WIDE, LANES), 1)
    columns = jnp.zeros((PAD, LANES), F32)
    for values, offset in ((around, 0), (beyond, 4 * SPANS)):
        spread = jnp.where(same_field, exact_dot(instance_rows, values), 0.0)
        gather = jnp.where(gather_slot + offset == gather_lane, 1.0, 0.0)
        columns = columns + exact_dot(spread, gather)
    high, low = split(columns)
    product = jnp.dot(weights[...], jnp.concatenate([high, low, high], axis=0), preferred_element_type=F32)

    def moved_part(m, shift):
        return pltpu.roll(product[m * PAD : (m + 1) * PAD, :], shift % LANES, 1)

    def inlet_coefficient(n, axial_cell):
        return pltpu.roll(coef_columns[axial_cell : axial_cell + 1, :], (LANES - 2 * SPANS * n) % LANES, 1)

    first_half = lane < SPANS
    along = jnp.where(first_half, moved_part(1, -SPANS), moved_part(1, -2 * SPANS))
    along = along + jnp.where(first_half, moved_part(2, -2 * SPANS), moved_part(2, SPANS))
    across = moved_part(3, -1)
    across = jnp.where(lane == SPANS - 1, moved_part(3, -(3 * SPANS + 3)), across)
    across = jnp.where(lane == 2 * SPANS - 1, moved_part(3, -(2 * SPANS + 4)), across)
    below = moved_part(4, 1)
    below = jnp.where(lane == 0, moved_part(4, -4 * SPANS), below)
    below = jnp.where(lane == SPANS, moved_part(4, -(3 * SPANS + 1)), below)
    coupled = inlet_coefficient(1, 0) * product[0:PAD, :]
    coupled = coupled + inlet_coefficient(2, 0) * along
    coupled = coupled + inlet_coefficient(3, 0) * (across + below)
    delta_columns[...] = columns
    delta_shift[0] = coupled
    delta_shift[1] = inlet_coefficient(5, 1) * product[6 * PAD : 7 * PAD, :]

    def second(i, carry):
        r = row_at(i)
        planes = []
        for a in range(2):
            shift = lax.rem(LANES - a * SPANS - r, LANES)
            moved = pltpu.roll(delta_columns[...], shift, 1)
            base[r, a] = base[r, a] + jnp.where(lane == 0, moved, 0.0)
        for a, plane in enumerate(update(0, r)):
            shift = lax.rem(LANES - a * SPANS - r, LANES)
            plane = plane - jnp.where(lane == 0, pltpu.roll(delta_shift[0], shift, 1), 0.0)
            shift = lax.rem(shift + 1, LANES)
            planes.append(plane - jnp.where(lane == 1, pltpu.roll(delta_shift[1], shift, 1), 0.0))
        emit(1, r, planes)
        return carry

    lax.fori_loop(0, SPANS, second, 0)

    def middle(i, carry):
        k, r = i // SPANS + 1, row_at(lax.rem(i, SPANS))
        emit(k + 1, r, update(k, r))
        return carry

    lax.fori_loop(0, (SWEEPS - 2) * SPANS, middle, 0)

    inlet[...] = jnp.zeros_like(inlet)

    def last(i, carry):
        r = row_at(i)
        planes = update(SWEEPS - 1, r)
        for a in range(2):
            out[a * SPANS + r] = planes[a]
            inlet[...] = jnp.where(lane == a * SPANS + r, pltpu.roll(planes[a], a * SPANS + r, 1), inlet[...])
        return carry

    lax.fori_loop(0, SPANS, last, 0)

    back = jnp.zeros(wide, F32)
    for a in range(2):
        spread = exact_dot(inlet[:, a * SPANS : (a + 1) * SPANS], spread_span)
        spread = jnp.where(same_field, spread, 0.0)
        back = back + panel_weight[a] * exact_dot(instance_columns, spread)
    panel_rows[0:NT, :] = back
    for t in range(NT):
        if shifts[t]:
            back_send[t, 0:1, :] = panel_rows[t : t + 1, :]
            back_copy(t).start()
    for t in range(NT):
        if shifts[t]:
            back_copy(t).wait_recv()
            panel_rows[t : t + 1, :] = back_recv[t, 0:1, :]
    sens[...] = jnp.transpose(panel_rows[0:NT, 0 : NF * PT * SPANS])

    for t in range(NT):
        if shifts[t]:
            panel_copy(t).wait_send()
            back_copy(t).wait_send()

    from_left.wait_send()
    from_right.wait_send()

    @pl.when(span < nr - 1)
    def _():
        from_lower.wait_send()

    @pl.when(span > 0)
    def _():
        from_upper.wait_send()

    def drain(i, carry):
        k, r = i // SPANS, lax.rem(i, SPANS)
        for copy in theta_copies(k, r):
            copy.wait_send()
        return carry

    lax.fori_loop(0, SWEEPS * SPANS, drain, 0)
    for k in range(SWEEPS):

        @pl.when(span > 0)
        def _():
            to_lower_span(k).wait_send()

        @pl.when(span < nr - 1)
        def _():
            to_upper_span(k).wait_send()


def store(planes, table, out, sens, sems):
    copies = [pltpu.make_async_copy(table, sens, sems.at[2 * SPANS])]
    for cell in range(2 * SPANS):
        copies.append(pltpu.make_async_copy(planes.at[cell, 0:ROWS], out.at[:, cell], sems.at[cell]))
    for copy in copies:
        copy.start()
    for copy in copies:
        copy.wait()


def on_device(ns, nr, rhs, diag_coef, face_coef, time_coef, jac_up, jac_down, wall_mask, stator_adj, owner, share):
    nt, nf, ct, spans, nax = rhs.shape
    plane = (SWEEPS, SPANS, 2, PAD, LANES)
    ring = (SWEEPS, SPANS + 1, 2, PAD, LANES)
    edge = (SWEEPS, SPANS, PAD, LANES)
    inputs = (
        rhs.reshape(nt * nf * ct * spans, nax),
        diag_coef.reshape(ct * spans, nax),
        face_coef.reshape(3, ct * spans, nax),
        time_coef.reshape(ct * spans, nax),
        jac_up,
        jac_down,
        wall_mask.reshape(ct * spans, nax),
        stator_adj.transpose(1, 2, 3, 0).reshape(nf * PT * spans, nt),
        owner.transpose(1, 2, 0).reshape(ct * spans, nt),
        share.transpose(1, 2, 0).reshape(ct * spans, nt),
        jnp.asarray(time_operator()),
    )
    planes, table = pl.pallas_call(
        functools.partial(kernel, ns, nr),
        out_shape=(
            pltpu.VMEM((ct * spans, PAD, nax), F32),
            pltpu.VMEM((nf * PT * spans, nt), F32),
        ),
        in_specs=[pl.BlockSpec(memory_space=pltpu.HBM)] * len(inputs),
        out_specs=(pl.BlockSpec(memory_space=pltpu.VMEM),) * 2,
        scratch_shapes=[pltpu.VMEM(x.shape, x.dtype) for x in inputs]
        + [
            pltpu.VMEM((NMAT * PAD, 3 * PAD), BF16),
            pltpu.VMEM((8, 2 * SPANS, LANES), F32),
            pltpu.VMEM(plane[1:], F32),
            pltpu.VMEM(plane, F32),
            pltpu.VMEM(plane, F32),
            pltpu.VMEM(plane, F32),
            pltpu.VMEM(ring, F32),
            pltpu.VMEM(ring, F32),
            pltpu.VMEM(plane, F32),
            pltpu.VMEM(plane, F32),
            pltpu.VMEM(edge, F32),
            pltpu.VMEM(edge, F32),
            pltpu.VMEM((NT, 1, WIDE), F32),
            pltpu.VMEM((NT, 1, WIDE), F32),
            pltpu.VMEM((16, WIDE), F32),
            pltpu.VMEM((2, NT, WIDE), F32),
            pltpu.VMEM((PAD, LANES), F32),
            pltpu.VMEM((NT, 1, WIDE), F32),
            pltpu.VMEM((NT, 1, WIDE), F32),
            pltpu.VMEM((48, 8), F32),
            pltpu.VMEM((16, WIDE), F32),
            pltpu.VMEM((4, 16, WIDE), F32),
            pltpu.VMEM((PAD, LANES), F32),
            pltpu.VMEM((2, PAD, LANES), F32),
            pltpu.SemaphoreType.DMA((len(inputs),)),
            pltpu.SemaphoreType.DMA((SWEEPS, SPANS, 2)),
            pltpu.SemaphoreType.DMA((SWEEPS, SPANS, 2)),
            pltpu.SemaphoreType.DMA((SWEEPS, 2)),
            pltpu.SemaphoreType.DMA((SWEEPS, 2)),
            pltpu.SemaphoreType.DMA((2, NT)),
            pltpu.SemaphoreType.DMA((2, NT)),
            pltpu.SemaphoreType.DMA((2, 4)),
        ],
        compiler_params=pltpu.CompilerParams(
            collective_id=0, has_side_effects=True, vmem_limit_bytes=60 * 2**20
        ),
    )(*inputs)
    out, sens = pl.pallas_call(
        store,
        out_shape=(
            jax.ShapeDtypeStruct((nt * nf, ct * spans, nax), F32),
            jax.ShapeDtypeStruct((nf * PT * spans, nt), F32),
        ),
        in_specs=[pl.BlockSpec(memory_space=pltpu.VMEM)] * 2,
        out_specs=(pl.BlockSpec(memory_space=pltpu.HBM),) * 2,
        scratch_shapes=[pltpu.SemaphoreType.DMA((2 * SPANS + 1,))],
    )(pltpu.with_memory_space_constraint(planes, pltpu.VMEM), pltpu.with_memory_space_constraint(table, pltpu.VMEM))
    sens = sens.reshape(nf, PT, spans, nt).transpose(3, 0, 1, 2)
    return out.reshape(rhs.shape), sens


def solution(mesh):
    in_specs = (
        P(None, None, "sector", "span", None),
        P("sector", "span", None),
        P(None, "sector", "span", None),
        P("sector", "span", None),
        P(),
        P(),
        P("sector", "span", None),
        P(None, None, "sector", "span"),
        P(None, "sector", "span"),
        P(None, "sector", "span"),
    )
    out_specs = (P(None, None, "sector", "span", None), P(None, None, "sector", "span"))
    return jax.shard_map(
        functools.partial(on_device, mesh.shape["sector"], mesh.shape["span"]),
        mesh=mesh,
        in_specs=in_specs,
        out_specs=out_specs,
        check_vma=False,
    )
```

```python
import functools

import jax
import jax.numpy as jnp
import ml_dtypes
import numpy as np
from jax import lax
from jax.experimental import pallas as pl
from jax.experimental.pallas import tpu as pltpu
from jax.sharding import PartitionSpec as P

SWEEPS = 4
NT = 11
NF = 7
ROWS = NT * NF
PAD = 80
NMAT = 7
SPANS = 8
PT = 4
LANES = 128
WIDE = 256
F32 = jnp.float32
BF16 = jnp.bfloat16
HIGHEST = lax.Precision.HIGHEST
MESH = pl.DeviceIdType.MESH


def time_operator():
    step = np.arange(NT)[:, None] - np.arange(NT)[None, :]
    sines = np.where(step == 0, 1.0, np.sin(np.pi * step / NT))
    spectral = np.where(step == 0, 0.0, 0.5 * (1.0 - 2.0 * (step % 2)) / sines)
    table = np.zeros((PAD, PAD), np.float32)
    table[:ROWS, :ROWS] = np.kron(spectral.T, np.eye(NF))
    high = table.astype(ml_dtypes.bfloat16)
    low = (table - high.astype(np.float32)).astype(ml_dtypes.bfloat16)
    return np.concatenate([high, high, low], axis=1)


def shift_of(instance, count):
    return ((instance * count) // (NT - 1) - instance // (NT - 1)) % count


def split(value):
    high = value.astype(BF16)
    low = (value - high.astype(F32)).astype(BF16)
    return high, low


def index_of(shape, dim):
    return lax.broadcasted_iota(jnp.int32, shape, dim).astype(F32)


def over_fields(rows):
    instance = jnp.floor((rows + 0.5) * (1.0 / NF))
    return instance, rows - NF * instance


def exact_dot(left, right):
    return jnp.dot(left, right, precision=HIGHEST, preferred_element_type=F32)


def kernel(ns, nr, *refs):
    hbm, refs = refs[:11], refs[11:]
    (out, sens), refs = refs[:2], refs[2:]
    vmem, refs = refs[:11], refs[11:]
    rhs, diag, face, time, jac_up, jac_down, wall, stator, owner, share, time_op = vmem
    (
        weights,
        coef,
        base,
        own_buf,
        tu_buf,
        td_buf,
        ru_buf,
        rd_buf,
        su_buf,
        sd_buf,
        panel_send,
        panel_recv,
        panel_rows,
        panel_weight,
        inlet,
        back_send,
        back_recv,
        jac_rows,
        delta_send,
        delta_recv,
        delta_columns,
        delta_shift,
        input_sems,
        theta_send,
        theta_recv,
        span_send,
        span_recv,
        panel_sems,
        back_sems,
        delta_sems,
    ) = refs
    sector = lax.axis_index("sector")
    span = lax.axis_index("span")
    shifts = [shift_of(t, ns) for t in range(NT)]
    partners = sorted({d % ns for s in shifts for d in (s, -s)} | {1 % ns, (ns - 1) % ns})
    partners = [d for d in partners if d != 0]

    def at_sector(step):
        return {"sector": lax.rem(sector + step, ns)}

    def load(n):
        return pltpu.make_async_copy(hbm[n], vmem[n], input_sems.at[n])

    for n in (7, 0, 1, 6, 8, 9, 4, 5, 10, 2, 3):
        load(n).start()

    ru_buf[:, SPANS] = jnp.zeros((SWEEPS,) + ru_buf.shape[2:], F32)
    rd_buf[:, 0] = jnp.zeros((SWEEPS,) + rd_buf.shape[2:], F32)

    delta_recv[...] = jnp.zeros_like(delta_recv)

    barrier = pltpu.get_barrier_semaphore()
    for step in partners:
        pl.semaphore_signal(barrier, inc=1, device_id=at_sector(step), device_id_type=MESH)

    @pl.when(span > 0)
    def _():
        pl.semaphore_signal(barrier, inc=1, device_id={"span": span - 1}, device_id_type=MESH)

    @pl.when(span < nr - 1)
    def _():
        pl.semaphore_signal(barrier, inc=1, device_id={"span": span + 1}, device_id_type=MESH)

    wide = (NT, WIDE)
    load(7).wait()
    panel_rows[...] = jnp.zeros_like(panel_rows)
    panel_rows[0:NT, 0 : NF * PT * SPANS] = jnp.transpose(stator[...])
    for t in range(NT):
        panel_send[t, 0:1, :] = panel_rows[t : t + 1, :]

    def panel_copy(t):
        return pltpu.make_async_remote_copy(
            src_ref=panel_send.at[t],
            dst_ref=panel_recv.at[t],
            send_sem=panel_sems.at[0, t],
            recv_sem=panel_sems.at[1, t],
            device_id=at_sector(ns - shifts[t]),
            device_id_type=MESH,
        )

    def back_copy(t):
        return pltpu.make_async_remote_copy(
            src_ref=back_send.at[t],
            dst_ref=back_recv.at[t],
            send_sem=back_sems.at[0, t],
            recv_sem=back_sems.at[1, t],
            device_id=at_sector(shifts[t]),
            device_id_type=MESH,
        )

    lane = lax.broadcasted_iota(jnp.int32, (PAD, LANES), 1)
    row = index_of((PAD, 3 * PAD), 0)
    column = index_of((PAD, 3 * PAD), 1)
    column = column - PAD * jnp.floor((column + 0.5) * (1.0 / PAD))
    row_instance, _ = over_fields(row)
    column_instance, _ = over_fields(column)
    same_instance = (row_instance == column_instance) & (row < ROWS) & (column < ROWS)
    instance_rows = jnp.where(
        (over_fields(index_of((PAD, NT), 0))[0] == index_of((PAD, NT), 1)) & (index_of((PAD, NT), 0) < ROWS), 1.0, 0.0
    )
    instance_columns = jnp.where(
        (over_fields(index_of((NT, PAD), 1))[0] == index_of((NT, PAD), 0)) & (index_of((NT, PAD), 1) < ROWS), 1.0, 0.0
    )
    wide_lane = lax.broadcasted_iota(jnp.int32, (PAD, WIDE), 1)
    wide_field = lax.shift_right_logical(wide_lane, 5).astype(F32)
    same_field = over_fields(index_of((PAD, WIDE), 0))[1] == wide_field
    lane_panel = jnp.bitwise_and(lax.shift_right_logical(lax.broadcasted_iota(jnp.int32, wide, 1), 3), PT - 1)

    load(4).wait()
    load(5).wait()
    load(10).wait()
    jac_rows[...] = jnp.zeros_like(jac_rows)
    for direction in range(3):
        for side, table in enumerate((jac_up, jac_down)):
            start = (2 * direction + side) * 8
            jac_rows[start : start + NF, 0:NF] = table[direction]
    high, low = split(jac_rows[...])
    wide_columns = index_of((8, 3 * PAD), 1)
    piece = jnp.floor((wide_columns + 0.5) * (1.0 / PAD))
    chosen = over_fields(wide_columns - PAD * piece)[1] == index_of((8, 3 * PAD), 0)
    pick_high = jnp.where(chosen & (piece < 2.0), 1.0, 0.0).astype(BF16)
    pick_low = jnp.where(chosen & (piece > 1.0), 1.0, 0.0).astype(BF16)
    columns = jnp.dot(high, pick_high, preferred_element_type=F32)
    columns = (columns + jnp.dot(low, pick_low, preferred_element_type=F32)).astype(BF16)
    _, field_of_row = over_fields(index_of((PAD, 8), 0))
    pick_row = jnp.where(field_of_row == index_of((PAD, 8), 1), 1.0, 0.0).astype(BF16)
    weights[0:PAD, :] = time_op[...]
    for m in range(1, NMAT):
        block = jnp.dot(pick_row, columns[8 * (m - 1) : 8 * m, :], preferred_element_type=F32)
        weights[m * PAD : (m + 1) * PAD, :] = jnp.where(same_instance, block, 0.0).astype(BF16)

    for n in (0, 1, 2, 3, 6, 8, 9):
        load(n).wait()
    inverse = wall[...].astype(F32) / diag[...]
    axial_lane = lax.broadcasted_iota(jnp.int32, inverse.shape, 1)
    axial = inverse * face[2]
    coef[0] = inverse
    coef[1] = inverse * time[...]
    coef[2] = inverse * face[0]
    coef[3] = inverse * face[1]
    coef[4] = jnp.where(axial_lane == LANES - 1, 0.0, axial)
    coef[5] = jnp.where(axial_lane == 0, 0.0, axial)
    coef[6] = jnp.zeros_like(inverse)
    coef[7] = jnp.zeros_like(inverse)
    coef_columns = jnp.transpose(coef[...].reshape(8 * 2 * SPANS, LANES))
    cell_lanes = jnp.bitwise_and(lax.broadcasted_iota(jnp.int32, (LANES, WIDE), 1), 4 * SPANS - 1)
    to_cells = jnp.where(
        (cell_lanes == lax.broadcasted_iota(jnp.int32, (LANES, WIDE), 0)) & (cell_lanes < 2 * SPANS), 1.0, 0.0
    )
    inlet_inverse = exact_dot(coef_columns[0:8, :], to_cells)[0:1, :]

    spread_lanes = lax.broadcasted_iota(jnp.int32, (SPANS, WIDE), 1)
    spread_span = jnp.where(
        jnp.bitwise_and(spread_lanes, SPANS - 1) == lax.broadcasted_iota(jnp.int32, (SPANS, WIDE), 0), 1.0, 0.0
    )
    for a in range(2):
        cells = pl.ds(a * SPANS, SPANS)
        share_wide = exact_dot(jnp.transpose(share[cells, :]), spread_span)
        first = jnp.bitwise_and(owner[cells, :], PT - 1).astype(F32)
        first_wide = exact_dot(jnp.transpose(first), spread_span)
        own_panel = lane_panel.astype(F32)
        lower = jnp.where(first_wide == own_panel, share_wide, 0.0)
        upper = jnp.where(first_wide == own_panel - 1.0, 1.0 - share_wide, 0.0)
        panel_weight[a] = lower + upper

    base[...] = jnp.zeros_like(base)
    for r in range(SPANS):
        for a in range(2):
            cell = a * SPANS + r
            plane = rhs[pl.ds(cell, ROWS, stride=2 * SPANS), :]
            base[r, a, 0:ROWS, :] = plane * coef[0, cell : cell + 1, :]

    beside = (span > 0).astype(jnp.int32) + (span < nr - 1).astype(jnp.int32)
    pl.semaphore_wait(barrier, len(partners) + beside)

    for t in range(NT):
        if shifts[t]:
            panel_copy(t).start()

    def theta_copies(k, r):
        up = pltpu.make_async_remote_copy(
            src_ref=su_buf.at[k, r],
            dst_ref=tu_buf.at[k, r],
            send_sem=theta_send.at[k, r, 0],
            recv_sem=theta_recv.at[k, r, 0],
            device_id=at_sector(ns - 1),
            device_id_type=MESH,
        )
        down = pltpu.make_async_remote_copy(
            src_ref=sd_buf.at[k, r],
            dst_ref=td_buf.at[k, r],
            send_sem=theta_send.at[k, r, 1],
            recv_sem=theta_recv.at[k, r, 1],
            device_id=at_sector(1),
            device_id_type=MESH,
        )
        return up, down

    def to_lower_span(k):
        return pltpu.make_async_remote_copy(
            src_ref=ru_buf.at[k, 0],
            dst_ref=ru_buf.at[k, SPANS],
            send_sem=span_send.at[k, 0],
            recv_sem=span_recv.at[k, 0],
            device_id={"span": span - 1},
            device_id_type=MESH,
        )

    def to_upper_span(k):
        return pltpu.make_async_remote_copy(
            src_ref=rd_buf.at[k, SPANS],
            dst_ref=rd_buf.at[k, 0],
            send_sem=span_send.at[k, 1],
            recv_sem=span_recv.at[k, 1],
            device_id={"span": span + 1},
            device_id_type=MESH,
        )

    def rows_at(i):
        low = lax.rem(i + SPANS // 2 - 1, SPANS // 2)
        return low, SPANS - 1 - low

    def coefficient(n, r, a):
        return coef[n, pl.ds(a * SPANS + r, 1), :]

    def emit(k, rows, planes_of):
        for r, planes in zip(rows, planes_of):
            columns = []
            for plane in planes:
                high, low = split(plane)
                columns.append(jnp.concatenate([high, low, high], axis=0))
            data = jnp.concatenate(columns, axis=1)
            products = [
                jnp.dot(weights[start * PAD : stop * PAD, :], data, preferred_element_type=F32)
                for start, stop in ((0, 4), (4, NMAT))
            ]

            def part(m, a):
                m, product = (m, products[0]) if m < 4 else (m - 4, products[1])
                return product[m * PAD : (m + 1) * PAD, a * LANES : (a + 1) * LANES]

            su_buf[k, r] = part(1, 0)
            sd_buf[k, r] = part(2, 1)
            for a in range(2):
                ru_buf[k, r, a] = part(3, a)
                rd_buf[k, r + 1, a] = part(4, a)
                total = base[r, a] - coefficient(1, r, a) * part(0, a)
                total = total - coefficient(2, r, a) * (part(2, 0) if a else part(1, 1))
                total = total - coefficient(4, r, a) * pltpu.roll(part(5, a), LANES - 1, 1)
                own_buf[k, r, a] = total - coefficient(5, r, a) * pltpu.roll(part(6, a), 1, 1)

        @pl.when((rows[0] == 0) & (span > 0))
        def _():
            to_lower_span(k).start()

        @pl.when((rows[0] == 0) & (span < nr - 1))
        def _():
            to_upper_span(k).start()

        for r in rows:
            for copy in theta_copies(k, r):
                copy.start()

    def update(k, rows):
        for r in rows:
            for copy in theta_copies(k, r):
                copy.wait_recv()

        @pl.when((rows[0] == 0) & (span < nr - 1))
        def _():
            to_lower_span(k).wait_recv()

        @pl.when((rows[0] == 0) & (span > 0))
        def _():
            to_upper_span(k).wait_recv()

        planes_of = []
        for r in rows:
            planes = []
            for a in range(2):
                outside = td_buf if a == 0 else tu_buf
                total = own_buf[k, r, a] - coefficient(2, r, a) * outside[k, r]
                planes.append(total - coefficient(3, r, a) * (ru_buf[k, r + 1, a] + rd_buf[k, r, a]))
            planes_of.append(planes)
        return planes_of

    def first(i, carry):
        rows = rows_at(i)
        emit(0, rows, [[base[r, a] for a in range(2)] for r in rows])
        return carry

    lax.fori_loop(0, SPANS // 2, first, 0)

    cell_row = jnp.bitwise_and(lax.broadcasted_iota(jnp.int32, (4 * SPANS, 2 * WIDE), 0), 2 * SPANS - 1)
    panel_lane = lax.broadcasted_iota(jnp.int32, (4 * SPANS, 2 * WIDE), 1)
    panel_cell = jnp.bitwise_and(panel_lane, SPANS - 1) + jnp.where(panel_lane < WIDE, 0, SPANS)
    to_panels = jnp.where(cell_row == panel_cell, 1.0, 0.0).astype(BF16)
    rows_twice = jnp.concatenate([instance_columns, instance_columns], axis=1).astype(BF16)

    for t in range(NT):
        if shifts[t]:
            panel_copy(t).wait_recv()
            panel_rows[t : t + 1, :] = panel_recv[t, 0:1, :]
    cells_wide = jnp.zeros(wide, F32)
    for a in range(2):
        shares = panel_weight[a] * panel_rows[0:NT, :]
        shares = shares + pltpu.roll(shares, WIDE - SPANS, 1)
        shares = shares + pltpu.roll(shares, WIDE - 2 * SPANS, 1)
        if a:
            shares = pltpu.roll(shares, a * SPANS, 1)
        cells_wide = jnp.where(lane_panel == a, shares, cells_wide)
    cells_wide = cells_wide * inlet_inverse
    delta_send[0:NT, :] = cells_wide

    def delta_copy(n, device):
        return pltpu.make_async_remote_copy(
            src_ref=delta_send,
            dst_ref=delta_recv.at[n],
            send_sem=delta_sems.at[0, n],
            recv_sem=delta_sems.at[1, n],
            device_id=device,
            device_id_type=MESH,
        )

    from_left = delta_copy(0, at_sector(1))
    from_right = delta_copy(1, at_sector(ns - 1))
    from_lower = delta_copy(2, {"span": span + 1})
    from_upper = delta_copy(3, {"span": span - 1})

    @pl.when(span < nr - 1)
    def _():
        from_lower.start()

    @pl.when(span > 0)
    def _():
        from_upper.start()

    from_left.start()
    from_right.start()
    from_left.wait_recv()
    from_right.wait_recv()

    slot = jnp.bitwise_and(lax.broadcasted_iota(jnp.int32, wide, 1), 4 * SPANS - 1)

    def place(values, n, shift, low, high):
        moved = pltpu.roll(delta_recv[n, 0:NT, :], shift % WIDE, 1)
        return jnp.where((slot >= low) & (slot < high), moved, values)

    around = place(cells_wide, 0, SPANS, 2 * SPANS, 3 * SPANS)
    around = place(around, 1, 3 * SPANS, 3 * SPANS, 4 * SPANS)
    gather_slot = jnp.bitwise_and(lax.broadcasted_iota(jnp.int32, (WIDE, LANES), 0), 4 * SPANS - 1)
    gather_lane = lax.broadcasted_iota(jnp.int32, (WIDE, LANES), 1)
    gather = jnp.where(gather_slot == gather_lane, 1.0, 0.0)

    def to_columns(values):
        return exact_dot(jnp.where(same_field, exact_dot(instance_rows, values), 0.0), gather)

    def stacked(columns):
        high, low = split(columns)
        return jnp.concatenate([high, low, high], axis=0)

    def inlet_coefficient(n, axial_cell):
        return pltpu.roll(coef_columns[axial_cell : axial_cell + 1, :], (LANES - 2 * SPANS * n) % LANES, 1)

    columns = to_columns(around)
    product = jnp.dot(weights[...], stacked(columns), preferred_element_type=F32)

    def moved_part(m, shift):
        return pltpu.roll(product[m * PAD : (m + 1) * PAD, :], shift % LANES, 1)

    first_half = lane < SPANS
    along = jnp.where(first_half, moved_part(1, -SPANS), moved_part(1, -2 * SPANS))
    along = along + jnp.where(first_half, moved_part(2, -2 * SPANS), moved_part(2, SPANS))
    across = jnp.where(jnp.bitwise_and(lane, SPANS - 1) == SPANS - 1, 0.0, moved_part(3, -1))
    below = jnp.where(jnp.bitwise_and(lane, SPANS - 1) == 0, 0.0, moved_part(4, 1))
    coupled = inlet_coefficient(1, 0) * product[0:PAD, :]
    coupled = coupled + inlet_coefficient(2, 0) * along
    coupled = coupled + inlet_coefficient(3, 0) * (across + below)
    delta_columns[...] = columns
    delta_shift[0] = columns - coupled
    delta_shift[1] = inlet_coefficient(5, 1) * product[6 * PAD : 7 * PAD, :]

    def beyond_span():
        @pl.when(span > 0)
        def _():
            from_lower.wait_recv()

        @pl.when(span < nr - 1)
        def _():
            from_upper.wait_recv()

        cells = jnp.zeros(wide, F32)
        for a in range(2):
            top, bottom = (a + 1) * SPANS - 1, a * SPANS
            cells = place(cells, 2, bottom - top, bottom, bottom + 1)
            cells = place(cells, 3, top - bottom, top, top + 1)
        product = jnp.dot(weights[3 * PAD : 5 * PAD, :], stacked(to_columns(cells)), preferred_element_type=F32)
        above = jnp.where(jnp.bitwise_and(lane, SPANS - 1) == SPANS - 1, product[0:PAD], 0.0)
        below = jnp.where(jnp.bitwise_and(lane, SPANS - 1) == 0, product[PAD : 2 * PAD], 0.0)
        delta_shift[0] = delta_shift[0] - inlet_coefficient(3, 0) * (above + below)

    def second(i, carry):
        rows = rows_at(i)
        planes_of = []
        for r, planes in zip(rows, update(0, rows)):
            corrected = []
            for a, plane in enumerate(planes):
                shift = lax.rem(LANES - a * SPANS - r, LANES)
                moved = pltpu.roll(delta_columns[...], shift, 1)
                base[r, a] = base[r, a] + jnp.where(lane == 0, moved, 0.0)
                plane = plane + jnp.where(lane == 0, pltpu.roll(delta_shift[0], shift, 1), 0.0)
                shift = lax.rem(shift + 1, LANES)
                corrected.append(plane - jnp.where(lane == 1, pltpu.roll(delta_shift[1], shift, 1), 0.0))
            planes_of.append(corrected)
        emit(1, rows, planes_of)
        return carry

    second(0, 0)
    beyond_span()
    lax.fori_loop(1, SPANS // 2, second, 0)

    def middle(i, carry):
        k, rows = i // (SPANS // 2) + 1, rows_at(lax.rem(i, SPANS // 2))
        emit(k + 1, rows, update(k, rows))
        return carry

    lax.fori_loop(0, (SWEEPS - 2) * (SPANS // 2), middle, 0)

    inlet[...] = jnp.zeros_like(inlet)

    def last(i, carry):
        rows = SPANS // 2 - 1 - i, SPANS // 2 + i
        for r, planes in zip(rows, update(SWEEPS - 1, rows)):
            for a in range(2):
                out[a * SPANS + r] = planes[a]
                inlet[...] = jnp.where(
                    lane == a * SPANS + r, pltpu.roll(planes[a], a * SPANS + r, 1), inlet[...]
                )
        return carry

    lax.fori_loop(0, SPANS // 2, last, 0)

    high, low = split(inlet[...])
    cells = jnp.concatenate([high[:, 0 : 2 * SPANS], low[:, 0 : 2 * SPANS]], axis=1)
    spread = jnp.dot(cells, to_panels, preferred_element_type=F32)
    spread = jnp.where(jnp.concatenate([same_field, same_field], axis=1), spread, 0.0)
    high, low = split(spread)
    gathered = jnp.dot(rows_twice, jnp.concatenate([high, low], axis=0), preferred_element_type=F32)
    back = panel_weight[0] * gathered[:, 0:WIDE] + panel_weight[1] * gathered[:, WIDE:]
    panel_rows[0:NT, :] = back
    for t in range(NT):
        if shifts[t]:
            back_send[t, 0:1, :] = panel_rows[t : t + 1, :]
            back_copy(t).start()
    for t in range(NT):
        if shifts[t]:
            back_copy(t).wait_recv()
            panel_rows[t : t + 1, :] = back_recv[t, 0:1, :]
    sens[...] = jnp.transpose(panel_rows[0:NT, 0 : NF * PT * SPANS])

    for t in range(NT):
        if shifts[t]:
            panel_copy(t).wait_send()
            back_copy(t).wait_send()

    from_left.wait_send()
    from_right.wait_send()

    @pl.when(span < nr - 1)
    def _():
        from_lower.wait_send()

    @pl.when(span > 0)
    def _():
        from_upper.wait_send()

    def drain(i, carry):
        k, r = i // SPANS, lax.rem(i, SPANS)
        for copy in theta_copies(k, r):
            copy.wait_send()
        return carry

    lax.fori_loop(0, SWEEPS * SPANS, drain, 0)
    for k in range(SWEEPS):

        @pl.when(span > 0)
        def _():
            to_lower_span(k).wait_send()

        @pl.when(span < nr - 1)
        def _():
            to_upper_span(k).wait_send()


def store(planes, table, out, sens, sems):
    copies = [pltpu.make_async_copy(table, sens, sems.at[2 * SPANS])]
    for cell in range(2 * SPANS):
        copies.append(pltpu.make_async_copy(planes.at[cell, 0:ROWS], out.at[:, cell], sems.at[cell]))
    for copy in copies:
        copy.start()
    for copy in copies:
        copy.wait()


def on_device(ns, nr, rhs, diag_coef, face_coef, time_coef, jac_up, jac_down, wall_mask, stator_adj, owner, share):
    nt, nf, ct, spans, nax = rhs.shape
    plane = (SWEEPS, SPANS, 2, PAD, LANES)
    ring = (SWEEPS, SPANS + 1, 2, PAD, LANES)
    edge = (SWEEPS, SPANS, PAD, LANES)
    inputs = (
        rhs.reshape(nt * nf * ct * spans, nax),
        diag_coef.reshape(ct * spans, nax),
        face_coef.reshape(3, ct * spans, nax),
        time_coef.reshape(ct * spans, nax),
        jac_up,
        jac_down,
        wall_mask.reshape(ct * spans, nax),
        stator_adj.transpose(1, 2, 3, 0).reshape(nf * PT * spans, nt),
        owner.transpose(1, 2, 0).reshape(ct * spans, nt),
        share.transpose(1, 2, 0).reshape(ct * spans, nt),
        jnp.asarray(time_operator()),
    )
    planes, table = pl.pallas_call(
        functools.partial(kernel, ns, nr),
        out_shape=(
            pltpu.VMEM((ct * spans, PAD, nax), F32),
            pltpu.VMEM((nf * PT * spans, nt), F32),
        ),
        in_specs=[pl.BlockSpec(memory_space=pltpu.HBM)] * len(inputs),
        out_specs=(pl.BlockSpec(memory_space=pltpu.VMEM),) * 2,
        scratch_shapes=[pltpu.VMEM(x.shape, x.dtype) for x in inputs]
        + [
            pltpu.VMEM((NMAT * PAD, 3 * PAD), BF16),
            pltpu.VMEM((8, 2 * SPANS, LANES), F32),
            pltpu.VMEM(plane[1:], F32),
            pltpu.VMEM(plane, F32),
            pltpu.VMEM(edge, F32),
            pltpu.VMEM(edge, F32),
            pltpu.VMEM(ring, F32),
            pltpu.VMEM(ring, F32),
            pltpu.VMEM(edge, F32),
            pltpu.VMEM(edge, F32),
            pltpu.VMEM((NT, 1, WIDE), F32),
            pltpu.VMEM((NT, 1, WIDE), F32),
            pltpu.VMEM((16, WIDE), F32),
            pltpu.VMEM((2, NT, WIDE), F32),
            pltpu.VMEM((PAD, LANES), F32),
            pltpu.VMEM((NT, 1, WIDE), F32),
            pltpu.VMEM((NT, 1, WIDE), F32),
            pltpu.VMEM((48, 8), F32),
            pltpu.VMEM((16, WIDE), F32),
            pltpu.VMEM((4, 16, WIDE), F32),
            pltpu.VMEM((PAD, LANES), F32),
            pltpu.VMEM((2, PAD, LANES), F32),
            pltpu.SemaphoreType.DMA((len(inputs),)),
            pltpu.SemaphoreType.DMA((SWEEPS, SPANS, 2)),
            pltpu.SemaphoreType.DMA((SWEEPS, SPANS, 2)),
            pltpu.SemaphoreType.DMA((SWEEPS, 2)),
            pltpu.SemaphoreType.DMA((SWEEPS, 2)),
            pltpu.SemaphoreType.DMA((2, NT)),
            pltpu.SemaphoreType.DMA((2, NT)),
            pltpu.SemaphoreType.DMA((2, 4)),
        ],
        compiler_params=pltpu.CompilerParams(
            collective_id=0, has_side_effects=True, vmem_limit_bytes=60 * 2**20
        ),
    )(*inputs)
    out, sens = pl.pallas_call(
        store,
        out_shape=(
            jax.ShapeDtypeStruct((nt * nf, ct * spans, nax), F32),
            jax.ShapeDtypeStruct((nf * PT * spans, nt), F32),
        ),
        in_specs=[pl.BlockSpec(memory_space=pltpu.VMEM)] * 2,
        out_specs=(pl.BlockSpec(memory_space=pltpu.HBM),) * 2,
        scratch_shapes=[pltpu.SemaphoreType.DMA((2 * SPANS + 1,))],
    )(pltpu.with_memory_space_constraint(planes, pltpu.VMEM), pltpu.with_memory_space_constraint(table, pltpu.VMEM))
    sens = sens.reshape(nf, PT, spans, nt).transpose(3, 0, 1, 2)
    return out.reshape(rhs.shape), sens


def solution(mesh):
    in_specs = (
        P(None, None, "sector", "span", None),
        P("sector", "span", None),
        P(None, "sector", "span", None),
        P("sector", "span", None),
        P(),
        P(),
        P("sector", "span", None),
        P(None, None, "sector", "span"),
        P(None, "sector", "span"),
        P(None, "sector", "span"),
    )
    out_specs = (P(None, None, "sector", "span", None), P(None, None, "sector", "span"))
    return jax.shard_map(
        functools.partial(on_device, mesh.shape["sector"], mesh.shape["span"]),
        mesh=mesh,
        in_specs=in_specs,
        out_specs=out_specs,
        check_vma=False,
    )
```

```python
import functools

import jax
import jax.numpy as jnp
import ml_dtypes
import numpy as np
from jax import lax
from jax.experimental import pallas as pl
from jax.experimental.pallas import tpu as pltpu
from jax.sharding import PartitionSpec as P

SWEEPS = 4
AHEAD = 2
NT = 11
NF = 7
ROWS = NT * NF
PAD = 80
NMAT = 7
SPANS = 8
PT = 4
LANES = 128
WIDE = 256
F32 = jnp.float32
BF16 = jnp.bfloat16
HIGHEST = lax.Precision.HIGHEST
MESH = pl.DeviceIdType.MESH


def time_operator():
    step = np.arange(NT)[:, None] - np.arange(NT)[None, :]
    sines = np.where(step == 0, 1.0, np.sin(np.pi * step / NT))
    spectral = np.where(step == 0, 0.0, 0.5 * (1.0 - 2.0 * (step % 2)) / sines)
    table = np.zeros((PAD, PAD), np.float32)
    table[:ROWS, :ROWS] = np.kron(spectral.T, np.eye(NF))
    high = table.astype(ml_dtypes.bfloat16)
    low = (table - high.astype(np.float32)).astype(ml_dtypes.bfloat16)
    return np.concatenate([high, high, low], axis=1)


def shift_of(instance, count):
    return ((instance * count) // (NT - 1) - instance // (NT - 1)) % count


def split(value):
    high = value.astype(BF16)
    low = (value - high.astype(F32)).astype(BF16)
    return high, low


def index_of(shape, dim):
    return lax.broadcasted_iota(jnp.int32, shape, dim).astype(F32)


def over_fields(rows):
    instance = jnp.floor((rows + 0.5) * (1.0 / NF))
    return instance, rows - NF * instance


def exact_dot(left, right):
    return jnp.dot(left, right, precision=HIGHEST, preferred_element_type=F32)


def kernel(ns, nr, *refs):
    hbm, refs = refs[:11], refs[11:]
    (out, sens), refs = refs[:2], refs[2:]
    vmem, refs = refs[:11], refs[11:]
    rhs, diag, face, time, jac_up, jac_down, wall, stator, owner, share, time_op = vmem
    (
        weights,
        coef,
        base,
        own_buf,
        tu_buf,
        td_buf,
        ru_buf,
        rd_buf,
        su_buf,
        sd_buf,
        panel_send,
        panel_recv,
        panel_rows,
        panel_weight,
        inlet,
        back_send,
        back_recv,
        jac_rows,
        delta_send,
        delta_recv,
        delta_columns,
        delta_shift,
        input_sems,
        theta_send,
        theta_recv,
        span_send,
        span_recv,
        panel_sems,
        back_sems,
        delta_sems,
        ahead_send,
        ahead_recv,
        ahead_sems,
        edge_coef,
        edge_coef_sems,
    ) = refs
    sector = lax.axis_index("sector")
    span = lax.axis_index("span")
    shifts = [shift_of(t, ns) for t in range(NT)]
    partners = sorted({d % ns for s in shifts for d in (s, -s)} | {1 % ns, (ns - 1) % ns})
    partners = [d for d in partners if d != 0]

    def at_sector(step):
        return {"sector": lax.rem(sector + step, ns)}

    def load(n):
        return pltpu.make_async_copy(hbm[n], vmem[n], input_sems.at[n])

    for n in (7, 0, 1, 6, 8, 9, 4, 5, 10, 2, 3):
        load(n).start()

    ru_buf[:, SPANS] = jnp.zeros((SWEEPS,) + ru_buf.shape[2:], F32)
    rd_buf[:, 0] = jnp.zeros((SWEEPS,) + rd_buf.shape[2:], F32)

    delta_recv[...] = jnp.zeros_like(delta_recv)

    barrier = pltpu.get_barrier_semaphore()
    for step in partners:
        pl.semaphore_signal(barrier, inc=1, device_id=at_sector(step), device_id_type=MESH)

    @pl.when(span > 0)
    def _():
        pl.semaphore_signal(barrier, inc=1, device_id={"span": span - 1}, device_id_type=MESH)

    @pl.when(span < nr - 1)
    def _():
        pl.semaphore_signal(barrier, inc=1, device_id={"span": span + 1}, device_id_type=MESH)

    wide = (NT, WIDE)
    load(7).wait()
    panel_rows[...] = jnp.zeros_like(panel_rows)
    panel_rows[0:NT, 0 : NF * PT * SPANS] = jnp.transpose(stator[...])
    for t in range(NT):
        panel_send[t, 0:1, :] = panel_rows[t : t + 1, :]

    def panel_copy(t):
        return pltpu.make_async_remote_copy(
            src_ref=panel_send.at[t],
            dst_ref=panel_recv.at[t],
            send_sem=panel_sems.at[0, t],
            recv_sem=panel_sems.at[1, t],
            device_id=at_sector(ns - shifts[t]),
            device_id_type=MESH,
        )

    def back_copy(t):
        return pltpu.make_async_remote_copy(
            src_ref=back_send.at[t],
            dst_ref=back_recv.at[t],
            send_sem=back_sems.at[0, t],
            recv_sem=back_sems.at[1, t],
            device_id=at_sector(shifts[t]),
            device_id_type=MESH,
        )

    lane = lax.broadcasted_iota(jnp.int32, (PAD, LANES), 1)
    row = index_of((PAD, 3 * PAD), 0)
    column = index_of((PAD, 3 * PAD), 1)
    column = column - PAD * jnp.floor((column + 0.5) * (1.0 / PAD))
    row_instance, _ = over_fields(row)
    column_instance, _ = over_fields(column)
    same_instance = (row_instance == column_instance) & (row < ROWS) & (column < ROWS)
    instance_rows = jnp.where(
        (over_fields(index_of((PAD, NT), 0))[0] == index_of((PAD, NT), 1)) & (index_of((PAD, NT), 0) < ROWS), 1.0, 0.0
    )
    instance_columns = jnp.where(
        (over_fields(index_of((NT, PAD), 1))[0] == index_of((NT, PAD), 0)) & (index_of((NT, PAD), 1) < ROWS), 1.0, 0.0
    )
    wide_lane = lax.broadcasted_iota(jnp.int32, (PAD, WIDE), 1)
    wide_field = lax.shift_right_logical(wide_lane, 5).astype(F32)
    same_field = over_fields(index_of((PAD, WIDE), 0))[1] == wide_field
    lane_panel = jnp.bitwise_and(lax.shift_right_logical(lax.broadcasted_iota(jnp.int32, wide, 1), 3), PT - 1)

    load(4).wait()
    load(5).wait()
    load(10).wait()
    jac_rows[...] = jnp.zeros_like(jac_rows)
    for direction in range(3):
        for side, table in enumerate((jac_up, jac_down)):
            start = (2 * direction + side) * 8
            jac_rows[start : start + NF, 0:NF] = table[direction]
    high, low = split(jac_rows[...])
    wide_columns = index_of((8, 3 * PAD), 1)
    piece = jnp.floor((wide_columns + 0.5) * (1.0 / PAD))
    chosen = over_fields(wide_columns - PAD * piece)[1] == index_of((8, 3 * PAD), 0)
    pick_high = jnp.where(chosen & (piece < 2.0), 1.0, 0.0).astype(BF16)
    pick_low = jnp.where(chosen & (piece > 1.0), 1.0, 0.0).astype(BF16)
    columns = jnp.dot(high, pick_high, preferred_element_type=F32)
    columns = (columns + jnp.dot(low, pick_low, preferred_element_type=F32)).astype(BF16)
    _, field_of_row = over_fields(index_of((PAD, 8), 0))
    pick_row = jnp.where(field_of_row == index_of((PAD, 8), 1), 1.0, 0.0).astype(BF16)
    weights[0:PAD, :] = time_op[...]
    for m in range(1, NMAT):
        block = jnp.dot(pick_row, columns[8 * (m - 1) : 8 * m, :], preferred_element_type=F32)
        weights[m * PAD : (m + 1) * PAD, :] = jnp.where(same_instance, block, 0.0).astype(BF16)

    for n in (0, 1, 2, 3, 6, 8, 9):
        load(n).wait()
    inverse = wall[...].astype(F32) / diag[...]
    axial_lane = lax.broadcasted_iota(jnp.int32, inverse.shape, 1)
    axial = inverse * face[2]
    coef[0] = inverse
    coef[1] = inverse * time[...]
    coef[2] = inverse * face[0]
    coef[3] = inverse * face[1]
    coef[4] = jnp.where(axial_lane == LANES - 1, 0.0, axial)
    coef[5] = jnp.where(axial_lane == 0, 0.0, axial)
    coef[6] = jnp.zeros_like(inverse)
    coef[7] = jnp.zeros_like(inverse)
    coef_columns = jnp.transpose(coef[...].reshape(8 * 2 * SPANS, LANES))
    cell_lanes = jnp.bitwise_and(lax.broadcasted_iota(jnp.int32, (LANES, WIDE), 1), 4 * SPANS - 1)
    to_cells = jnp.where(
        (cell_lanes == lax.broadcasted_iota(jnp.int32, (LANES, WIDE), 0)) & (cell_lanes < 2 * SPANS), 1.0, 0.0
    )
    inlet_inverse = exact_dot(coef_columns[0:8, :], to_cells)[0:1, :]

    spread_lanes = lax.broadcasted_iota(jnp.int32, (SPANS, WIDE), 1)
    spread_span = jnp.where(
        jnp.bitwise_and(spread_lanes, SPANS - 1) == lax.broadcasted_iota(jnp.int32, (SPANS, WIDE), 0), 1.0, 0.0
    )
    for a in range(2):
        cells = pl.ds(a * SPANS, SPANS)
        share_wide = exact_dot(jnp.transpose(share[cells, :]), spread_span)
        first = jnp.bitwise_and(owner[cells, :], PT - 1).astype(F32)
        first_wide = exact_dot(jnp.transpose(first), spread_span)
        own_panel = lane_panel.astype(F32)
        lower = jnp.where(first_wide == own_panel, share_wide, 0.0)
        upper = jnp.where(first_wide == own_panel - 1.0, 1.0 - share_wide, 0.0)
        panel_weight[a] = lower + upper

    base[...] = jnp.zeros_like(base)
    for r in range(SPANS):
        for a in range(2):
            cell = a * SPANS + r
            plane = rhs[pl.ds(cell, ROWS, stride=2 * SPANS), :]
            base[r, a, 0:ROWS, :] = plane * coef[0, cell : cell + 1, :]

    beside = (span > 0).astype(jnp.int32) + (span < nr - 1).astype(jnp.int32)
    pl.semaphore_wait(barrier, len(partners) + beside)

    for t in range(NT):
        if shifts[t]:
            panel_copy(t).start()

    def theta_copies(k, r):
        up = pltpu.make_async_remote_copy(
            src_ref=su_buf.at[k, r],
            dst_ref=tu_buf.at[k, r],
            send_sem=theta_send.at[k, r, 0],
            recv_sem=theta_recv.at[k, r, 0],
            device_id=at_sector(ns - 1),
            device_id_type=MESH,
        )
        down = pltpu.make_async_remote_copy(
            src_ref=sd_buf.at[k, r],
            dst_ref=td_buf.at[k, r],
            send_sem=theta_send.at[k, r, 1],
            recv_sem=theta_recv.at[k, r, 1],
            device_id=at_sector(1),
            device_id_type=MESH,
        )
        return up, down

    def to_lower_span(k):
        return pltpu.make_async_remote_copy(
            src_ref=ru_buf.at[k, 0],
            dst_ref=ru_buf.at[k, SPANS],
            send_sem=span_send.at[k, 0],
            recv_sem=span_recv.at[k, 0],
            device_id={"span": span - 1},
            device_id_type=MESH,
        )

    def to_upper_span(k):
        return pltpu.make_async_remote_copy(
            src_ref=rd_buf.at[k, SPANS],
            dst_ref=rd_buf.at[k, 0],
            send_sem=span_send.at[k, 1],
            recv_sem=span_recv.at[k, 1],
            device_id={"span": span + 1},
            device_id_type=MESH,
        )

    def beside_copy(source, target, sems, upward):
        slot = 0 if upward else 1
        return pltpu.make_async_remote_copy(
            src_ref=source,
            dst_ref=target.at[slot],
            send_sem=sems.at[0, slot],
            recv_sem=sems.at[1, slot],
            device_id={"span": span + 1 if upward else span - 1},
            device_id_type=MESH,
        )

    def coef_copy(upward):
        return beside_copy(coef.at[3], edge_coef, edge_coef_sems, upward)

    def ahead_copy(upward):
        return beside_copy(ahead_send.at[int(upward)], ahead_recv, ahead_sems, upward)

    @pl.when(span > 0)
    def _():
        coef_copy(False).start()

    @pl.when(span < nr - 1)
    def _():
        coef_copy(True).start()

    def send_ahead(k):
        for upward, r in ((False, 0), (True, SPANS - 1)):
            for a in range(2):
                outside = td_buf if a == 0 else tu_buf
                inside = rd_buf[k, r, a] if upward else ru_buf[k, r + 1, a]
                total = own_buf[k, r, a] - coefficient(2, r, a) * outside[k, r]
                ahead_send[int(upward), a] = total - coefficient(3, r, a) * inside

        @pl.when(span > 0)
        def _():
            ahead_copy(False).start()

        @pl.when(span < nr - 1)
        def _():
            ahead_copy(True).start()

    def receive_ahead(k):
        def complete(slot, r, terms, m):
            columns = []
            for a in range(2):
                cell = a * SPANS + r
                plane = ahead_recv[slot, a] - edge_coef[slot, cell : cell + 1, :] * terms[a]
                high, low = split(plane)
                columns.append(jnp.concatenate([high, low, high], axis=0))
            data = jnp.concatenate(columns, axis=1)
            return jnp.dot(weights[m * PAD : (m + 1) * PAD, :], data, preferred_element_type=F32)

        @pl.when(span < nr - 1)
        def _():
            coef_copy(False).wait_recv()
            ahead_copy(False).wait_recv()
            product = complete(1, 0, [rd_buf[k - 1, SPANS, a] for a in range(2)], 3)
            for a in range(2):
                ru_buf[k, SPANS, a] = product[:, a * LANES : (a + 1) * LANES]

        @pl.when(span > 0)
        def _():
            coef_copy(True).wait_recv()
            ahead_copy(True).wait_recv()
            product = complete(0, SPANS - 1, [ru_buf[k - 1, 0, a] for a in range(2)], 4)
            for a in range(2):
                rd_buf[k, 0, a] = product[:, a * LANES : (a + 1) * LANES]

    def rows_at(i):
        low = lax.rem(i + SPANS // 2 - 1, SPANS // 2)
        return low, SPANS - 1 - low

    def coefficient(n, r, a):
        return coef[n, pl.ds(a * SPANS + r, 1), :]

    def emit(k, rows, planes_of):
        for r, planes in zip(rows, planes_of):
            columns = []
            for plane in planes:
                high, low = split(plane)
                columns.append(jnp.concatenate([high, low, high], axis=0))
            data = jnp.concatenate(columns, axis=1)
            products = [
                jnp.dot(weights[start * PAD : stop * PAD, :], data, preferred_element_type=F32)
                for start, stop in ((0, 4), (4, NMAT))
            ]

            def part(m, a):
                m, product = (m, products[0]) if m < 4 else (m - 4, products[1])
                return product[m * PAD : (m + 1) * PAD, a * LANES : (a + 1) * LANES]

            su_buf[k, r] = part(1, 0)
            sd_buf[k, r] = part(2, 1)
            for a in range(2):
                ru_buf[k, r, a] = part(3, a)
                rd_buf[k, r + 1, a] = part(4, a)
                total = base[r, a] - coefficient(1, r, a) * part(0, a)
                total = total - coefficient(2, r, a) * (part(2, 0) if a else part(1, 1))
                total = total - coefficient(4, r, a) * pltpu.roll(part(5, a), LANES - 1, 1)
                own_buf[k, r, a] = total - coefficient(5, r, a) * pltpu.roll(part(6, a), 1, 1)

        if k != AHEAD:

            @pl.when((rows[0] == 0) & (span > 0))
            def _():
                to_lower_span(k).start()

            @pl.when((rows[0] == 0) & (span < nr - 1))
            def _():
                to_upper_span(k).start()

        for r in rows:
            for copy in theta_copies(k, r):
                copy.start()

    def update(k, rows):
        for r in rows:
            for copy in theta_copies(k, r):
                copy.wait_recv()

        if k == AHEAD - 1:

            @pl.when(rows[0] == 0)
            def _():
                send_ahead(k)

        if k == AHEAD:

            @pl.when(rows[0] == 0)
            def _():
                receive_ahead(k)

        else:

            @pl.when((rows[0] == 0) & (span < nr - 1))
            def _():
                to_lower_span(k).wait_recv()

            @pl.when((rows[0] == 0) & (span > 0))
            def _():
                to_upper_span(k).wait_recv()

        planes_of = []
        for r in rows:
            planes = []
            for a in range(2):
                outside = td_buf if a == 0 else tu_buf
                total = own_buf[k, r, a] - coefficient(2, r, a) * outside[k, r]
                planes.append(total - coefficient(3, r, a) * (ru_buf[k, r + 1, a] + rd_buf[k, r, a]))
            planes_of.append(planes)
        return planes_of

    def first(i, carry):
        rows = rows_at(i)
        emit(0, rows, [[base[r, a] for a in range(2)] for r in rows])
        return carry

    lax.fori_loop(0, SPANS // 2, first, 0)

    cell_row = jnp.bitwise_and(lax.broadcasted_iota(jnp.int32, (4 * SPANS, 2 * WIDE), 0), 2 * SPANS - 1)
    panel_lane = lax.broadcasted_iota(jnp.int32, (4 * SPANS, 2 * WIDE), 1)
    panel_cell = jnp.bitwise_and(panel_lane, SPANS - 1) + jnp.where(panel_lane < WIDE, 0, SPANS)
    to_panels = jnp.where(cell_row == panel_cell, 1.0, 0.0).astype(BF16)
    rows_twice = jnp.concatenate([instance_columns, instance_columns], axis=1).astype(BF16)

    for t in range(NT):
        if shifts[t]:
            panel_copy(t).wait_recv()
            panel_rows[t : t + 1, :] = panel_recv[t, 0:1, :]
    cells_wide = jnp.zeros(wide, F32)
    for a in range(2):
        shares = panel_weight[a] * panel_rows[0:NT, :]
        shares = shares + pltpu.roll(shares, WIDE - SPANS, 1)
        shares = shares + pltpu.roll(shares, WIDE - 2 * SPANS, 1)
        if a:
            shares = pltpu.roll(shares, a * SPANS, 1)
        cells_wide = jnp.where(lane_panel == a, shares, cells_wide)
    cells_wide = cells_wide * inlet_inverse
    delta_send[0:NT, :] = cells_wide

    def delta_copy(n, device):
        return pltpu.make_async_remote_copy(
            src_ref=delta_send,
            dst_ref=delta_recv.at[n],
            send_sem=delta_sems.at[0, n],
            recv_sem=delta_sems.at[1, n],
            device_id=device,
            device_id_type=MESH,
        )

    from_left = delta_copy(0, at_sector(1))
    from_right = delta_copy(1, at_sector(ns - 1))
    from_lower = delta_copy(2, {"span": span + 1})
    from_upper = delta_copy(3, {"span": span - 1})

    @pl.when(span < nr - 1)
    def _():
        from_lower.start()

    @pl.when(span > 0)
    def _():
        from_upper.start()

    from_left.start()
    from_right.start()
    from_left.wait_recv()
    from_right.wait_recv()

    slot = jnp.bitwise_and(lax.broadcasted_iota(jnp.int32, wide, 1), 4 * SPANS - 1)

    def place(values, n, shift, low, high):
        moved = pltpu.roll(delta_recv[n, 0:NT, :], shift % WIDE, 1)
        return jnp.where((slot >= low) & (slot < high), moved, values)

    around = place(cells_wide, 0, SPANS, 2 * SPANS, 3 * SPANS)
    around = place(around, 1, 3 * SPANS, 3 * SPANS, 4 * SPANS)
    gather_slot = jnp.bitwise_and(lax.broadcasted_iota(jnp.int32, (WIDE, LANES), 0), 4 * SPANS - 1)
    gather_lane = lax.broadcasted_iota(jnp.int32, (WIDE, LANES), 1)
    gather = jnp.where(gather_slot == gather_lane, 1.0, 0.0)

    def to_columns(values):
        return exact_dot(jnp.where(same_field, exact_dot(instance_rows, values), 0.0), gather)

    def stacked(columns):
        high, low = split(columns)
        return jnp.concatenate([high, low, high], axis=0)

    def inlet_coefficient(n, axial_cell):
        return pltpu.roll(coef_columns[axial_cell : axial_cell + 1, :], (LANES - 2 * SPANS * n) % LANES, 1)

    columns = to_columns(around)
    product = jnp.dot(weights[...], stacked(columns), preferred_element_type=F32)

    def moved_part(m, shift):
        return pltpu.roll(product[m * PAD : (m + 1) * PAD, :], shift % LANES, 1)

    first_half = lane < SPANS
    along = jnp.where(first_half, moved_part(1, -SPANS), moved_part(1, -2 * SPANS))
    along = along + jnp.where(first_half, moved_part(2, -2 * SPANS), moved_part(2, SPANS))
    across = jnp.where(jnp.bitwise_and(lane, SPANS - 1) == SPANS - 1, 0.0, moved_part(3, -1))
    below = jnp.where(jnp.bitwise_and(lane, SPANS - 1) == 0, 0.0, moved_part(4, 1))
    coupled = inlet_coefficient(1, 0) * product[0:PAD, :]
    coupled = coupled + inlet_coefficient(2, 0) * along
    coupled = coupled + inlet_coefficient(3, 0) * (across + below)
    delta_columns[...] = columns
    delta_shift[0] = columns - coupled
    delta_shift[1] = inlet_coefficient(5, 1) * product[6 * PAD : 7 * PAD, :]

    def beyond_span():
        @pl.when(span > 0)
        def _():
            from_lower.wait_recv()

        @pl.when(span < nr - 1)
        def _():
            from_upper.wait_recv()

        cells = jnp.zeros(wide, F32)
        for a in range(2):
            top, bottom = (a + 1) * SPANS - 1, a * SPANS
            cells = place(cells, 2, bottom - top, bottom, bottom + 1)
            cells = place(cells, 3, top - bottom, top, top + 1)
        product = jnp.dot(weights[3 * PAD : 5 * PAD, :], stacked(to_columns(cells)), preferred_element_type=F32)
        above = jnp.where(jnp.bitwise_and(lane, SPANS - 1) == SPANS - 1, product[0:PAD], 0.0)
        below = jnp.where(jnp.bitwise_and(lane, SPANS - 1) == 0, product[PAD : 2 * PAD], 0.0)
        delta_shift[0] = delta_shift[0] - inlet_coefficient(3, 0) * (above + below)

    def second(i, carry):
        rows = rows_at(i)
        planes_of = []
        for r, planes in zip(rows, update(0, rows)):
            corrected = []
            for a, plane in enumerate(planes):
                shift = lax.rem(LANES - a * SPANS - r, LANES)
                moved = pltpu.roll(delta_columns[...], shift, 1)
                base[r, a] = base[r, a] + jnp.where(lane == 0, moved, 0.0)
                plane = plane + jnp.where(lane == 0, pltpu.roll(delta_shift[0], shift, 1), 0.0)
                shift = lax.rem(shift + 1, LANES)
                corrected.append(plane - jnp.where(lane == 1, pltpu.roll(delta_shift[1], shift, 1), 0.0))
            planes_of.append(corrected)
        emit(1, rows, planes_of)
        return carry

    second(0, 0)
    beyond_span()
    lax.fori_loop(1, SPANS // 2, second, 0)

    for k in range(1, SWEEPS - 1):

        def middle(i, carry, k=k):
            rows = rows_at(i)
            emit(k + 1, rows, update(k, rows))
            return carry

        lax.fori_loop(0, SPANS // 2, middle, 0)

    inlet[...] = jnp.zeros_like(inlet)

    def last(i, carry):
        rows = SPANS // 2 - 1 - i, SPANS // 2 + i
        for r, planes in zip(rows, update(SWEEPS - 1, rows)):
            for a in range(2):
                out[a * SPANS + r] = planes[a]
                inlet[...] = jnp.where(
                    lane == a * SPANS + r, pltpu.roll(planes[a], a * SPANS + r, 1), inlet[...]
                )
        return carry

    lax.fori_loop(0, SPANS // 2, last, 0)

    high, low = split(inlet[...])
    cells = jnp.concatenate([high[:, 0 : 2 * SPANS], low[:, 0 : 2 * SPANS]], axis=1)
    spread = jnp.dot(cells, to_panels, preferred_element_type=F32)
    spread = jnp.where(jnp.concatenate([same_field, same_field], axis=1), spread, 0.0)
    high, low = split(spread)
    gathered = jnp.dot(rows_twice, jnp.concatenate([high, low], axis=0), preferred_element_type=F32)
    back = panel_weight[0] * gathered[:, 0:WIDE] + panel_weight[1] * gathered[:, WIDE:]
    panel_rows[0:NT, :] = back
    for t in range(NT):
        if shifts[t]:
            back_send[t, 0:1, :] = panel_rows[t : t + 1, :]
            back_copy(t).start()
    for t in range(NT):
        if shifts[t]:
            back_copy(t).wait_recv()
            panel_rows[t : t + 1, :] = back_recv[t, 0:1, :]
    sens[...] = jnp.transpose(panel_rows[0:NT, 0 : NF * PT * SPANS])

    for t in range(NT):
        if shifts[t]:
            panel_copy(t).wait_send()
            back_copy(t).wait_send()

    from_left.wait_send()
    from_right.wait_send()

    @pl.when(span < nr - 1)
    def _():
        from_lower.wait_send()

    @pl.when(span > 0)
    def _():
        from_upper.wait_send()

    def drain(i, carry):
        k, r = i // SPANS, lax.rem(i, SPANS)
        for copy in theta_copies(k, r):
            copy.wait_send()
        return carry

    lax.fori_loop(0, SWEEPS * SPANS, drain, 0)
    @pl.when(span > 0)
    def _():
        coef_copy(False).wait_send()
        ahead_copy(False).wait_send()
        for k in range(SWEEPS):
            if k != AHEAD:
                to_lower_span(k).wait_send()

    @pl.when(span < nr - 1)
    def _():
        coef_copy(True).wait_send()
        ahead_copy(True).wait_send()
        for k in range(SWEEPS):
            if k != AHEAD:
                to_upper_span(k).wait_send()


def store(planes, table, out, sens, sems):
    copies = [pltpu.make_async_copy(table, sens, sems.at[2 * SPANS])]
    for cell in range(2 * SPANS):
        copies.append(pltpu.make_async_copy(planes.at[cell, 0:ROWS], out.at[:, cell], sems.at[cell]))
    for copy in copies:
        copy.start()
    for copy in copies:
        copy.wait()


def on_device(ns, nr, rhs, diag_coef, face_coef, time_coef, jac_up, jac_down, wall_mask, stator_adj, owner, share):
    nt, nf, ct, spans, nax = rhs.shape
    plane = (SWEEPS, SPANS, 2, PAD, LANES)
    ring = (SWEEPS, SPANS + 1, 2, PAD, LANES)
    edge = (SWEEPS, SPANS, PAD, LANES)
    inputs = (
        rhs.reshape(nt * nf * ct * spans, nax),
        diag_coef.reshape(ct * spans, nax),
        face_coef.reshape(3, ct * spans, nax),
        time_coef.reshape(ct * spans, nax),
        jac_up,
        jac_down,
        wall_mask.reshape(ct * spans, nax),
        stator_adj.transpose(1, 2, 3, 0).reshape(nf * PT * spans, nt),
        owner.transpose(1, 2, 0).reshape(ct * spans, nt),
        share.transpose(1, 2, 0).reshape(ct * spans, nt),
        jnp.asarray(time_operator()),
    )
    planes, table = pl.pallas_call(
        functools.partial(kernel, ns, nr),
        out_shape=(
            pltpu.VMEM((ct * spans, PAD, nax), F32),
            pltpu.VMEM((nf * PT * spans, nt), F32),
        ),
        in_specs=[pl.BlockSpec(memory_space=pltpu.HBM)] * len(inputs),
        out_specs=(pl.BlockSpec(memory_space=pltpu.VMEM),) * 2,
        scratch_shapes=[pltpu.VMEM(x.shape, x.dtype) for x in inputs]
        + [
            pltpu.VMEM((NMAT * PAD, 3 * PAD), BF16),
            pltpu.VMEM((8, 2 * SPANS, LANES), F32),
            pltpu.VMEM(plane[1:], F32),
            pltpu.VMEM(plane, F32),
            pltpu.VMEM(edge, F32),
            pltpu.VMEM(edge, F32),
            pltpu.VMEM(ring, F32),
            pltpu.VMEM(ring, F32),
            pltpu.VMEM(edge, F32),
            pltpu.VMEM(edge, F32),
            pltpu.VMEM((NT, 1, WIDE), F32),
            pltpu.VMEM((NT, 1, WIDE), F32),
            pltpu.VMEM((16, WIDE), F32),
            pltpu.VMEM((2, NT, WIDE), F32),
            pltpu.VMEM((PAD, LANES), F32),
            pltpu.VMEM((NT, 1, WIDE), F32),
            pltpu.VMEM((NT, 1, WIDE), F32),
            pltpu.VMEM((48, 8), F32),
            pltpu.VMEM((16, WIDE), F32),
            pltpu.VMEM((4, 16, WIDE), F32),
            pltpu.VMEM((PAD, LANES), F32),
            pltpu.VMEM((2, PAD, LANES), F32),
            pltpu.SemaphoreType.DMA((len(inputs),)),
            pltpu.SemaphoreType.DMA((SWEEPS, SPANS, 2)),
            pltpu.SemaphoreType.DMA((SWEEPS, SPANS, 2)),
            pltpu.SemaphoreType.DMA((SWEEPS, 2)),
            pltpu.SemaphoreType.DMA((SWEEPS, 2)),
            pltpu.SemaphoreType.DMA((2, NT)),
            pltpu.SemaphoreType.DMA((2, NT)),
            pltpu.SemaphoreType.DMA((2, 4)),
            pltpu.VMEM((2, 2, PAD, LANES), F32),
            pltpu.VMEM((2, 2, PAD, LANES), F32),
            pltpu.SemaphoreType.DMA((2, 2)),
            pltpu.VMEM((2, 2 * SPANS, LANES), F32),
            pltpu.SemaphoreType.DMA((2, 2)),
        ],
        compiler_params=pltpu.CompilerParams(
            collective_id=0, has_side_effects=True, vmem_limit_bytes=60 * 2**20
        ),
    )(*inputs)
    out, sens = pl.pallas_call(
        store,
        out_shape=(
            jax.ShapeDtypeStruct((nt * nf, ct * spans, nax), F32),
            jax.ShapeDtypeStruct((nf * PT * spans, nt), F32),
        ),
        in_specs=[pl.BlockSpec(memory_space=pltpu.VMEM)] * 2,
        out_specs=(pl.BlockSpec(memory_space=pltpu.HBM),) * 2,
        scratch_shapes=[pltpu.SemaphoreType.DMA((2 * SPANS + 1,))],
    )(pltpu.with_memory_space_constraint(planes, pltpu.VMEM), pltpu.with_memory_space_constraint(table, pltpu.VMEM))
    sens = sens.reshape(nf, PT, spans, nt).transpose(3, 0, 1, 2)
    return out.reshape(rhs.shape), sens


def solution(mesh):
    in_specs = (
        P(None, None, "sector", "span", None),
        P("sector", "span", None),
        P(None, "sector", "span", None),
        P("sector", "span", None),
        P(),
        P(),
        P("sector", "span", None),
        P(None, None, "sector", "span"),
        P(None, "sector", "span"),
        P(None, "sector", "span"),
    )
    out_specs = (P(None, None, "sector", "span", None), P(None, None, "sector", "span"))
    return jax.shard_map(
        functools.partial(on_device, mesh.shape["sector"], mesh.shape["span"]),
        mesh=mesh,
        in_specs=in_specs,
        out_specs=out_specs,
        check_vma=False,
    )
```

```python
import functools

import jax
import jax.numpy as jnp
import ml_dtypes
import numpy as np
from jax import lax
from jax.experimental import pallas as pl
from jax.experimental.pallas import tpu as pltpu
from jax.sharding import PartitionSpec as P

SWEEPS = 4
AHEAD = 2
NT = 11
NF = 7
ROWS = NT * NF
PAD = 80
NMAT = 7
SPANS = 8
PT = 4
LANES = 128
WIDE = 256
F32 = jnp.float32
BF16 = jnp.bfloat16
HIGHEST = lax.Precision.HIGHEST
MESH = pl.DeviceIdType.MESH


def time_operator():
    step = np.arange(NT)[:, None] - np.arange(NT)[None, :]
    sines = np.where(step == 0, 1.0, np.sin(np.pi * step / NT))
    spectral = np.where(step == 0, 0.0, 0.5 * (1.0 - 2.0 * (step % 2)) / sines)
    table = np.zeros((PAD, PAD), np.float32)
    table[:ROWS, :ROWS] = np.kron(spectral.T, np.eye(NF))
    high = table.astype(ml_dtypes.bfloat16)
    low = (table - high.astype(np.float32)).astype(ml_dtypes.bfloat16)
    return np.concatenate([high, high, low], axis=1)


def shift_of(instance, count):
    return ((instance * count) // (NT - 1) - instance // (NT - 1)) % count


def split(value):
    high = value.astype(BF16)
    low = (value - high.astype(F32)).astype(BF16)
    return high, low


def index_of(shape, dim):
    return lax.broadcasted_iota(jnp.int32, shape, dim).astype(F32)


def over_fields(rows):
    instance = jnp.floor((rows + 0.5) * (1.0 / NF))
    return instance, rows - NF * instance


def exact_dot(left, right):
    return jnp.dot(left, right, precision=HIGHEST, preferred_element_type=F32)


def kernel(ns, nr, *refs):
    hbm, refs = refs[:11], refs[11:]
    (out, sens), refs = refs[:2], refs[2:]
    vmem, refs = refs[:11], refs[11:]
    rhs, diag, face, time, jac_up, jac_down, wall, stator, owner, share, time_op = vmem
    (
        weights,
        coef,
        base,
        own_buf,
        tu_buf,
        td_buf,
        ru_buf,
        rd_buf,
        su_buf,
        sd_buf,
        panel_send,
        panel_recv,
        panel_rows,
        panel_weight,
        inlet,
        back_send,
        back_recv,
        jac_rows,
        delta_send,
        delta_recv,
        delta_columns,
        delta_shift,
        input_sems,
        theta_send,
        theta_recv,
        span_send,
        span_recv,
        panel_sems,
        back_sems,
        delta_sems,
        ahead_send,
        ahead_recv,
        ahead_sems,
        edge_coef,
        edge_coef_sems,
    ) = refs
    sector = lax.axis_index("sector")
    span = lax.axis_index("span")
    shifts = [shift_of(t, ns) for t in range(NT)]
    partners = sorted({d % ns for s in shifts for d in (s, -s)} | {1 % ns, (ns - 1) % ns})
    partners = [d for d in partners if d != 0]

    def at_sector(step):
        return {"sector": lax.rem(sector + step, ns)}

    def load(n):
        return pltpu.make_async_copy(hbm[n], vmem[n], input_sems.at[n])

    for n in (7, 0, 1, 6, 8, 9, 4, 5, 10, 2, 3):
        load(n).start()

    ru_buf[:, SPANS] = jnp.zeros((SWEEPS,) + ru_buf.shape[2:], F32)
    rd_buf[:, 0] = jnp.zeros((SWEEPS,) + rd_buf.shape[2:], F32)

    delta_recv[...] = jnp.zeros_like(delta_recv)

    barrier = pltpu.get_barrier_semaphore()
    for step in partners:
        pl.semaphore_signal(barrier, inc=1, device_id=at_sector(step), device_id_type=MESH)

    @pl.when(span > 0)
    def _():
        pl.semaphore_signal(barrier, inc=1, device_id={"span": span - 1}, device_id_type=MESH)

    @pl.when(span < nr - 1)
    def _():
        pl.semaphore_signal(barrier, inc=1, device_id={"span": span + 1}, device_id_type=MESH)

    wide = (NT, WIDE)
    load(7).wait()
    panel_rows[...] = jnp.zeros_like(panel_rows)
    panel_rows[0:NT, 0 : NF * PT * SPANS] = jnp.transpose(stator[...])
    for t in range(NT):
        panel_send[t, 0:1, :] = panel_rows[t : t + 1, :]

    def panel_copy(t):
        return pltpu.make_async_remote_copy(
            src_ref=panel_send.at[t],
            dst_ref=panel_recv.at[t],
            send_sem=panel_sems.at[0, t],
            recv_sem=panel_sems.at[1, t],
            device_id=at_sector(ns - shifts[t]),
            device_id_type=MESH,
        )

    def back_copy(t):
        return pltpu.make_async_remote_copy(
            src_ref=back_send.at[t],
            dst_ref=back_recv.at[t],
            send_sem=back_sems.at[0, t],
            recv_sem=back_sems.at[1, t],
            device_id=at_sector(shifts[t]),
            device_id_type=MESH,
        )

    lane = lax.broadcasted_iota(jnp.int32, (PAD, LANES), 1)
    row = index_of((PAD, 3 * PAD), 0)
    column = index_of((PAD, 3 * PAD), 1)
    column = column - PAD * jnp.floor((column + 0.5) * (1.0 / PAD))
    row_instance, _ = over_fields(row)
    column_instance, _ = over_fields(column)
    same_instance = (row_instance == column_instance) & (row < ROWS) & (column < ROWS)
    instance_rows = jnp.where(
        (over_fields(index_of((PAD, NT), 0))[0] == index_of((PAD, NT), 1)) & (index_of((PAD, NT), 0) < ROWS), 1.0, 0.0
    )
    instance_columns = jnp.where(
        (over_fields(index_of((NT, PAD), 1))[0] == index_of((NT, PAD), 0)) & (index_of((NT, PAD), 1) < ROWS), 1.0, 0.0
    )
    wide_lane = lax.broadcasted_iota(jnp.int32, (PAD, WIDE), 1)
    wide_field = lax.shift_right_logical(wide_lane, 5).astype(F32)
    same_field = over_fields(index_of((PAD, WIDE), 0))[1] == wide_field
    lane_panel = jnp.bitwise_and(lax.shift_right_logical(lax.broadcasted_iota(jnp.int32, wide, 1), 3), PT - 1)

    load(4).wait()
    load(5).wait()
    load(10).wait()
    jac_rows[...] = jnp.zeros_like(jac_rows)
    for direction in range(3):
        for side, table in enumerate((jac_up, jac_down)):
            start = (2 * direction + side) * 8
            jac_rows[start : start + NF, 0:NF] = table[direction]
    high, low = split(jac_rows[...])
    wide_columns = index_of((8, 3 * PAD), 1)
    piece = jnp.floor((wide_columns + 0.5) * (1.0 / PAD))
    chosen = over_fields(wide_columns - PAD * piece)[1] == index_of((8, 3 * PAD), 0)
    pick_high = jnp.where(chosen & (piece < 2.0), 1.0, 0.0).astype(BF16)
    pick_low = jnp.where(chosen & (piece > 1.0), 1.0, 0.0).astype(BF16)
    columns = jnp.dot(high, pick_high, preferred_element_type=F32)
    columns = (columns + jnp.dot(low, pick_low, preferred_element_type=F32)).astype(BF16)
    _, field_of_row = over_fields(index_of((PAD, 8), 0))
    pick_row = jnp.where(field_of_row == index_of((PAD, 8), 1), 1.0, 0.0).astype(BF16)
    weights[0:PAD, :] = time_op[...]
    for m in range(1, NMAT):
        block = jnp.dot(pick_row, columns[8 * (m - 1) : 8 * m, :], preferred_element_type=F32)
        weights[m * PAD : (m + 1) * PAD, :] = jnp.where(same_instance, block, 0.0).astype(BF16)

    for n in (0, 1, 2, 3, 6, 8, 9):
        load(n).wait()
    inverse = wall[...].astype(F32) / diag[...]
    axial_lane = lax.broadcasted_iota(jnp.int32, inverse.shape, 1)
    axial = inverse * face[2]
    coef[0] = inverse
    coef[1] = inverse * time[...]
    coef[2] = inverse * face[0]
    coef[3] = inverse * face[1]
    coef[4] = jnp.where(axial_lane == LANES - 1, 0.0, axial)
    coef[5] = jnp.where(axial_lane == 0, 0.0, axial)
    coef[6] = jnp.zeros_like(inverse)
    coef[7] = jnp.zeros_like(inverse)
    coef_columns = jnp.transpose(coef[...].reshape(8 * 2 * SPANS, LANES))
    cell_lanes = jnp.bitwise_and(lax.broadcasted_iota(jnp.int32, (LANES, WIDE), 1), 4 * SPANS - 1)
    to_cells = jnp.where(
        (cell_lanes == lax.broadcasted_iota(jnp.int32, (LANES, WIDE), 0)) & (cell_lanes < 2 * SPANS), 1.0, 0.0
    )
    inlet_inverse = exact_dot(coef_columns[0:8, :], to_cells)[0:1, :]

    spread_lanes = lax.broadcasted_iota(jnp.int32, (SPANS, WIDE), 1)
    spread_span = jnp.where(
        jnp.bitwise_and(spread_lanes, SPANS - 1) == lax.broadcasted_iota(jnp.int32, (SPANS, WIDE), 0), 1.0, 0.0
    )
    for a in range(2):
        cells = pl.ds(a * SPANS, SPANS)
        share_wide = exact_dot(jnp.transpose(share[cells, :]), spread_span)
        first = jnp.bitwise_and(owner[cells, :], PT - 1).astype(F32)
        first_wide = exact_dot(jnp.transpose(first), spread_span)
        own_panel = lane_panel.astype(F32)
        lower = jnp.where(first_wide == own_panel, share_wide, 0.0)
        upper = jnp.where(first_wide == own_panel - 1.0, 1.0 - share_wide, 0.0)
        panel_weight[a] = lower + upper

    base[...] = jnp.zeros_like(base)
    for r in range(SPANS):
        for a in range(2):
            cell = a * SPANS + r
            plane = rhs[pl.ds(cell, ROWS, stride=2 * SPANS), :]
            base[r, a, 0:ROWS, :] = plane * coef[0, cell : cell + 1, :]

    beside = (span > 0).astype(jnp.int32) + (span < nr - 1).astype(jnp.int32)
    pl.semaphore_wait(barrier, len(partners) + beside)

    for t in range(NT):
        if shifts[t]:
            panel_copy(t).start()

    def theta_copies(k, r):
        up = pltpu.make_async_remote_copy(
            src_ref=su_buf.at[k, r],
            dst_ref=tu_buf.at[k, r],
            send_sem=theta_send.at[k, r, 0],
            recv_sem=theta_recv.at[k, r, 0],
            device_id=at_sector(ns - 1),
            device_id_type=MESH,
        )
        down = pltpu.make_async_remote_copy(
            src_ref=sd_buf.at[k, r],
            dst_ref=td_buf.at[k, r],
            send_sem=theta_send.at[k, r, 1],
            recv_sem=theta_recv.at[k, r, 1],
            device_id=at_sector(1),
            device_id_type=MESH,
        )
        return up, down

    def to_lower_span(k):
        return pltpu.make_async_remote_copy(
            src_ref=ru_buf.at[k, 0],
            dst_ref=ru_buf.at[k, SPANS],
            send_sem=span_send.at[k, 0],
            recv_sem=span_recv.at[k, 0],
            device_id={"span": span - 1},
            device_id_type=MESH,
        )

    def to_upper_span(k):
        return pltpu.make_async_remote_copy(
            src_ref=rd_buf.at[k, SPANS],
            dst_ref=rd_buf.at[k, 0],
            send_sem=span_send.at[k, 1],
            recv_sem=span_recv.at[k, 1],
            device_id={"span": span + 1},
            device_id_type=MESH,
        )

    def beside_copy(source, target, sems, upward):
        slot = 0 if upward else 1
        return pltpu.make_async_remote_copy(
            src_ref=source,
            dst_ref=target.at[slot],
            send_sem=sems.at[0, slot],
            recv_sem=sems.at[1, slot],
            device_id={"span": span + 1 if upward else span - 1},
            device_id_type=MESH,
        )

    def coef_copy(upward):
        return beside_copy(coef.at[3], edge_coef, edge_coef_sems, upward)

    def ahead_copy(upward):
        return beside_copy(ahead_send.at[int(upward)], ahead_recv, ahead_sems, upward)

    @pl.when(span > 0)
    def _():
        coef_copy(False).start()

    @pl.when(span < nr - 1)
    def _():
        coef_copy(True).start()

    def send_ahead(k):
        for upward, r in ((False, 0), (True, SPANS - 1)):
            for a in range(2):
                outside = td_buf if a == 0 else tu_buf
                inside = rd_buf[k, r, a] if upward else ru_buf[k, r + 1, a]
                total = own_buf[k, r, a] - coefficient(2, r, a) * outside[k, r]
                ahead_send[int(upward), a] = total - coefficient(3, r, a) * inside

        @pl.when(span > 0)
        def _():
            ahead_copy(False).start()

        @pl.when(span < nr - 1)
        def _():
            ahead_copy(True).start()

    def receive_ahead(k):
        def complete(slot, r, terms, m):
            columns = []
            for a in range(2):
                cell = a * SPANS + r
                plane = ahead_recv[slot, a] - edge_coef[slot, cell : cell + 1, :] * terms[a]
                high, low = split(plane)
                columns.append(jnp.concatenate([high, low, high], axis=0))
            data = jnp.concatenate(columns, axis=1)
            return jnp.dot(weights[m * PAD : (m + 1) * PAD, :], data, preferred_element_type=F32)

        @pl.when(span < nr - 1)
        def _():
            coef_copy(False).wait_recv()
            ahead_copy(False).wait_recv()
            product = complete(1, 0, [rd_buf[k - 1, SPANS, a] for a in range(2)], 3)
            for a in range(2):
                ru_buf[k, SPANS, a] = product[:, a * LANES : (a + 1) * LANES]

        @pl.when(span > 0)
        def _():
            coef_copy(True).wait_recv()
            ahead_copy(True).wait_recv()
            product = complete(0, SPANS - 1, [ru_buf[k - 1, 0, a] for a in range(2)], 4)
            for a in range(2):
                rd_buf[k, 0, a] = product[:, a * LANES : (a + 1) * LANES]

    def rows_at(i):
        low = lax.rem(i + SPANS // 2 - 2, SPANS // 2)
        return low, SPANS - 1 - low

    def coefficient(n, r, a):
        return coef[n, pl.ds(a * SPANS + r, 1), :]

    def emit(k, rows, planes_of):
        for r, planes in zip(rows, planes_of):
            columns = []
            for plane in planes:
                high, low = split(plane)
                columns.append(jnp.concatenate([high, low, high], axis=0))
            data = jnp.concatenate(columns, axis=1)
            products = [
                jnp.dot(weights[start * PAD : stop * PAD, :], data, preferred_element_type=F32)
                for start, stop in ((0, 4), (4, NMAT))
            ]

            def part(m, a):
                m, product = (m, products[0]) if m < 4 else (m - 4, products[1])
                return product[m * PAD : (m + 1) * PAD, a * LANES : (a + 1) * LANES]

            su_buf[k, r] = part(1, 0)
            sd_buf[k, r] = part(2, 1)
            for a in range(2):
                ru_buf[k, r, a] = part(3, a)
                rd_buf[k, r + 1, a] = part(4, a)
                total = base[r, a] - coefficient(1, r, a) * part(0, a)
                total = total - coefficient(2, r, a) * (part(2, 0) if a else part(1, 1))
                total = total - coefficient(4, r, a) * pltpu.roll(part(5, a), LANES - 1, 1)
                own_buf[k, r, a] = total - coefficient(5, r, a) * pltpu.roll(part(6, a), 1, 1)

        if k != AHEAD:

            @pl.when((rows[0] == 0) & (span > 0))
            def _():
                to_lower_span(k).start()

            @pl.when((rows[0] == 0) & (span < nr - 1))
            def _():
                to_upper_span(k).start()

        for r in rows:
            for copy in theta_copies(k, r):
                copy.start()

    def update(k, rows):
        for r in rows:
            for copy in theta_copies(k, r):
                copy.wait_recv()

        if k == AHEAD - 1:

            @pl.when(rows[0] == 0)
            def _():
                send_ahead(k)

        if k == AHEAD:

            @pl.when(rows[0] == 0)
            def _():
                receive_ahead(k)

        else:

            @pl.when((rows[0] == 0) & (span < nr - 1))
            def _():
                to_lower_span(k).wait_recv()

            @pl.when((rows[0] == 0) & (span > 0))
            def _():
                to_upper_span(k).wait_recv()

        planes_of = []
        for r in rows:
            planes = []
            for a in range(2):
                outside = td_buf if a == 0 else tu_buf
                total = own_buf[k, r, a] - coefficient(2, r, a) * outside[k, r]
                planes.append(total - coefficient(3, r, a) * (ru_buf[k, r + 1, a] + rd_buf[k, r, a]))
            planes_of.append(planes)
        return planes_of

    def first(i, carry):
        rows = rows_at(i)
        emit(0, rows, [[base[r, a] for a in range(2)] for r in rows])
        return carry

    lax.fori_loop(0, SPANS // 2, first, 0)

    cell_row = jnp.bitwise_and(lax.broadcasted_iota(jnp.int32, (4 * SPANS, 2 * WIDE), 0), 2 * SPANS - 1)
    panel_lane = lax.broadcasted_iota(jnp.int32, (4 * SPANS, 2 * WIDE), 1)
    panel_cell = jnp.bitwise_and(panel_lane, SPANS - 1) + jnp.where(panel_lane < WIDE, 0, SPANS)
    to_panels = jnp.where(cell_row == panel_cell, 1.0, 0.0).astype(BF16)
    rows_twice = jnp.concatenate([instance_columns, instance_columns], axis=1).astype(BF16)

    half_column = jnp.bitwise_and(lax.broadcasted_iota(jnp.int32, (PAD, 32), 1), 15).astype(F32)
    of_instance = over_fields(index_of((PAD, 32), 0))[0] == half_column
    spread_rows = jnp.where(of_instance & (index_of((PAD, 32), 0) < ROWS), 1.0, 0.0).astype(BF16)
    gather_slot = jnp.bitwise_and(lax.broadcasted_iota(jnp.int32, (2 * WIDE, LANES), 0), 4 * SPANS - 1)
    gather_lane = lax.broadcasted_iota(jnp.int32, (2 * WIDE, LANES), 1)
    gather = jnp.where(gather_slot == gather_lane, 1.0, 0.0).astype(BF16)

    for t in range(NT):
        if shifts[t]:
            panel_copy(t).wait_recv()
            panel_rows[t : t + 1, :] = panel_recv[t, 0:1, :]
    cells_wide = jnp.zeros(wide, F32)
    for a in range(2):
        shares = panel_weight[a] * panel_rows[0:NT, :]
        shares = shares + pltpu.roll(shares, WIDE - SPANS, 1)
        shares = shares + pltpu.roll(shares, WIDE - 2 * SPANS, 1)
        if a:
            shares = pltpu.roll(shares, a * SPANS, 1)
        cells_wide = jnp.where(lane_panel == a, shares, cells_wide)
    cells_wide = cells_wide * inlet_inverse
    delta_send[0:NT, :] = cells_wide

    def delta_copy(n, device):
        return pltpu.make_async_remote_copy(
            src_ref=delta_send,
            dst_ref=delta_recv.at[n],
            send_sem=delta_sems.at[0, n],
            recv_sem=delta_sems.at[1, n],
            device_id=device,
            device_id_type=MESH,
        )

    from_left = delta_copy(0, at_sector(1))
    from_right = delta_copy(1, at_sector(ns - 1))
    from_lower = delta_copy(2, {"span": span + 1})
    from_upper = delta_copy(3, {"span": span - 1})

    @pl.when(span < nr - 1)
    def _():
        from_lower.start()

    @pl.when(span > 0)
    def _():
        from_upper.start()

    from_left.start()
    from_right.start()

    slot = jnp.bitwise_and(lax.broadcasted_iota(jnp.int32, wide, 1), 4 * SPANS - 1)

    def place(values, n, shift, low, high):
        moved = pltpu.roll(delta_recv[n, 0:NT, :], shift % WIDE, 1)
        return jnp.where((slot >= low) & (slot < high), moved, values)

    def to_columns(values):
        high, low = split(jnp.concatenate([values, jnp.zeros((16 - NT, WIDE), F32)], axis=0))
        spread = jnp.dot(spread_rows, jnp.concatenate([high, low], axis=0), preferred_element_type=F32)
        high, low = split(jnp.where(same_field, spread, 0.0))
        return jnp.dot(jnp.concatenate([high, low], axis=1), gather, preferred_element_type=F32)

    def stacked(columns):
        high, low = split(columns)
        return jnp.concatenate([high, low, high], axis=0)

    def inlet_coefficient(n, axial_cell):
        return pltpu.roll(coef_columns[axial_cell : axial_cell + 1, :], (LANES - 2 * SPANS * n) % LANES, 1)

    columns = to_columns(cells_wide)
    product = jnp.dot(weights[...], stacked(columns), preferred_element_type=F32)
    from_left.wait_recv()
    from_right.wait_recv()
    around = place(jnp.zeros(wide, F32), 0, SPANS, 2 * SPANS, 3 * SPANS)
    around = place(around, 1, 3 * SPANS, 3 * SPANS, 4 * SPANS)
    around = jnp.dot(weights[PAD : 3 * PAD, :], stacked(to_columns(around)), preferred_element_type=F32)
    around = pltpu.roll(around, LANES - 2 * SPANS, 1)

    def moved_part(m, shift):
        return pltpu.roll(product[m * PAD : (m + 1) * PAD, :], shift % LANES, 1)

    first_half = lane < SPANS
    along = jnp.where(first_half, moved_part(1, -SPANS), around[0:PAD])
    along = along + jnp.where(first_half, around[PAD : 2 * PAD], moved_part(2, SPANS))
    across = jnp.where(jnp.bitwise_and(lane, SPANS - 1) == SPANS - 1, 0.0, moved_part(3, -1))
    below = jnp.where(jnp.bitwise_and(lane, SPANS - 1) == 0, 0.0, moved_part(4, 1))
    coupled = inlet_coefficient(1, 0) * product[0:PAD, :]
    coupled = coupled + inlet_coefficient(2, 0) * along
    coupled = coupled + inlet_coefficient(3, 0) * (across + below)
    delta_columns[...] = columns
    delta_shift[0] = columns - coupled
    delta_shift[1] = inlet_coefficient(5, 1) * product[6 * PAD : 7 * PAD, :]

    def beyond_span():
        @pl.when(span > 0)
        def _():
            from_lower.wait_recv()

        @pl.when(span < nr - 1)
        def _():
            from_upper.wait_recv()

        cells = jnp.zeros(wide, F32)
        for a in range(2):
            top, bottom = (a + 1) * SPANS - 1, a * SPANS
            cells = place(cells, 2, bottom - top, bottom, bottom + 1)
            cells = place(cells, 3, top - bottom, top, top + 1)
        product = jnp.dot(weights[3 * PAD : 5 * PAD, :], stacked(to_columns(cells)), preferred_element_type=F32)
        above = jnp.where(jnp.bitwise_and(lane, SPANS - 1) == SPANS - 1, product[0:PAD], 0.0)
        below = jnp.where(jnp.bitwise_and(lane, SPANS - 1) == 0, product[PAD : 2 * PAD], 0.0)
        delta_shift[0] = delta_shift[0] - inlet_coefficient(3, 0) * (above + below)

    def second(i, carry):
        rows = rows_at(i)
        planes_of = []
        for r, planes in zip(rows, update(0, rows)):
            corrected = []
            for a, plane in enumerate(planes):
                shift = lax.rem(LANES - a * SPANS - r, LANES)
                moved = pltpu.roll(delta_columns[...], shift, 1)
                base[r, a] = base[r, a] + jnp.where(lane == 0, moved, 0.0)
                plane = plane + jnp.where(lane == 0, pltpu.roll(delta_shift[0], shift, 1), 0.0)
                shift = lax.rem(shift + 1, LANES)
                corrected.append(plane - jnp.where(lane == 1, pltpu.roll(delta_shift[1], shift, 1), 0.0))
            planes_of.append(corrected)
        emit(1, rows, planes_of)
        return carry

    second(0, 0)
    second(1, 0)
    beyond_span()
    lax.fori_loop(2, SPANS // 2, second, 0)

    for k in range(1, SWEEPS - 1):

        def middle(i, carry, k=k):
            rows = rows_at(i)
            emit(k + 1, rows, update(k, rows))
            return carry

        lax.fori_loop(0, SPANS // 2, middle, 0)

    inlet[...] = jnp.zeros_like(inlet)

    def last(i, carry):
        rows = SPANS // 2 - 1 - i, SPANS // 2 + i
        for r, planes in zip(rows, update(SWEEPS - 1, rows)):
            for a in range(2):
                out[a * SPANS + r] = planes[a]
                inlet[...] = jnp.where(
                    lane == a * SPANS + r, pltpu.roll(planes[a], a * SPANS + r, 1), inlet[...]
                )
        return carry

    lax.fori_loop(0, SPANS // 2, last, 0)

    high, low = split(inlet[...])
    cells = jnp.concatenate([high[:, 0 : 2 * SPANS], low[:, 0 : 2 * SPANS]], axis=1)
    spread = jnp.dot(cells, to_panels, preferred_element_type=F32)
    spread = jnp.where(jnp.concatenate([same_field, same_field], axis=1), spread, 0.0)
    high, low = split(spread)
    gathered = jnp.dot(rows_twice, jnp.concatenate([high, low], axis=0), preferred_element_type=F32)
    back = panel_weight[0] * gathered[:, 0:WIDE] + panel_weight[1] * gathered[:, WIDE:]
    panel_rows[0:NT, :] = back
    for t in range(NT):
        if shifts[t]:
            back_send[t, 0:1, :] = panel_rows[t : t + 1, :]
            back_copy(t).start()
    for t in range(NT):
        if shifts[t]:
            back_copy(t).wait_recv()
            panel_rows[t : t + 1, :] = back_recv[t, 0:1, :]
    sens[...] = jnp.transpose(panel_rows[0:NT, 0 : NF * PT * SPANS])

    for t in range(NT):
        if shifts[t]:
            panel_copy(t).wait_send()
            back_copy(t).wait_send()

    from_left.wait_send()
    from_right.wait_send()

    @pl.when(span < nr - 1)
    def _():
        from_lower.wait_send()

    @pl.when(span > 0)
    def _():
        from_upper.wait_send()

    def drain(i, carry):
        k, r = i // SPANS, lax.rem(i, SPANS)
        for copy in theta_copies(k, r):
            copy.wait_send()
        return carry

    lax.fori_loop(0, SWEEPS * SPANS, drain, 0)
    @pl.when(span > 0)
    def _():
        coef_copy(False).wait_send()
        ahead_copy(False).wait_send()
        for k in range(SWEEPS):
            if k != AHEAD:
                to_lower_span(k).wait_send()

    @pl.when(span < nr - 1)
    def _():
        coef_copy(True).wait_send()
        ahead_copy(True).wait_send()
        for k in range(SWEEPS):
            if k != AHEAD:
                to_upper_span(k).wait_send()


def store(planes, table, out, sens, sems):
    copies = [pltpu.make_async_copy(table, sens, sems.at[2 * SPANS])]
    for cell in range(2 * SPANS):
        copies.append(pltpu.make_async_copy(planes.at[cell, 0:ROWS], out.at[:, cell], sems.at[cell]))
    for copy in copies:
        copy.start()
    for copy in copies:
        copy.wait()


def on_device(ns, nr, rhs, diag_coef, face_coef, time_coef, jac_up, jac_down, wall_mask, stator_adj, owner, share):
    nt, nf, ct, spans, nax = rhs.shape
    plane = (SWEEPS, SPANS, 2, PAD, LANES)
    ring = (SWEEPS, SPANS + 1, 2, PAD, LANES)
    edge = (SWEEPS, SPANS, PAD, LANES)
    inputs = (
        rhs.reshape(nt * nf * ct * spans, nax),
        diag_coef.reshape(ct * spans, nax),
        face_coef.reshape(3, ct * spans, nax),
        time_coef.reshape(ct * spans, nax),
        jac_up,
        jac_down,
        wall_mask.reshape(ct * spans, nax),
        stator_adj.transpose(1, 2, 3, 0).reshape(nf * PT * spans, nt),
        owner.transpose(1, 2, 0).reshape(ct * spans, nt),
        share.transpose(1, 2, 0).reshape(ct * spans, nt),
        jnp.asarray(time_operator()),
    )
    planes, table = pl.pallas_call(
        functools.partial(kernel, ns, nr),
        out_shape=(
            pltpu.VMEM((ct * spans, PAD, nax), F32),
            pltpu.VMEM((nf * PT * spans, nt), F32),
        ),
        in_specs=[pl.BlockSpec(memory_space=pltpu.HBM)] * len(inputs),
        out_specs=(pl.BlockSpec(memory_space=pltpu.VMEM),) * 2,
        scratch_shapes=[pltpu.VMEM(x.shape, x.dtype) for x in inputs]
        + [
            pltpu.VMEM((NMAT * PAD, 3 * PAD), BF16),
            pltpu.VMEM((8, 2 * SPANS, LANES), F32),
            pltpu.VMEM(plane[1:], F32),
            pltpu.VMEM(plane, F32),
            pltpu.VMEM(edge, F32),
            pltpu.VMEM(edge, F32),
            pltpu.VMEM(ring, F32),
            pltpu.VMEM(ring, F32),
            pltpu.VMEM(edge, F32),
            pltpu.VMEM(edge, F32),
            pltpu.VMEM((NT, 1, WIDE), F32),
            pltpu.VMEM((NT, 1, WIDE), F32),
            pltpu.VMEM((16, WIDE), F32),
            pltpu.VMEM((2, NT, WIDE), F32),
            pltpu.VMEM((PAD, LANES), F32),
            pltpu.VMEM((NT, 1, WIDE), F32),
            pltpu.VMEM((NT, 1, WIDE), F32),
            pltpu.VMEM((48, 8), F32),
            pltpu.VMEM((16, WIDE), F32),
            pltpu.VMEM((4, 16, WIDE), F32),
            pltpu.VMEM((PAD, LANES), F32),
            pltpu.VMEM((2, PAD, LANES), F32),
            pltpu.SemaphoreType.DMA((len(inputs),)),
            pltpu.SemaphoreType.DMA((SWEEPS, SPANS, 2)),
            pltpu.SemaphoreType.DMA((SWEEPS, SPANS, 2)),
            pltpu.SemaphoreType.DMA((SWEEPS, 2)),
            pltpu.SemaphoreType.DMA((SWEEPS, 2)),
            pltpu.SemaphoreType.DMA((2, NT)),
            pltpu.SemaphoreType.DMA((2, NT)),
            pltpu.SemaphoreType.DMA((2, 4)),
            pltpu.VMEM((2, 2, PAD, LANES), F32),
            pltpu.VMEM((2, 2, PAD, LANES), F32),
            pltpu.SemaphoreType.DMA((2, 2)),
            pltpu.VMEM((2, 2 * SPANS, LANES), F32),
            pltpu.SemaphoreType.DMA((2, 2)),
        ],
        compiler_params=pltpu.CompilerParams(
            collective_id=0, has_side_effects=True, vmem_limit_bytes=60 * 2**20
        ),
    )(*inputs)
    out, sens = pl.pallas_call(
        store,
        out_shape=(
            jax.ShapeDtypeStruct((nt * nf, ct * spans, nax), F32),
            jax.ShapeDtypeStruct((nf * PT * spans, nt), F32),
        ),
        in_specs=[pl.BlockSpec(memory_space=pltpu.VMEM)] * 2,
        out_specs=(pl.BlockSpec(memory_space=pltpu.HBM),) * 2,
        scratch_shapes=[pltpu.SemaphoreType.DMA((2 * SPANS + 1,))],
    )(pltpu.with_memory_space_constraint(planes, pltpu.VMEM), pltpu.with_memory_space_constraint(table, pltpu.VMEM))
    sens = sens.reshape(nf, PT, spans, nt).transpose(3, 0, 1, 2)
    return out.reshape(rhs.shape), sens


def solution(mesh):
    in_specs = (
        P(None, None, "sector", "span", None),
        P("sector", "span", None),
        P(None, "sector", "span", None),
        P("sector", "span", None),
        P(),
        P(),
        P("sector", "span", None),
        P(None, None, "sector", "span"),
        P(None, "sector", "span"),
        P(None, "sector", "span"),
    )
    out_specs = (P(None, None, "sector", "span", None), P(None, None, "sector", "span"))
    return jax.shard_map(
        functools.partial(on_device, mesh.shape["sector"], mesh.shape["span"]),
        mesh=mesh,
        in_specs=in_specs,
        out_specs=out_specs,
        check_vma=False,
    )
```

```python
import functools

import jax
import jax.numpy as jnp
import ml_dtypes
import numpy as np
from jax import lax
from jax.experimental import pallas as pl
from jax.experimental.pallas import tpu as pltpu
from jax.sharding import PartitionSpec as P

SWEEPS = 4
AHEAD = 2
NT = 11
NF = 7
ROWS = NT * NF
PAD = 80
NMAT = 7
SPANS = 8
PT = 4
LANES = 128
WIDE = 256
F32 = jnp.float32
BF16 = jnp.bfloat16
HIGHEST = lax.Precision.HIGHEST
MESH = pl.DeviceIdType.MESH


def time_operator():
    step = np.arange(NT)[:, None] - np.arange(NT)[None, :]
    sines = np.where(step == 0, 1.0, np.sin(np.pi * step / NT))
    spectral = np.where(step == 0, 0.0, 0.5 * (1.0 - 2.0 * (step % 2)) / sines)
    table = np.zeros((PAD, PAD), np.float32)
    table[:ROWS, :ROWS] = np.kron(spectral.T, np.eye(NF))
    high = table.astype(ml_dtypes.bfloat16)
    low = (table - high.astype(np.float32)).astype(ml_dtypes.bfloat16)
    return np.concatenate([high, high, low], axis=1)


def shift_of(instance, count):
    return ((instance * count) // (NT - 1) - instance // (NT - 1)) % count


def split(value):
    high = value.astype(BF16)
    low = (value - high.astype(F32)).astype(BF16)
    return high, low


def index_of(shape, dim):
    return lax.broadcasted_iota(jnp.int32, shape, dim).astype(F32)


def over_fields(rows):
    instance = jnp.floor((rows + 0.5) * (1.0 / NF))
    return instance, rows - NF * instance


def exact_dot(left, right):
    return jnp.dot(left, right, precision=HIGHEST, preferred_element_type=F32)


def kernel(ns, nr, *refs):
    hbm, refs = refs[:11], refs[11:]
    (out, sens), refs = refs[:2], refs[2:]
    vmem, refs = refs[:11], refs[11:]
    rhs, diag, face, time, jac_up, jac_down, wall, stator, owner, share, time_op = vmem
    (
        weights,
        coef,
        base,
        own_buf,
        tu_buf,
        td_buf,
        ru_buf,
        rd_buf,
        su_buf,
        sd_buf,
        panel_send,
        panel_recv,
        panel_rows,
        panel_weight,
        inlet,
        back_send,
        back_recv,
        jac_rows,
        delta_send,
        delta_recv,
        delta_columns,
        delta_shift,
        input_sems,
        theta_send,
        theta_recv,
        span_send,
        span_recv,
        panel_sems,
        back_sems,
        delta_sems,
        ahead_send,
        ahead_recv,
        ahead_sems,
        edge_coef,
        edge_coef_sems,
    ) = refs
    sector = lax.axis_index("sector")
    span = lax.axis_index("span")
    shifts = [shift_of(t, ns) for t in range(NT)]
    partners = sorted({d % ns for s in shifts for d in (s, -s)} | {1 % ns, (ns - 1) % ns})
    partners = [d for d in partners if d != 0]

    def at_sector(step):
        return {"sector": lax.rem(sector + step, ns)}

    def load(n):
        target = vmem[n] if n else rhs.at[0 : ROWS * 2 * SPANS]
        return pltpu.make_async_copy(hbm[n], target, input_sems.at[n])

    for n in (7, 0, 1, 6, 8, 9, 4, 5, 10, 2, 3):
        load(n).start()

    ru_buf[:, SPANS] = jnp.zeros((SWEEPS,) + ru_buf.shape[2:], F32)
    rd_buf[:, 0] = jnp.zeros((SWEEPS,) + rd_buf.shape[2:], F32)

    delta_recv[...] = jnp.zeros_like(delta_recv)

    barrier = pltpu.get_barrier_semaphore()
    for step in partners:
        pl.semaphore_signal(barrier, inc=1, device_id=at_sector(step), device_id_type=MESH)

    @pl.when(span > 0)
    def _():
        pl.semaphore_signal(barrier, inc=1, device_id={"span": span - 1}, device_id_type=MESH)

    @pl.when(span < nr - 1)
    def _():
        pl.semaphore_signal(barrier, inc=1, device_id={"span": span + 1}, device_id_type=MESH)

    wide = (NT, WIDE)
    load(7).wait()
    panel_rows[...] = jnp.zeros_like(panel_rows)
    panel_rows[0:NT, 0 : NF * PT * SPANS] = jnp.transpose(stator[...])
    for t in range(NT):
        panel_send[t, 0:1, :] = panel_rows[t : t + 1, :]

    def panel_copy(t):
        return pltpu.make_async_remote_copy(
            src_ref=panel_send.at[t],
            dst_ref=panel_recv.at[t],
            send_sem=panel_sems.at[0, t],
            recv_sem=panel_sems.at[1, t],
            device_id=at_sector(ns - shifts[t]),
            device_id_type=MESH,
        )

    def back_copy(t):
        return pltpu.make_async_remote_copy(
            src_ref=back_send.at[t],
            dst_ref=back_recv.at[t],
            send_sem=back_sems.at[0, t],
            recv_sem=back_sems.at[1, t],
            device_id=at_sector(shifts[t]),
            device_id_type=MESH,
        )

    lane = lax.broadcasted_iota(jnp.int32, (PAD, LANES), 1)
    row = index_of((PAD, 3 * PAD), 0)
    column = index_of((PAD, 3 * PAD), 1)
    column = column - PAD * jnp.floor((column + 0.5) * (1.0 / PAD))
    row_instance, _ = over_fields(row)
    column_instance, _ = over_fields(column)
    same_instance = (row_instance == column_instance) & (row < ROWS) & (column < ROWS)
    instance_rows = jnp.where(
        (over_fields(index_of((PAD, NT), 0))[0] == index_of((PAD, NT), 1)) & (index_of((PAD, NT), 0) < ROWS), 1.0, 0.0
    )
    instance_columns = jnp.where(
        (over_fields(index_of((NT, PAD), 1))[0] == index_of((NT, PAD), 0)) & (index_of((NT, PAD), 1) < ROWS), 1.0, 0.0
    )
    wide_lane = lax.broadcasted_iota(jnp.int32, (PAD, WIDE), 1)
    wide_field = lax.shift_right_logical(wide_lane, 5).astype(F32)
    same_field = over_fields(index_of((PAD, WIDE), 0))[1] == wide_field
    lane_panel = jnp.bitwise_and(lax.shift_right_logical(lax.broadcasted_iota(jnp.int32, wide, 1), 3), PT - 1)

    load(4).wait()
    load(5).wait()
    load(10).wait()
    jac_rows[...] = jnp.zeros_like(jac_rows)
    for direction in range(3):
        for side, table in enumerate((jac_up, jac_down)):
            start = (2 * direction + side) * 8
            jac_rows[start : start + NF, 0:NF] = table[direction]
    high, low = split(jac_rows[...])
    wide_columns = index_of((8, 3 * PAD), 1)
    piece = jnp.floor((wide_columns + 0.5) * (1.0 / PAD))
    chosen = over_fields(wide_columns - PAD * piece)[1] == index_of((8, 3 * PAD), 0)
    pick_high = jnp.where(chosen & (piece < 2.0), 1.0, 0.0).astype(BF16)
    pick_low = jnp.where(chosen & (piece > 1.0), 1.0, 0.0).astype(BF16)
    columns = jnp.dot(high, pick_high, preferred_element_type=F32)
    columns = (columns + jnp.dot(low, pick_low, preferred_element_type=F32)).astype(BF16)
    _, field_of_row = over_fields(index_of((PAD, 8), 0))
    pick_row = jnp.where(field_of_row == index_of((PAD, 8), 1), 1.0, 0.0).astype(BF16)
    weights[0:PAD, :] = time_op[...]
    for m in range(1, NMAT):
        block = jnp.dot(pick_row, columns[8 * (m - 1) : 8 * m, :], preferred_element_type=F32)
        weights[m * PAD : (m + 1) * PAD, :] = jnp.where(same_instance, block, 0.0).astype(BF16)

    for n in (0, 1, 2, 3, 6, 8, 9):
        load(n).wait()
    inverse = wall[...].astype(F32) / diag[...]
    axial_lane = lax.broadcasted_iota(jnp.int32, inverse.shape, 1)
    axial = inverse * face[2]
    coef[0] = inverse
    coef[1] = inverse * time[...]
    coef[2] = inverse * face[0]
    coef[3] = inverse * face[1]
    coef[4] = jnp.where(axial_lane == LANES - 1, 0.0, axial)
    coef[5] = jnp.where(axial_lane == 0, 0.0, axial)
    coef[6] = jnp.zeros_like(inverse)
    coef[7] = jnp.zeros_like(inverse)
    coef_columns = jnp.transpose(coef[...].reshape(8 * 2 * SPANS, LANES))
    cell_lanes = jnp.bitwise_and(lax.broadcasted_iota(jnp.int32, (LANES, WIDE), 1), 4 * SPANS - 1)
    to_cells = jnp.where(
        (cell_lanes == lax.broadcasted_iota(jnp.int32, (LANES, WIDE), 0)) & (cell_lanes < 2 * SPANS), 1.0, 0.0
    )
    inlet_inverse = exact_dot(coef_columns[0:8, :], to_cells)[0:1, :]

    spread_lanes = lax.broadcasted_iota(jnp.int32, (SPANS, WIDE), 1)
    spread_span = jnp.where(
        jnp.bitwise_and(spread_lanes, SPANS - 1) == lax.broadcasted_iota(jnp.int32, (SPANS, WIDE), 0), 1.0, 0.0
    )
    for a in range(2):
        cells = pl.ds(a * SPANS, SPANS)
        share_wide = exact_dot(jnp.transpose(share[cells, :]), spread_span)
        first = jnp.bitwise_and(owner[cells, :], PT - 1).astype(F32)
        first_wide = exact_dot(jnp.transpose(first), spread_span)
        own_panel = lane_panel.astype(F32)
        lower = jnp.where(first_wide == own_panel, share_wide, 0.0)
        upper = jnp.where(first_wide == own_panel - 1.0, 1.0 - share_wide, 0.0)
        panel_weight[a] = lower + upper

    base[...] = jnp.zeros_like(base)
    for r in range(SPANS):
        for a in range(2):
            cell = a * SPANS + r
            plane = rhs[pl.ds(cell, ROWS, stride=2 * SPANS), :]
            base[r, a, 0:ROWS, :] = plane * coef[0, cell : cell + 1, :]

    beside = (span > 0).astype(jnp.int32) + (span < nr - 1).astype(jnp.int32)
    pl.semaphore_wait(barrier, len(partners) + beside)

    for t in range(NT):
        if shifts[t]:
            panel_copy(t).start()

    def theta_copies(k, r):
        up = pltpu.make_async_remote_copy(
            src_ref=su_buf.at[k, r],
            dst_ref=tu_buf.at[k, r],
            send_sem=theta_send.at[k, r, 0],
            recv_sem=theta_recv.at[k, r, 0],
            device_id=at_sector(ns - 1),
            device_id_type=MESH,
        )
        down = pltpu.make_async_remote_copy(
            src_ref=sd_buf.at[k, r],
            dst_ref=td_buf.at[k, r],
            send_sem=theta_send.at[k, r, 1],
            recv_sem=theta_recv.at[k, r, 1],
            device_id=at_sector(1),
            device_id_type=MESH,
        )
        return up, down

    def to_lower_span(k):
        return pltpu.make_async_remote_copy(
            src_ref=ru_buf.at[k, 0],
            dst_ref=ru_buf.at[k, SPANS],
            send_sem=span_send.at[k, 0],
            recv_sem=span_recv.at[k, 0],
            device_id={"span": span - 1},
            device_id_type=MESH,
        )

    def to_upper_span(k):
        return pltpu.make_async_remote_copy(
            src_ref=rd_buf.at[k, SPANS],
            dst_ref=rd_buf.at[k, 0],
            send_sem=span_send.at[k, 1],
            recv_sem=span_recv.at[k, 1],
            device_id={"span": span + 1},
            device_id_type=MESH,
        )

    def beside_copy(source, target, sems, upward):
        slot = 0 if upward else 1
        return pltpu.make_async_remote_copy(
            src_ref=source,
            dst_ref=target.at[slot],
            send_sem=sems.at[0, slot],
            recv_sem=sems.at[1, slot],
            device_id={"span": span + 1 if upward else span - 1},
            device_id_type=MESH,
        )

    def coef_copy(upward):
        return beside_copy(coef.at[3], edge_coef, edge_coef_sems, upward)

    def ahead_copy(upward):
        return beside_copy(ahead_send.at[int(upward)], ahead_recv, ahead_sems, upward)

    @pl.when(span > 0)
    def _():
        coef_copy(False).start()

    @pl.when(span < nr - 1)
    def _():
        coef_copy(True).start()

    def send_ahead(k):
        for upward, r in ((False, 0), (True, SPANS - 1)):
            for a in range(2):
                outside = td_buf if a == 0 else tu_buf
                inside = rd_buf[k, r, a] if upward else ru_buf[k, r + 1, a]
                total = own_buf[k, r, a] - coefficient(2, r, a) * outside[k, r]
                ahead_send[int(upward), a] = total - coefficient(3, r, a) * inside

        @pl.when(span > 0)
        def _():
            ahead_copy(False).start()

        @pl.when(span < nr - 1)
        def _():
            ahead_copy(True).start()

    def receive_ahead(k):
        def complete(slot, r, terms, m):
            columns = []
            for a in range(2):
                cell = a * SPANS + r
                plane = ahead_recv[slot, a] - edge_coef[slot, cell : cell + 1, :] * terms[a]
                high, low = split(plane)
                columns.append(jnp.concatenate([high, low, high], axis=0))
            data = jnp.concatenate(columns, axis=1)
            return jnp.dot(weights[m * PAD : (m + 1) * PAD, :], data, preferred_element_type=F32)

        @pl.when(span < nr - 1)
        def _():
            coef_copy(False).wait_recv()
            ahead_copy(False).wait_recv()
            product = complete(1, 0, [rd_buf[k - 1, SPANS, a] for a in range(2)], 3)
            for a in range(2):
                ru_buf[k, SPANS, a] = product[:, a * LANES : (a + 1) * LANES]

        @pl.when(span > 0)
        def _():
            coef_copy(True).wait_recv()
            ahead_copy(True).wait_recv()
            product = complete(0, SPANS - 1, [ru_buf[k - 1, 0, a] for a in range(2)], 4)
            for a in range(2):
                rd_buf[k, 0, a] = product[:, a * LANES : (a + 1) * LANES]

    def rows_at(i):
        low = lax.rem(i + SPANS // 2 - 2, SPANS // 2)
        return low, SPANS - 1 - low

    def coefficient(n, r, a):
        return coef[n, pl.ds(a * SPANS + r, 1), :]

    def emit(k, rows, planes_of):
        for r, planes in zip(rows, planes_of):
            columns = []
            for plane in planes:
                high, low = split(plane)
                columns.append(jnp.concatenate([high, low, high], axis=0))
            data = jnp.concatenate(columns, axis=1)
            products = [
                jnp.dot(weights[start * PAD : stop * PAD, :], data, preferred_element_type=F32)
                for start, stop in ((0, 4), (4, NMAT))
            ]

            def part(m, a):
                m, product = (m, products[0]) if m < 4 else (m - 4, products[1])
                return product[m * PAD : (m + 1) * PAD, a * LANES : (a + 1) * LANES]

            su_buf[k, r] = part(1, 0)
            sd_buf[k, r] = part(2, 1)
            for a in range(2):
                ru_buf[k, r, a] = part(3, a)
                rd_buf[k, r + 1, a] = part(4, a)
                total = base[r, a] - coefficient(1, r, a) * part(0, a)
                total = total - coefficient(2, r, a) * (part(2, 0) if a else part(1, 1))
                total = total - coefficient(4, r, a) * pltpu.roll(part(5, a), LANES - 1, 1)
                own_buf[k, r, a] = total - coefficient(5, r, a) * pltpu.roll(part(6, a), 1, 1)

        if k != AHEAD:

            @pl.when((rows[0] == 0) & (span > 0))
            def _():
                to_lower_span(k).start()

            @pl.when((rows[0] == 0) & (span < nr - 1))
            def _():
                to_upper_span(k).start()

        for r in rows:
            for copy in theta_copies(k, r):
                copy.start()

    def update(k, rows):
        for r in rows:
            for copy in theta_copies(k, r):
                copy.wait_recv()

        if k == AHEAD - 1:

            @pl.when(rows[0] == 0)
            def _():
                send_ahead(k)

        if k == AHEAD:

            @pl.when(rows[0] == 0)
            def _():
                receive_ahead(k)

        else:

            @pl.when((rows[0] == 0) & (span < nr - 1))
            def _():
                to_lower_span(k).wait_recv()

            @pl.when((rows[0] == 0) & (span > 0))
            def _():
                to_upper_span(k).wait_recv()

        planes_of = []
        for r in rows:
            planes = []
            for a in range(2):
                outside = td_buf if a == 0 else tu_buf
                total = own_buf[k, r, a] - coefficient(2, r, a) * outside[k, r]
                planes.append(total - coefficient(3, r, a) * (ru_buf[k, r + 1, a] + rd_buf[k, r, a]))
            planes_of.append(planes)
        return planes_of

    def first(i, carry):
        rows = rows_at(i)
        emit(0, rows, [[base[r, a] for a in range(2)] for r in rows])
        return carry

    lax.fori_loop(0, SPANS // 2, first, 0)

    cell_row = jnp.bitwise_and(lax.broadcasted_iota(jnp.int32, (4 * SPANS, 2 * WIDE), 0), 2 * SPANS - 1)
    panel_lane = lax.broadcasted_iota(jnp.int32, (4 * SPANS, 2 * WIDE), 1)
    panel_cell = jnp.bitwise_and(panel_lane, SPANS - 1) + jnp.where(panel_lane < WIDE, 0, SPANS)
    to_panels = jnp.where(cell_row == panel_cell, 1.0, 0.0).astype(BF16)
    rows_twice = jnp.concatenate([instance_columns, instance_columns], axis=1).astype(BF16)

    half_column = jnp.bitwise_and(lax.broadcasted_iota(jnp.int32, (PAD, 32), 1), 15).astype(F32)
    of_instance = over_fields(index_of((PAD, 32), 0))[0] == half_column
    spread_rows = jnp.where(of_instance & (index_of((PAD, 32), 0) < ROWS), 1.0, 0.0).astype(BF16)
    gather_slot = jnp.bitwise_and(lax.broadcasted_iota(jnp.int32, (2 * WIDE, LANES), 0), 4 * SPANS - 1)
    gather_lane = lax.broadcasted_iota(jnp.int32, (2 * WIDE, LANES), 1)
    gather = jnp.where(gather_slot == gather_lane, 1.0, 0.0).astype(BF16)

    for t in range(NT):
        if shifts[t]:
            panel_copy(t).wait_recv()
            panel_rows[t : t + 1, :] = panel_recv[t, 0:1, :]
    cells_wide = jnp.zeros(wide, F32)
    for a in range(2):
        shares = panel_weight[a] * panel_rows[0:NT, :]
        shares = shares + pltpu.roll(shares, WIDE - SPANS, 1)
        shares = shares + pltpu.roll(shares, WIDE - 2 * SPANS, 1)
        if a:
            shares = pltpu.roll(shares, a * SPANS, 1)
        cells_wide = jnp.where(lane_panel == a, shares, cells_wide)
    cells_wide = cells_wide * inlet_inverse
    delta_send[0:NT, :] = cells_wide

    def delta_copy(n, device):
        return pltpu.make_async_remote_copy(
            src_ref=delta_send,
            dst_ref=delta_recv.at[n],
            send_sem=delta_sems.at[0, n],
            recv_sem=delta_sems.at[1, n],
            device_id=device,
            device_id_type=MESH,
        )

    from_left = delta_copy(0, at_sector(1))
    from_right = delta_copy(1, at_sector(ns - 1))
    from_lower = delta_copy(2, {"span": span + 1})
    from_upper = delta_copy(3, {"span": span - 1})

    @pl.when(span < nr - 1)
    def _():
        from_lower.start()

    @pl.when(span > 0)
    def _():
        from_upper.start()

    from_left.start()
    from_right.start()

    slot = jnp.bitwise_and(lax.broadcasted_iota(jnp.int32, wide, 1), 4 * SPANS - 1)

    def place(values, n, shift, low, high):
        moved = pltpu.roll(delta_recv[n, 0:NT, :], shift % WIDE, 1)
        return jnp.where((slot >= low) & (slot < high), moved, values)

    def to_columns(values):
        high, low = split(jnp.concatenate([values, jnp.zeros((16 - NT, WIDE), F32)], axis=0))
        spread = jnp.dot(spread_rows, jnp.concatenate([high, low], axis=0), preferred_element_type=F32)
        high, low = split(jnp.where(same_field, spread, 0.0))
        return jnp.dot(jnp.concatenate([high, low], axis=1), gather, preferred_element_type=F32)

    def stacked(columns):
        high, low = split(columns)
        return jnp.concatenate([high, low, high], axis=0)

    def inlet_coefficient(n, axial_cell):
        return pltpu.roll(coef_columns[axial_cell : axial_cell + 1, :], (LANES - 2 * SPANS * n) % LANES, 1)

    columns = to_columns(cells_wide)
    product = jnp.dot(weights[...], stacked(columns), preferred_element_type=F32)
    from_left.wait_recv()
    from_right.wait_recv()
    around = place(jnp.zeros(wide, F32), 0, SPANS, 2 * SPANS, 3 * SPANS)
    around = place(around, 1, 3 * SPANS, 3 * SPANS, 4 * SPANS)
    around = jnp.dot(weights[PAD : 3 * PAD, :], stacked(to_columns(around)), preferred_element_type=F32)
    around = pltpu.roll(around, LANES - 2 * SPANS, 1)

    def moved_part(m, shift):
        return pltpu.roll(product[m * PAD : (m + 1) * PAD, :], shift % LANES, 1)

    first_half = lane < SPANS
    along = jnp.where(first_half, moved_part(1, -SPANS), around[0:PAD])
    along = along + jnp.where(first_half, around[PAD : 2 * PAD], moved_part(2, SPANS))
    across = jnp.where(jnp.bitwise_and(lane, SPANS - 1) == SPANS - 1, 0.0, moved_part(3, -1))
    below = jnp.where(jnp.bitwise_and(lane, SPANS - 1) == 0, 0.0, moved_part(4, 1))
    coupled = inlet_coefficient(1, 0) * product[0:PAD, :]
    coupled = coupled + inlet_coefficient(2, 0) * along
    coupled = coupled + inlet_coefficient(3, 0) * (across + below)
    delta_columns[...] = columns
    delta_shift[0] = columns - coupled
    delta_shift[1] = inlet_coefficient(5, 1) * product[6 * PAD : 7 * PAD, :]

    def beyond_span():
        @pl.when(span > 0)
        def _():
            from_lower.wait_recv()

        @pl.when(span < nr - 1)
        def _():
            from_upper.wait_recv()

        cells = jnp.zeros(wide, F32)
        for a in range(2):
            top, bottom = (a + 1) * SPANS - 1, a * SPANS
            cells = place(cells, 2, bottom - top, bottom, bottom + 1)
            cells = place(cells, 3, top - bottom, top, top + 1)
        product = jnp.dot(weights[3 * PAD : 5 * PAD, :], stacked(to_columns(cells)), preferred_element_type=F32)
        above = jnp.where(jnp.bitwise_and(lane, SPANS - 1) == SPANS - 1, product[0:PAD], 0.0)
        below = jnp.where(jnp.bitwise_and(lane, SPANS - 1) == 0, product[PAD : 2 * PAD], 0.0)
        delta_shift[0] = delta_shift[0] - inlet_coefficient(3, 0) * (above + below)

    def second(i, carry):
        rows = rows_at(i)
        planes_of = []
        for r, planes in zip(rows, update(0, rows)):
            corrected = []
            for a, plane in enumerate(planes):
                shift = lax.rem(LANES - a * SPANS - r, LANES)
                moved = pltpu.roll(delta_columns[...], shift, 1)
                base[r, a] = base[r, a] + jnp.where(lane == 0, moved, 0.0)
                plane = plane + jnp.where(lane == 0, pltpu.roll(delta_shift[0], shift, 1), 0.0)
                shift = lax.rem(shift + 1, LANES)
                corrected.append(plane - jnp.where(lane == 1, pltpu.roll(delta_shift[1], shift, 1), 0.0))
            planes_of.append(corrected)
        emit(1, rows, planes_of)
        return carry

    second(0, 0)
    second(1, 0)
    beyond_span()
    lax.fori_loop(2, SPANS // 2, second, 0)

    for k in range(1, SWEEPS - 1):

        def middle(i, carry, k=k):
            rows = rows_at(i)
            emit(k + 1, rows, update(k, rows))
            return carry

        lax.fori_loop(0, SPANS // 2, middle, 0)

    inlet[...] = jnp.zeros_like(inlet)

    def last(i, carry):
        rows = SPANS // 2 - 1 - i, SPANS // 2 + i
        for r, planes in zip(rows, update(SWEEPS - 1, rows)):
            for a in range(2):
                out[a * SPANS + r] = planes[a]
                inlet[...] = jnp.where(
                    lane == a * SPANS + r, pltpu.roll(planes[a], a * SPANS + r, 1), inlet[...]
                )
        return carry

    lax.fori_loop(0, SPANS // 2, last, 0)

    high, low = split(inlet[...])
    cells = jnp.concatenate([high[:, 0 : 2 * SPANS], low[:, 0 : 2 * SPANS]], axis=1)
    spread = jnp.dot(cells, to_panels, preferred_element_type=F32)
    spread = jnp.where(jnp.concatenate([same_field, same_field], axis=1), spread, 0.0)
    high, low = split(spread)
    gathered = jnp.dot(rows_twice, jnp.concatenate([high, low], axis=0), preferred_element_type=F32)
    back = panel_weight[0] * gathered[:, 0:WIDE] + panel_weight[1] * gathered[:, WIDE:]
    panel_rows[0:NT, :] = back
    for t in range(NT):
        if shifts[t]:
            back_send[t, 0:1, :] = panel_rows[t : t + 1, :]
            back_copy(t).start()
    for t in range(NT):
        if shifts[t]:
            back_copy(t).wait_recv()
            panel_rows[t : t + 1, :] = back_recv[t, 0:1, :]
    sens[...] = jnp.transpose(panel_rows[0:NT, 0 : NF * PT * SPANS])

    for t in range(NT):
        if shifts[t]:
            panel_copy(t).wait_send()
            back_copy(t).wait_send()

    from_left.wait_send()
    from_right.wait_send()

    @pl.when(span < nr - 1)
    def _():
        from_lower.wait_send()

    @pl.when(span > 0)
    def _():
        from_upper.wait_send()

    def drain(i, carry):
        k, r = i // SPANS, lax.rem(i, SPANS)
        for copy in theta_copies(k, r):
            copy.wait_send()
        return carry

    lax.fori_loop(0, SWEEPS * SPANS, drain, 0)
    @pl.when(span > 0)
    def _():
        coef_copy(False).wait_send()
        ahead_copy(False).wait_send()
        for k in range(SWEEPS):
            if k != AHEAD:
                to_lower_span(k).wait_send()

    @pl.when(span < nr - 1)
    def _():
        coef_copy(True).wait_send()
        ahead_copy(True).wait_send()
        for k in range(SWEEPS):
            if k != AHEAD:
                to_upper_span(k).wait_send()


def store(planes, table, out, sens, sems):
    copies = [pltpu.make_async_copy(table, sens, sems.at[2 * SPANS])]
    for cell in range(2 * SPANS):
        copies.append(pltpu.make_async_copy(planes.at[cell, 0:ROWS], out.at[:, cell], sems.at[cell]))
    for copy in copies:
        copy.start()
    for copy in copies:
        copy.wait()


def on_device(ns, nr, rhs, diag_coef, face_coef, time_coef, jac_up, jac_down, wall_mask, stator_adj, owner, share):
    nt, nf, ct, spans, nax = rhs.shape
    plane = (SWEEPS, SPANS, 2, PAD, LANES)
    ring = (SWEEPS, SPANS + 1, 2, PAD, LANES)
    edge = (SWEEPS, SPANS, PAD, LANES)
    inputs = (
        rhs.reshape(nt * nf * ct * spans, nax),
        diag_coef.reshape(ct * spans, nax),
        face_coef.reshape(3, ct * spans, nax),
        time_coef.reshape(ct * spans, nax),
        jac_up,
        jac_down,
        wall_mask.reshape(ct * spans, nax),
        stator_adj.transpose(1, 2, 3, 0).reshape(nf * PT * spans, nt),
        owner.transpose(1, 2, 0).reshape(ct * spans, nt),
        share.transpose(1, 2, 0).reshape(ct * spans, nt),
        jnp.asarray(time_operator()),
    )
    planes, table = pl.pallas_call(
        functools.partial(kernel, ns, nr),
        out_shape=(
            pltpu.VMEM((ct * spans, PAD, nax), F32),
            pltpu.VMEM((nf * PT * spans, nt), F32),
        ),
        in_specs=[pl.BlockSpec(memory_space=pltpu.HBM)] * len(inputs),
        out_specs=(pl.BlockSpec(memory_space=pltpu.VMEM),) * 2,
        scratch_shapes=[pltpu.VMEM((PAD * ct * spans, nax), F32)]
        + [pltpu.VMEM(x.shape, x.dtype) for x in inputs[1:]]
        + [
            pltpu.VMEM((NMAT * PAD, 3 * PAD), BF16),
            pltpu.VMEM((8, 2 * SPANS, LANES), F32),
            pltpu.VMEM(plane[1:], F32),
            pltpu.VMEM(plane, F32),
            pltpu.VMEM(edge, F32),
            pltpu.VMEM(edge, F32),
            pltpu.VMEM(ring, F32),
            pltpu.VMEM(ring, F32),
            pltpu.VMEM(edge, F32),
            pltpu.VMEM(edge, F32),
            pltpu.VMEM((NT, 1, WIDE), F32),
            pltpu.VMEM((NT, 1, WIDE), F32),
            pltpu.VMEM((16, WIDE), F32),
            pltpu.VMEM((2, NT, WIDE), F32),
            pltpu.VMEM((PAD, LANES), F32),
            pltpu.VMEM((NT, 1, WIDE), F32),
            pltpu.VMEM((NT, 1, WIDE), F32),
            pltpu.VMEM((48, 8), F32),
            pltpu.VMEM((16, WIDE), F32),
            pltpu.VMEM((4, 16, WIDE), F32),
            pltpu.VMEM((PAD, LANES), F32),
            pltpu.VMEM((2, PAD, LANES), F32),
            pltpu.SemaphoreType.DMA((len(inputs),)),
            pltpu.SemaphoreType.DMA((SWEEPS, SPANS, 2)),
            pltpu.SemaphoreType.DMA((SWEEPS, SPANS, 2)),
            pltpu.SemaphoreType.DMA((SWEEPS, 2)),
            pltpu.SemaphoreType.DMA((SWEEPS, 2)),
            pltpu.SemaphoreType.DMA((2, NT)),
            pltpu.SemaphoreType.DMA((2, NT)),
            pltpu.SemaphoreType.DMA((2, 4)),
            pltpu.VMEM((2, 2, PAD, LANES), F32),
            pltpu.VMEM((2, 2, PAD, LANES), F32),
            pltpu.SemaphoreType.DMA((2, 2)),
            pltpu.VMEM((2, 2 * SPANS, LANES), F32),
            pltpu.SemaphoreType.DMA((2, 2)),
        ],
        compiler_params=pltpu.CompilerParams(
            collective_id=0, has_side_effects=True, vmem_limit_bytes=60 * 2**20
        ),
    )(*inputs)
    out, sens = pl.pallas_call(
        store,
        out_shape=(
            jax.ShapeDtypeStruct((nt * nf, ct * spans, nax), F32),
            jax.ShapeDtypeStruct((nf * PT * spans, nt), F32),
        ),
        in_specs=[pl.BlockSpec(memory_space=pltpu.VMEM)] * 2,
        out_specs=(pl.BlockSpec(memory_space=pltpu.HBM),) * 2,
        scratch_shapes=[pltpu.SemaphoreType.DMA((2 * SPANS + 1,))],
    )(pltpu.with_memory_space_constraint(planes, pltpu.VMEM), pltpu.with_memory_space_constraint(table, pltpu.VMEM))
    sens = sens.reshape(nf, PT, spans, nt).transpose(3, 0, 1, 2)
    return out.reshape(rhs.shape), sens


def solution(mesh):
    in_specs = (
        P(None, None, "sector", "span", None),
        P("sector", "span", None),
        P(None, "sector", "span", None),
        P("sector", "span", None),
        P(),
        P(),
        P("sector", "span", None),
        P(None, None, "sector", "span"),
        P(None, "sector", "span"),
        P(None, "sector", "span"),
    )
    out_specs = (P(None, None, "sector", "span", None), P(None, None, "sector", "span"))
    return jax.shard_map(
        functools.partial(on_device, mesh.shape["sector"], mesh.shape["span"]),
        mesh=mesh,
        in_specs=in_specs,
        out_specs=out_specs,
        check_vma=False,
    )
```

```python
import functools

import jax
import jax.numpy as jnp
import ml_dtypes
import numpy as np
from jax import lax
from jax.experimental import pallas as pl
from jax.experimental.pallas import tpu as pltpu
from jax.sharding import PartitionSpec as P

SWEEPS = 4
AHEAD = 2
NT = 11
NF = 7
ROWS = NT * NF
PAD = 80
NMAT = 7
SPANS = 8
PT = 4
LANES = 128
WIDE = 256
F32 = jnp.float32
BF16 = jnp.bfloat16
HIGHEST = lax.Precision.HIGHEST
MESH = pl.DeviceIdType.MESH


def time_operator():
    step = np.arange(NT)[:, None] - np.arange(NT)[None, :]
    sines = np.where(step == 0, 1.0, np.sin(np.pi * step / NT))
    spectral = np.where(step == 0, 0.0, 0.5 * (1.0 - 2.0 * (step % 2)) / sines)
    table = np.zeros((PAD, PAD), np.float32)
    table[:ROWS, :ROWS] = np.kron(spectral.T, np.eye(NF))
    high = table.astype(ml_dtypes.bfloat16)
    low = (table - high.astype(np.float32)).astype(ml_dtypes.bfloat16)
    return np.concatenate([high, high, low], axis=1)


def shift_of(instance, count):
    return ((instance * count) // (NT - 1) - instance // (NT - 1)) % count


def split(value):
    high = value.astype(BF16)
    low = (value - high.astype(F32)).astype(BF16)
    return high, low


def index_of(shape, dim):
    return lax.broadcasted_iota(jnp.int32, shape, dim).astype(F32)


def over_fields(rows):
    instance = jnp.floor((rows + 0.5) * (1.0 / NF))
    return instance, rows - NF * instance


def exact_dot(left, right):
    return jnp.dot(left, right, precision=HIGHEST, preferred_element_type=F32)


def kernel(ns, nr, *refs):
    hbm, refs = refs[:11], refs[11:]
    (out, sens), refs = refs[:2], refs[2:]
    vmem, refs = refs[:11], refs[11:]
    rhs, diag, face, time, jac_up, jac_down, wall, stator, owner, share, time_op = vmem
    (
        weights,
        coef,
        base,
        own_buf,
        tu_buf,
        td_buf,
        ru_buf,
        rd_buf,
        su_buf,
        sd_buf,
        panel_send,
        panel_recv,
        panel_rows,
        panel_weight,
        inlet,
        back_send,
        back_recv,
        jac_rows,
        delta_send,
        delta_recv,
        delta_columns,
        delta_shift,
        input_sems,
        theta_send,
        theta_recv,
        span_send,
        span_recv,
        panel_sems,
        back_sems,
        delta_sems,
        ahead_send,
        ahead_recv,
        ahead_sems,
        edge_coef,
        edge_coef_sems,
    ) = refs
    sector = lax.axis_index("sector")
    span = lax.axis_index("span")
    shifts = [shift_of(t, ns) for t in range(NT)]
    partners = sorted({d % ns for s in shifts for d in (s, -s)} | {1 % ns, (ns - 1) % ns})
    partners = [d for d in partners if d != 0]

    def at_sector(step):
        return {"sector": lax.rem(sector + step, ns)}

    def load(n):
        target = vmem[n] if n else rhs.at[0 : ROWS * 2 * SPANS]
        return pltpu.make_async_copy(hbm[n], target, input_sems.at[n])

    for n in (7, 0, 1, 6, 8, 9, 4, 5, 10, 2, 3):
        load(n).start()

    ru_buf[:, SPANS] = jnp.zeros((SWEEPS,) + ru_buf.shape[2:], F32)
    rd_buf[:, 0] = jnp.zeros((SWEEPS,) + rd_buf.shape[2:], F32)

    delta_recv[...] = jnp.zeros_like(delta_recv)

    barrier = pltpu.get_barrier_semaphore()
    for step in partners:
        pl.semaphore_signal(barrier, inc=1, device_id=at_sector(step), device_id_type=MESH)

    @pl.when(span > 0)
    def _():
        pl.semaphore_signal(barrier, inc=1, device_id={"span": span - 1}, device_id_type=MESH)

    @pl.when(span < nr - 1)
    def _():
        pl.semaphore_signal(barrier, inc=1, device_id={"span": span + 1}, device_id_type=MESH)

    wide = (NT, WIDE)
    load(7).wait()
    panel_rows[...] = jnp.zeros_like(panel_rows)
    panel_rows[0:NT, 0 : NF * PT * SPANS] = jnp.transpose(stator[...])
    for t in range(NT):
        panel_send[t, 0:1, :] = panel_rows[t : t + 1, :]

    def panel_copy(t):
        return pltpu.make_async_remote_copy(
            src_ref=panel_send.at[t],
            dst_ref=panel_recv.at[t],
            send_sem=panel_sems.at[0, t],
            recv_sem=panel_sems.at[1, t],
            device_id=at_sector(ns - shifts[t]),
            device_id_type=MESH,
        )

    def back_copy(t):
        return pltpu.make_async_remote_copy(
            src_ref=back_send.at[t],
            dst_ref=back_recv.at[t],
            send_sem=back_sems.at[0, t],
            recv_sem=back_sems.at[1, t],
            device_id=at_sector(shifts[t]),
            device_id_type=MESH,
        )

    lane = lax.broadcasted_iota(jnp.int32, (PAD, LANES), 1)
    row = index_of((PAD, 3 * PAD), 0)
    column = index_of((PAD, 3 * PAD), 1)
    column = column - PAD * jnp.floor((column + 0.5) * (1.0 / PAD))
    row_instance, _ = over_fields(row)
    column_instance, _ = over_fields(column)
    same_instance = (row_instance == column_instance) & (row < ROWS) & (column < ROWS)
    instance_rows = jnp.where(
        (over_fields(index_of((PAD, NT), 0))[0] == index_of((PAD, NT), 1)) & (index_of((PAD, NT), 0) < ROWS), 1.0, 0.0
    )
    instance_columns = jnp.where(
        (over_fields(index_of((NT, PAD), 1))[0] == index_of((NT, PAD), 0)) & (index_of((NT, PAD), 1) < ROWS), 1.0, 0.0
    )
    wide_lane = lax.broadcasted_iota(jnp.int32, (PAD, WIDE), 1)
    wide_field = lax.shift_right_logical(wide_lane, 5).astype(F32)
    same_field = over_fields(index_of((PAD, WIDE), 0))[1] == wide_field
    lane_panel = jnp.bitwise_and(lax.shift_right_logical(lax.broadcasted_iota(jnp.int32, wide, 1), 3), PT - 1)

    load(4).wait()
    load(5).wait()
    load(10).wait()
    jac_rows[...] = jnp.zeros_like(jac_rows)
    for direction in range(3):
        for side, table in enumerate((jac_up, jac_down)):
            start = (2 * direction + side) * 8
            jac_rows[start : start + NF, 0:NF] = table[direction]
    high, low = split(jac_rows[...])
    wide_columns = index_of((8, 3 * PAD), 1)
    piece = jnp.floor((wide_columns + 0.5) * (1.0 / PAD))
    chosen = over_fields(wide_columns - PAD * piece)[1] == index_of((8, 3 * PAD), 0)
    pick_high = jnp.where(chosen & (piece < 2.0), 1.0, 0.0).astype(BF16)
    pick_low = jnp.where(chosen & (piece > 1.0), 1.0, 0.0).astype(BF16)
    columns = jnp.dot(high, pick_high, preferred_element_type=F32)
    columns = (columns + jnp.dot(low, pick_low, preferred_element_type=F32)).astype(BF16)
    _, field_of_row = over_fields(index_of((PAD, 8), 0))
    pick_row = jnp.where(field_of_row == index_of((PAD, 8), 1), 1.0, 0.0).astype(BF16)
    weights[0:PAD, :] = time_op[...]
    for m in range(1, NMAT):
        block = jnp.dot(pick_row, columns[8 * (m - 1) : 8 * m, :], preferred_element_type=F32)
        weights[m * PAD : (m + 1) * PAD, :] = jnp.where(same_instance, block, 0.0).astype(BF16)

    for n in (0, 1, 2, 3, 6, 8, 9):
        load(n).wait()
    inverse = wall[...].astype(F32) / diag[...]
    axial_lane = lax.broadcasted_iota(jnp.int32, inverse.shape, 1)
    axial = inverse * face[2]
    coef[0] = inverse
    coef[1] = inverse * time[...]
    coef[2] = inverse * face[0]
    coef[3] = inverse * face[1]
    coef[4] = jnp.where(axial_lane == LANES - 1, 0.0, axial)
    coef[5] = jnp.where(axial_lane == 0, 0.0, axial)
    coef[6] = jnp.zeros_like(inverse)
    coef[7] = jnp.zeros_like(inverse)
    coef_columns = jnp.transpose(coef[...].reshape(8 * 2 * SPANS, LANES))
    cell_lanes = jnp.bitwise_and(lax.broadcasted_iota(jnp.int32, (LANES, WIDE), 1), 4 * SPANS - 1)
    to_cells = jnp.where(
        (cell_lanes == lax.broadcasted_iota(jnp.int32, (LANES, WIDE), 0)) & (cell_lanes < 2 * SPANS), 1.0, 0.0
    )
    inlet_inverse = exact_dot(coef_columns[0:8, :], to_cells)[0:1, :]

    spread_lanes = lax.broadcasted_iota(jnp.int32, (SPANS, WIDE), 1)
    spread_span = jnp.where(
        jnp.bitwise_and(spread_lanes, SPANS - 1) == lax.broadcasted_iota(jnp.int32, (SPANS, WIDE), 0), 1.0, 0.0
    )
    for a in range(2):
        cells = pl.ds(a * SPANS, SPANS)
        share_wide = exact_dot(jnp.transpose(share[cells, :]), spread_span)
        first = jnp.bitwise_and(owner[cells, :], PT - 1).astype(F32)
        first_wide = exact_dot(jnp.transpose(first), spread_span)
        own_panel = lane_panel.astype(F32)
        lower = jnp.where(first_wide == own_panel, share_wide, 0.0)
        upper = jnp.where(first_wide == own_panel - 1.0, 1.0 - share_wide, 0.0)
        panel_weight[a] = lower + upper

    base[...] = jnp.zeros_like(base)
    for r in range(SPANS):
        for a in range(2):
            cell = a * SPANS + r
            plane = rhs[pl.ds(cell, ROWS, stride=2 * SPANS), :]
            base[r, a, 0:ROWS, :] = plane * coef[0, cell : cell + 1, :]

    beside = (span > 0).astype(jnp.int32) + (span < nr - 1).astype(jnp.int32)
    pl.semaphore_wait(barrier, len(partners) + beside)

    for t in range(NT):
        if shifts[t]:
            panel_copy(t).start()

    def theta_copies(k, r):
        up = pltpu.make_async_remote_copy(
            src_ref=su_buf.at[k, r],
            dst_ref=tu_buf.at[k, r],
            send_sem=theta_send.at[k, r, 0],
            recv_sem=theta_recv.at[k, r, 0],
            device_id=at_sector(ns - 1),
            device_id_type=MESH,
        )
        down = pltpu.make_async_remote_copy(
            src_ref=sd_buf.at[k, r],
            dst_ref=td_buf.at[k, r],
            send_sem=theta_send.at[k, r, 1],
            recv_sem=theta_recv.at[k, r, 1],
            device_id=at_sector(1),
            device_id_type=MESH,
        )
        return up, down

    def to_lower_span(k):
        return pltpu.make_async_remote_copy(
            src_ref=ru_buf.at[k, 0],
            dst_ref=ru_buf.at[k, SPANS],
            send_sem=span_send.at[k, 0],
            recv_sem=span_recv.at[k, 0],
            device_id={"span": span - 1},
            device_id_type=MESH,
        )

    def to_upper_span(k):
        return pltpu.make_async_remote_copy(
            src_ref=rd_buf.at[k, SPANS],
            dst_ref=rd_buf.at[k, 0],
            send_sem=span_send.at[k, 1],
            recv_sem=span_recv.at[k, 1],
            device_id={"span": span + 1},
            device_id_type=MESH,
        )

    def beside_copy(source, target, sems, upward):
        slot = 0 if upward else 1
        return pltpu.make_async_remote_copy(
            src_ref=source,
            dst_ref=target.at[slot],
            send_sem=sems.at[0, slot],
            recv_sem=sems.at[1, slot],
            device_id={"span": span + 1 if upward else span - 1},
            device_id_type=MESH,
        )

    def coef_copy(upward):
        return beside_copy(coef.at[3], edge_coef, edge_coef_sems, upward)

    def ahead_copy(upward):
        return beside_copy(ahead_send.at[int(upward)], ahead_recv, ahead_sems, upward)

    @pl.when(span > 0)
    def _():
        coef_copy(False).start()

    @pl.when(span < nr - 1)
    def _():
        coef_copy(True).start()

    def send_ahead(k):
        for upward, r in ((False, 0), (True, SPANS - 1)):
            for a in range(2):
                outside = td_buf if a == 0 else tu_buf
                inside = rd_buf[k, r, a] if upward else ru_buf[k, r + 1, a]
                total = own_buf[k, r, a] - coefficient(2, r, a) * outside[k, r]
                ahead_send[int(upward), a] = total - coefficient(3, r, a) * inside

        @pl.when(span > 0)
        def _():
            ahead_copy(False).start()

        @pl.when(span < nr - 1)
        def _():
            ahead_copy(True).start()

    def receive_ahead(k):
        def complete(slot, r, terms, m):
            columns = []
            for a in range(2):
                cell = a * SPANS + r
                plane = ahead_recv[slot, a] - edge_coef[slot, cell : cell + 1, :] * terms[a]
                high, low = split(plane)
                columns.append(jnp.concatenate([high, low, high], axis=0))
            data = jnp.concatenate(columns, axis=1)
            return jnp.dot(weights[m * PAD : (m + 1) * PAD, :], data, preferred_element_type=F32)

        @pl.when(span < nr - 1)
        def _():
            coef_copy(False).wait_recv()
            ahead_copy(False).wait_recv()
            product = complete(1, 0, [rd_buf[k - 1, SPANS, a] for a in range(2)], 3)
            for a in range(2):
                ru_buf[k, SPANS, a] = product[:, a * LANES : (a + 1) * LANES]

        @pl.when(span > 0)
        def _():
            coef_copy(True).wait_recv()
            ahead_copy(True).wait_recv()
            product = complete(0, SPANS - 1, [ru_buf[k - 1, 0, a] for a in range(2)], 4)
            for a in range(2):
                rd_buf[k, 0, a] = product[:, a * LANES : (a + 1) * LANES]

    def rows_at(i):
        low = lax.rem(i + SPANS // 2 - 2, SPANS // 2)
        return low, SPANS - 1 - low

    def coefficient(n, r, a):
        return coef[n, pl.ds(a * SPANS + r, 1), :]

    def emit(k, rows, planes_of):
        for r, planes in zip(rows, planes_of):
            columns = []
            for plane in planes:
                high, low = split(plane)
                columns.append(jnp.concatenate([high, low, high], axis=0))
            data = jnp.concatenate(columns, axis=1)
            products = [
                jnp.dot(weights[start * PAD : stop * PAD, :], data, preferred_element_type=F32)
                for start, stop in ((0, 3), (3, 5), (5, NMAT))
            ]

            def part(m, a):
                m, product = (m, products[0]) if m < 3 else (m - 3, products[1]) if m < 5 else (m - 5, products[2])
                return product[m * PAD : (m + 1) * PAD, a * LANES : (a + 1) * LANES]

            su_buf[k, r] = part(1, 0)
            sd_buf[k, r] = part(2, 1)
            for a in range(2):
                ru_buf[k, r, a] = part(3, a)
                rd_buf[k, r + 1, a] = part(4, a)
                total = base[r, a] - coefficient(1, r, a) * part(0, a)
                total = total - coefficient(2, r, a) * (part(2, 0) if a else part(1, 1))
                total = total - coefficient(4, r, a) * pltpu.roll(part(5, a), LANES - 1, 1)
                own_buf[k, r, a] = total - coefficient(5, r, a) * pltpu.roll(part(6, a), 1, 1)

        if k != AHEAD:

            @pl.when((rows[0] == 0) & (span > 0))
            def _():
                to_lower_span(k).start()

            @pl.when((rows[0] == 0) & (span < nr - 1))
            def _():
                to_upper_span(k).start()

        for r in rows:
            for copy in theta_copies(k, r):
                copy.start()

    def update(k, rows):
        for r in rows:
            for copy in theta_copies(k, r):
                copy.wait_recv()

        if k == AHEAD - 1:

            @pl.when(rows[0] == 0)
            def _():
                send_ahead(k)

        if k == AHEAD:

            @pl.when(rows[0] == 0)
            def _():
                receive_ahead(k)

        else:

            @pl.when((rows[0] == 0) & (span < nr - 1))
            def _():
                to_lower_span(k).wait_recv()

            @pl.when((rows[0] == 0) & (span > 0))
            def _():
                to_upper_span(k).wait_recv()

        planes_of = []
        for r in rows:
            planes = []
            for a in range(2):
                outside = td_buf if a == 0 else tu_buf
                total = own_buf[k, r, a] - coefficient(2, r, a) * outside[k, r]
                planes.append(total - coefficient(3, r, a) * (ru_buf[k, r + 1, a] + rd_buf[k, r, a]))
            planes_of.append(planes)
        return planes_of

    def first(i, carry):
        rows = rows_at(i)
        emit(0, rows, [[base[r, a] for a in range(2)] for r in rows])
        return carry

    lax.fori_loop(0, SPANS // 2, first, 0)

    cell_row = jnp.bitwise_and(lax.broadcasted_iota(jnp.int32, (4 * SPANS, 2 * WIDE), 0), 2 * SPANS - 1)
    panel_lane = lax.broadcasted_iota(jnp.int32, (4 * SPANS, 2 * WIDE), 1)
    panel_cell = jnp.bitwise_and(panel_lane, SPANS - 1) + jnp.where(panel_lane < WIDE, 0, SPANS)
    to_panels = jnp.where(cell_row == panel_cell, 1.0, 0.0).astype(BF16)
    rows_twice = jnp.concatenate([instance_columns, instance_columns], axis=1).astype(BF16)

    half_column = jnp.bitwise_and(lax.broadcasted_iota(jnp.int32, (PAD, 32), 1), 15).astype(F32)
    of_instance = over_fields(index_of((PAD, 32), 0))[0] == half_column
    spread_rows = jnp.where(of_instance & (index_of((PAD, 32), 0) < ROWS), 1.0, 0.0).astype(BF16)
    gather_slot = jnp.bitwise_and(lax.broadcasted_iota(jnp.int32, (2 * WIDE, LANES), 0), 4 * SPANS - 1)
    gather_lane = lax.broadcasted_iota(jnp.int32, (2 * WIDE, LANES), 1)
    gather = jnp.where(gather_slot == gather_lane, 1.0, 0.0).astype(BF16)

    for t in range(NT):
        if shifts[t]:
            panel_copy(t).wait_recv()
            panel_rows[t : t + 1, :] = panel_recv[t, 0:1, :]
    cells_wide = jnp.zeros(wide, F32)
    for a in range(2):
        shares = panel_weight[a] * panel_rows[0:NT, :]
        shares = shares + pltpu.roll(shares, WIDE - SPANS, 1)
        shares = shares + pltpu.roll(shares, WIDE - 2 * SPANS, 1)
        if a:
            shares = pltpu.roll(shares, a * SPANS, 1)
        cells_wide = jnp.where(lane_panel == a, shares, cells_wide)
    cells_wide = cells_wide * inlet_inverse
    delta_send[0:NT, :] = cells_wide

    def delta_copy(n, device):
        return pltpu.make_async_remote_copy(
            src_ref=delta_send,
            dst_ref=delta_recv.at[n],
            send_sem=delta_sems.at[0, n],
            recv_sem=delta_sems.at[1, n],
            device_id=device,
            device_id_type=MESH,
        )

    from_left = delta_copy(0, at_sector(1))
    from_right = delta_copy(1, at_sector(ns - 1))
    from_lower = delta_copy(2, {"span": span + 1})
    from_upper = delta_copy(3, {"span": span - 1})

    @pl.when(span < nr - 1)
    def _():
        from_lower.start()

    @pl.when(span > 0)
    def _():
        from_upper.start()

    from_left.start()
    from_right.start()

    slot = jnp.bitwise_and(lax.broadcasted_iota(jnp.int32, wide, 1), 4 * SPANS - 1)

    def place(values, n, shift, low, high):
        moved = pltpu.roll(delta_recv[n, 0:NT, :], shift % WIDE, 1)
        return jnp.where((slot >= low) & (slot < high), moved, values)

    def to_columns(values):
        high, low = split(jnp.concatenate([values, jnp.zeros((16 - NT, WIDE), F32)], axis=0))
        spread = jnp.dot(spread_rows, jnp.concatenate([high, low], axis=0), preferred_element_type=F32)
        high, low = split(jnp.where(same_field, spread, 0.0))
        return jnp.dot(jnp.concatenate([high, low], axis=1), gather, preferred_element_type=F32)

    def stacked(columns):
        high, low = split(columns)
        return jnp.concatenate([high, low, high], axis=0)

    def inlet_coefficient(n, axial_cell):
        return pltpu.roll(coef_columns[axial_cell : axial_cell + 1, :], (LANES - 2 * SPANS * n) % LANES, 1)

    columns = to_columns(cells_wide)
    product = jnp.dot(weights[...], stacked(columns), preferred_element_type=F32)
    from_left.wait_recv()
    from_right.wait_recv()
    around = place(jnp.zeros(wide, F32), 0, SPANS, 2 * SPANS, 3 * SPANS)
    around = place(around, 1, 3 * SPANS, 3 * SPANS, 4 * SPANS)
    around = jnp.dot(weights[PAD : 3 * PAD, :], stacked(to_columns(around)), preferred_element_type=F32)
    around = pltpu.roll(around, LANES - 2 * SPANS, 1)

    def moved_part(m, shift):
        return pltpu.roll(product[m * PAD : (m + 1) * PAD, :], shift % LANES, 1)

    first_half = lane < SPANS
    along = jnp.where(first_half, moved_part(1, -SPANS), around[0:PAD])
    along = along + jnp.where(first_half, around[PAD : 2 * PAD], moved_part(2, SPANS))
    across = jnp.where(jnp.bitwise_and(lane, SPANS - 1) == SPANS - 1, 0.0, moved_part(3, -1))
    below = jnp.where(jnp.bitwise_and(lane, SPANS - 1) == 0, 0.0, moved_part(4, 1))
    coupled = inlet_coefficient(1, 0) * product[0:PAD, :]
    coupled = coupled + inlet_coefficient(2, 0) * along
    coupled = coupled + inlet_coefficient(3, 0) * (across + below)
    delta_columns[...] = columns
    delta_shift[0] = columns - coupled
    delta_shift[1] = inlet_coefficient(5, 1) * product[6 * PAD : 7 * PAD, :]

    def beyond_span():
        @pl.when(span > 0)
        def _():
            from_lower.wait_recv()

        @pl.when(span < nr - 1)
        def _():
            from_upper.wait_recv()

        cells = jnp.zeros(wide, F32)
        for a in range(2):
            top, bottom = (a + 1) * SPANS - 1, a * SPANS
            cells = place(cells, 2, bottom - top, bottom, bottom + 1)
            cells = place(cells, 3, top - bottom, top, top + 1)
        product = jnp.dot(weights[3 * PAD : 5 * PAD, :], stacked(to_columns(cells)), preferred_element_type=F32)
        above = jnp.where(jnp.bitwise_and(lane, SPANS - 1) == SPANS - 1, product[0:PAD], 0.0)
        below = jnp.where(jnp.bitwise_and(lane, SPANS - 1) == 0, product[PAD : 2 * PAD], 0.0)
        delta_shift[0] = delta_shift[0] - inlet_coefficient(3, 0) * (above + below)

    def second(i, carry):
        rows = rows_at(i)
        planes_of = []
        for r, planes in zip(rows, update(0, rows)):
            corrected = []
            for a, plane in enumerate(planes):
                shift = lax.rem(LANES - a * SPANS - r, LANES)
                moved = pltpu.roll(delta_columns[...], shift, 1)
                base[r, a] = base[r, a] + jnp.where(lane == 0, moved, 0.0)
                plane = plane + jnp.where(lane == 0, pltpu.roll(delta_shift[0], shift, 1), 0.0)
                shift = lax.rem(shift + 1, LANES)
                corrected.append(plane - jnp.where(lane == 1, pltpu.roll(delta_shift[1], shift, 1), 0.0))
            planes_of.append(corrected)
        emit(1, rows, planes_of)
        return carry

    second(0, 0)
    second(1, 0)
    beyond_span()
    lax.fori_loop(2, SPANS // 2, second, 0)

    for k in range(1, SWEEPS - 1):

        def middle(i, carry, k=k):
            rows = rows_at(i)
            emit(k + 1, rows, update(k, rows))
            return carry

        lax.fori_loop(0, SPANS // 2, middle, 0)

    inlet[...] = jnp.zeros_like(inlet)

    def last(i, carry):
        rows = SPANS // 2 - 1 - i, SPANS // 2 + i
        for r, planes in zip(rows, update(SWEEPS - 1, rows)):
            for a in range(2):
                out[a * SPANS + r] = planes[a]
                inlet[...] = jnp.where(
                    lane == a * SPANS + r, pltpu.roll(planes[a], a * SPANS + r, 1), inlet[...]
                )
        return carry

    lax.fori_loop(0, SPANS // 2, last, 0)

    high, low = split(inlet[...])
    cells = jnp.concatenate([high[:, 0 : 2 * SPANS], low[:, 0 : 2 * SPANS]], axis=1)
    spread = jnp.dot(cells, to_panels, preferred_element_type=F32)
    spread = jnp.where(jnp.concatenate([same_field, same_field], axis=1), spread, 0.0)
    high, low = split(spread)
    gathered = jnp.dot(rows_twice, jnp.concatenate([high, low], axis=0), preferred_element_type=F32)
    back = panel_weight[0] * gathered[:, 0:WIDE] + panel_weight[1] * gathered[:, WIDE:]
    panel_rows[0:NT, :] = back
    for t in range(NT):
        if shifts[t]:
            back_send[t, 0:1, :] = panel_rows[t : t + 1, :]
            back_copy(t).start()
    for t in range(NT):
        if shifts[t]:
            back_copy(t).wait_recv()
            panel_rows[t : t + 1, :] = back_recv[t, 0:1, :]
    sens[...] = jnp.transpose(panel_rows[0:NT, 0 : NF * PT * SPANS])

    for t in range(NT):
        if shifts[t]:
            panel_copy(t).wait_send()
            back_copy(t).wait_send()

    from_left.wait_send()
    from_right.wait_send()

    @pl.when(span < nr - 1)
    def _():
        from_lower.wait_send()

    @pl.when(span > 0)
    def _():
        from_upper.wait_send()

    def drain(i, carry):
        k, r = i // SPANS, lax.rem(i, SPANS)
        for copy in theta_copies(k, r):
            copy.wait_send()
        return carry

    lax.fori_loop(0, SWEEPS * SPANS, drain, 0)
    @pl.when(span > 0)
    def _():
        coef_copy(False).wait_send()
        ahead_copy(False).wait_send()
        for k in range(SWEEPS):
            if k != AHEAD:
                to_lower_span(k).wait_send()

    @pl.when(span < nr - 1)
    def _():
        coef_copy(True).wait_send()
        ahead_copy(True).wait_send()
        for k in range(SWEEPS):
            if k != AHEAD:
                to_upper_span(k).wait_send()


def store(planes, table, out, sens, sems):
    copies = [pltpu.make_async_copy(table, sens, sems.at[2 * SPANS])]
    for cell in range(2 * SPANS):
        copies.append(pltpu.make_async_copy(planes.at[cell, 0:ROWS], out.at[:, cell], sems.at[cell]))
    for copy in copies:
        copy.start()
    for copy in copies:
        copy.wait()


def on_device(ns, nr, rhs, diag_coef, face_coef, time_coef, jac_up, jac_down, wall_mask, stator_adj, owner, share):
    nt, nf, ct, spans, nax = rhs.shape
    plane = (SWEEPS, SPANS, 2, PAD, LANES)
    ring = (SWEEPS, SPANS + 1, 2, PAD, LANES)
    edge = (SWEEPS, SPANS, PAD, LANES)
    inputs = (
        rhs.reshape(nt * nf * ct * spans, nax),
        diag_coef.reshape(ct * spans, nax),
        face_coef.reshape(3, ct * spans, nax),
        time_coef.reshape(ct * spans, nax),
        jac_up,
        jac_down,
        wall_mask.reshape(ct * spans, nax),
        stator_adj.transpose(1, 2, 3, 0).reshape(nf * PT * spans, nt),
        owner.transpose(1, 2, 0).reshape(ct * spans, nt),
        share.transpose(1, 2, 0).reshape(ct * spans, nt),
        jnp.asarray(time_operator()),
    )
    planes, table = pl.pallas_call(
        functools.partial(kernel, ns, nr),
        out_shape=(
            pltpu.VMEM((ct * spans, PAD, nax), F32),
            pltpu.VMEM((nf * PT * spans, nt), F32),
        ),
        in_specs=[pl.BlockSpec(memory_space=pltpu.HBM)] * len(inputs),
        out_specs=(pl.BlockSpec(memory_space=pltpu.VMEM),) * 2,
        scratch_shapes=[pltpu.VMEM((PAD * ct * spans, nax), F32)]
        + [pltpu.VMEM(x.shape, x.dtype) for x in inputs[1:]]
        + [
            pltpu.VMEM((NMAT * PAD, 3 * PAD), BF16),
            pltpu.VMEM((8, 2 * SPANS, LANES), F32),
            pltpu.VMEM(plane[1:], F32),
            pltpu.VMEM(plane, F32),
            pltpu.VMEM(edge, F32),
            pltpu.VMEM(edge, F32),
            pltpu.VMEM(ring, F32),
            pltpu.VMEM(ring, F32),
            pltpu.VMEM(edge, F32),
            pltpu.VMEM(edge, F32),
            pltpu.VMEM((NT, 1, WIDE), F32),
            pltpu.VMEM((NT, 1, WIDE), F32),
            pltpu.VMEM((16, WIDE), F32),
            pltpu.VMEM((2, NT, WIDE), F32),
            pltpu.VMEM((PAD, LANES), F32),
            pltpu.VMEM((NT, 1, WIDE), F32),
            pltpu.VMEM((NT, 1, WIDE), F32),
            pltpu.VMEM((48, 8), F32),
            pltpu.VMEM((16, WIDE), F32),
            pltpu.VMEM((4, 16, WIDE), F32),
            pltpu.VMEM((PAD, LANES), F32),
            pltpu.VMEM((2, PAD, LANES), F32),
            pltpu.SemaphoreType.DMA((len(inputs),)),
            pltpu.SemaphoreType.DMA((SWEEPS, SPANS, 2)),
            pltpu.SemaphoreType.DMA((SWEEPS, SPANS, 2)),
            pltpu.SemaphoreType.DMA((SWEEPS, 2)),
            pltpu.SemaphoreType.DMA((SWEEPS, 2)),
            pltpu.SemaphoreType.DMA((2, NT)),
            pltpu.SemaphoreType.DMA((2, NT)),
            pltpu.SemaphoreType.DMA((2, 4)),
            pltpu.VMEM((2, 2, PAD, LANES), F32),
            pltpu.VMEM((2, 2, PAD, LANES), F32),
            pltpu.SemaphoreType.DMA((2, 2)),
            pltpu.VMEM((2, 2 * SPANS, LANES), F32),
            pltpu.SemaphoreType.DMA((2, 2)),
        ],
        compiler_params=pltpu.CompilerParams(
            collective_id=0, has_side_effects=True, vmem_limit_bytes=60 * 2**20
        ),
    )(*inputs)
    out, sens = pl.pallas_call(
        store,
        out_shape=(
            jax.ShapeDtypeStruct((nt * nf, ct * spans, nax), F32),
            jax.ShapeDtypeStruct((nf * PT * spans, nt), F32),
        ),
        in_specs=[pl.BlockSpec(memory_space=pltpu.VMEM)] * 2,
        out_specs=(pl.BlockSpec(memory_space=pltpu.HBM),) * 2,
        scratch_shapes=[pltpu.SemaphoreType.DMA((2 * SPANS + 1,))],
    )(pltpu.with_memory_space_constraint(planes, pltpu.VMEM), pltpu.with_memory_space_constraint(table, pltpu.VMEM))
    sens = sens.reshape(nf, PT, spans, nt).transpose(3, 0, 1, 2)
    return out.reshape(rhs.shape), sens


def solution(mesh):
    in_specs = (
        P(None, None, "sector", "span", None),
        P("sector", "span", None),
        P(None, "sector", "span", None),
        P("sector", "span", None),
        P(),
        P(),
        P("sector", "span", None),
        P(None, None, "sector", "span"),
        P(None, "sector", "span"),
        P(None, "sector", "span"),
    )
    out_specs = (P(None, None, "sector", "span", None), P(None, None, "sector", "span"))
    return jax.shard_map(
        functools.partial(on_device, mesh.shape["sector"], mesh.shape["span"]),
        mesh=mesh,
        in_specs=in_specs,
        out_specs=out_specs,
        check_vma=False,
    )
```
